32 devices in a mesh: batch: 4 (over z), pb: 2 (over x), ka: 4 (over y, core).
Axes of the slice: x: 2, y: 2, z: 4, core: 2. Of those that a mesh axis runs over, the one named last changes fastest.
Arguments:
- inputs: bfloat16 [16, 1024, 768], P('batch', ('pb', 'ka')), may hold values from -6 to 6
- block_place: int32 [16, 8], P('batch'), may hold values from 0 to 7, each once within a row
- ln1_gain: float32 [768], replicated, may hold values from 0.1 to 1.9
- ln1_shift: float32 [768], replicated, may hold values from -3 to 3
- w_qkv: bfloat16 [768, 2304], replicated, may hold values from -0.21875 to 0.21875
- w_out: bfloat16 [768, 768], replicated, may hold values from -1.25 to 1.25
- ln2_gain: float32 [768], replicated, may hold values from 0.1 to 1.9
- ln2_shift: float32 [768], replicated, may hold values from -3 to 3
- w_up: bfloat16 [768, 3072], replicated, may hold values from -0.21875 to 0.21875
- w_down: bfloat16 [3072, 768], replicated, may hold values from -0.109375 to 0.109375
- cotangent: bfloat16 [16, 1024, 768], P('batch', ('pb', 'ka')), may hold values from -6 to 6
Outputs:
- outputs: bfloat16 [16, 1024, 768], P('batch', ('pb', 'ka'))
- grad_inputs: bfloat16 [16, 1024, 768], P('batch', ('pb', 'ka'))
- grad_qkv: float32 [768, 2304], P('batch', ('pb', 'ka'))
- grad_proj: float32 [768, 768], P('batch', ('pb', 'ka'))
- grad_up: float32 [768, 3072], P('batch', ('pb', 'ka'))
- grad_down: float32 [3072, 768], P('batch', ('pb', 'ka'))
- grad_norms: float32 [4, 768], P(None, ('pb', 'ka'))
The draws below stay inside these ranges and needn't reach their ends.
Inputs may be any that keep to these rules, and one draw needn't show every extreme that they name: Each row of block_place lists every number 0 to 7 exactly once.
All inputs are finite; a program needn't handle non-finite values.
Results may differ from the reference program's by a relative error of at most 0.015.
The reference program's roundings to bfloat16 on the way count: a program that leaves them out, or rounds other values in their place, can miss the bound.
Values may be sent and summed in bfloat16 or wider, within the bound.
No kernel may reach another device: no remote copies, remote signals or barrier semaphores. Data moves between devices by JAX's collectives and lax.ppermute only.
A program may use at most 192 MiB of HBM per device.

```python
import jax
import jax.numpy as jnp
from jax import lax

D = 768
FF = 3072
HEADS = 12
HEAD = 64
SEQ_LEN = 1024
NBLK = 8
BLOCK = 128
SEQS = 16


def spiked(values, stream_key, source, target, shards_of, factor):
    owner, partner = [(jnp.arange(values.shape[dim]) // (values.shape[dim] // shards_of)).reshape([-1 if axis == dim else 1 for axis in range(values.ndim)]) for dim in (source, target)]
    chosen = jax.random.permutation(stream_key, shards_of)[partner]
    strong = (owner == chosen) | (owner == (partner + shards_of // 2) % shards_of)
    return jnp.where(strong, factor * values, values)


def shard_levels(key, extent, shards, low, top_value):
    level = 1.0
    for dim, shards_of in shards:
        heights = jax.random.uniform(jax.random.fold_in(jax.random.fold_in(key, 6), dim), (shards_of,), jnp.float32, low / len(shards), top_value / len(shards))
        level = level * jnp.repeat(jnp.exp(heights), extent[dim] // shards_of).reshape((-1,) + (1,) * (len(extent) - 1 - dim))
    return level


def bell_draw(rng, extent, deviation, bound, shards=(), kind=jnp.bfloat16):
    values = deviation * jax.random.normal(rng, extent, jnp.float32)
    if shards:
        values = values * shard_levels(rng, extent, shards, -0.22, 0.18)
    return jnp.clip(values, -bound, bound).astype(kind)


def heavy_noise(stream_key, dims, scale, reach, split, heavy, held_as=jnp.bfloat16):
    drawn = scale * jax.random.normal(stream_key, dims, jnp.float32)
    if split:
        drawn = drawn * shard_levels(stream_key, dims, split, -0.22, 0.18)
    return jnp.clip(spiked(drawn, jax.random.fold_in(stream_key, 3), *heavy), -reach, reach).astype(held_as)


def setup_inputs(seed: int = 0) -> dict:
    splits = jax.random.split(jax.random.key(seed), 12)
    return {
        "inputs": heavy_noise(splits[0], (SEQS, SEQ_LEN, D), 1.0, 6.0, ((0, 4), (1, 8)), (0, 2, 4, 2.0)),
        "block_place": jax.vmap(lambda own: jax.random.permutation(own, NBLK))(jax.random.split(splits[1], SEQS)).reshape((SEQS, NBLK)).astype(jnp.int32),
        "ln1_gain": jnp.clip(1.0 + 0.18 * jax.random.normal(splits[2], (D,), jnp.float32), 0.1, 1.9),
        "ln1_shift": bell_draw(splits[3], (D,), 0.5, 3.0, (), jnp.float32),
        "w_qkv": bell_draw(splits[4], (D, 3 * D), D ** -0.5, 0.21875),
        "w_out": bell_draw(splits[5], (D, D), (D // 32) ** -0.5, 1.25),
        "ln2_gain": jnp.clip(1.0 + 0.18 * jax.random.normal(splits[6], (D,), jnp.float32), 0.1, 1.9),
        "ln2_shift": bell_draw(splits[7], (D,), 0.5, 3.0, (), jnp.float32),
        "w_up": bell_draw(splits[8], (D, FF), D ** -0.5, 0.21875),
        "w_down": bell_draw(splits[9], (FF, D), FF ** -0.5, 0.109375),
        "cotangent": bell_draw(splits[10], (SEQS, SEQ_LEN, D), 1.0, 6.0, ((0, 4), (1, 8))),
    }


@jax.custom_vjp
def low(v):
    return lax.optimization_barrier(v.astype(jnp.bfloat16)).astype(jnp.float32)

@jax.custom_vjp
def low_back(v):
    return v

def low_keep(v):
    return (low(v), None)

def low_pass(kept, grad):
    return (grad,)

def back_keep(v):
    return (v, None)

def back_low(kept, grad):
    return (low(grad),)
low.defvjp(low_keep, low_pass)
low_back.defvjp(back_keep, back_low)
highest = lax.Precision.HIGHEST
norm_eps = 1e-05

def norm_rows(values, gain_vec, shift_vec):
    average = lax.optimization_barrier(jnp.mean(values, axis=-1, keepdims=True))
    centred = values - average
    spread = lax.optimization_barrier(jnp.mean(centred * centred, axis=-1, keepdims=True))
    return centred * lax.rsqrt(spread + norm_eps) * gain_vec + shift_vec

def gelu_tanh(values):
    return jax.nn.gelu(values, approximate=True)

def split_heads(matrix):
    return matrix.reshape(matrix.shape[0], matrix.shape[1], HEADS, HEAD)

def attend(queries, key_rows, value_rows, positions):
    factor = HEAD ** (-0.5)
    scores = low_back(factor * jnp.einsum('bqhe,bkhe->bhqk', queries, key_rows, precision=highest))
    visible = positions[:, None, None, :] <= positions[:, None, :, None]
    magnitude = jnp.abs(scores)
    row_peak = lax.optimization_barrier(jnp.max(jnp.where(visible, magnitude, -1e+30), axis=-1, keepdims=True))
    exponents = jnp.exp(jnp.where(visible, magnitude - row_peak, -1e+30))
    totals = lax.optimization_barrier(jnp.sum(exponents, axis=-1, keepdims=True))
    weights = low(jnp.sign(scores) * (exponents / totals))
    return jnp.einsum('bhqk,bkhe->bqhe', weights, value_rows, precision=highest)

def forward(params, source, positions):
    gain1, shift1, w_qkv, w_out, gain2, shift2, w_up, w_down = params
    seq_count = source.shape[0]
    normed1 = low(norm_rows(source, gain1, shift1))
    packed = low(low_back(jnp.einsum('btd,de->bte', normed1, w_qkv, precision=highest)))
    queries = split_heads(packed[..., :D])
    key_rows = split_heads(packed[..., D:2 * D])
    value_rows = split_heads(packed[..., 2 * D:])
    attended = jax.checkpoint(attend)(queries, key_rows, value_rows, positions)
    attended = low(low_back(attended.reshape(seq_count, SEQ_LEN, D)))
    residual = source + low_back(jnp.einsum('btd,de->bte', attended, w_out, precision=highest))
    normed2 = low(norm_rows(residual, gain2, shift2))
    hidden = low(gelu_tanh(low_back(jnp.einsum('btd,df->btf', normed2, w_up, precision=highest))))
    return residual + jnp.einsum('btf,fd->btd', hidden, w_down, precision=highest)

def reference(inputs, block_place, ln1_gain, ln1_shift, w_qkv, w_out, ln2_gain, ln2_shift, w_up, w_down, cotangent):
    params = tuple((element.astype(jnp.float32) for element in (ln1_gain, ln1_shift, w_qkv, w_out, ln2_gain, ln2_shift, w_up, w_down)))
    offsets = jnp.arange(SEQ_LEN, dtype=jnp.int32)
    slot_ids = (offsets // BLOCK).astype(jnp.int32)
    positions = (jnp.take(block_place, slot_ids, axis=1) * BLOCK + (offsets % BLOCK)[None, :]).astype(jnp.int32)
    groups = SEQS // 2
    source = inputs.astype(jnp.float32).reshape(groups, 2, SEQ_LEN, D)
    places = positions.reshape(groups, 2, SEQ_LEN)
    seed_rows = cotangent.astype(jnp.float32).reshape(groups, 2, SEQ_LEN, D)

    def one_group(grad_sums, pieces):
        group_source, group_pos, group_seed = pieces

        def apply_layer(weights_in, source_in):
            return forward(weights_in, source_in, group_pos)
        result, pullback = jax.vjp(apply_layer, params, group_source)
        grad_params, grad_source = pullback(group_seed)
        grad_sums = jax.tree.map(jnp.add, grad_sums, grad_params)
        return (grad_sums, (result.astype(jnp.bfloat16), grad_source.astype(jnp.bfloat16)))
    zeros_init = tuple((jnp.zeros_like(element) for element in params))
    grad_sums, (outputs, grad_inputs) = lax.scan(one_group, zeros_init, (source, places, seed_rows))
    outputs = outputs.reshape(SEQS, SEQ_LEN, D)
    grad_inputs = grad_inputs.reshape(SEQS, SEQ_LEN, D)
    grad_norms = jnp.stack([grad_sums[0], grad_sums[1], grad_sums[4], grad_sums[5]])
    return (outputs, grad_inputs, grad_sums[2], grad_sums[3], grad_sums[6], grad_sums[7], grad_norms)
```

```python
import functools

import jax
import jax.numpy as jnp
from jax import lax
from jax.experimental import pallas as pl
from jax.experimental.pallas import tpu as pltpu
from jax.sharding import PartitionSpec as P

HEADS = 12
HEAD = 64
PAIR = 2 * HEAD
QTILE = 256
SCALE = HEAD ** (-0.5)
HUGE = 3e38
HIDDEN = -1e30

norm_eps = 1e-05
BF16 = jnp.bfloat16
F32 = jnp.float32


def norm_rows(values, gain_vec, shift_vec):
    average = jnp.mean(values, axis=-1, keepdims=True)
    centred = values - average
    spread = jnp.mean(centred * centred, axis=-1, keepdims=True)
    return centred * lax.rsqrt(spread + norm_eps) * gain_vec + shift_vec


def gelu_tanh(values):
    return jax.nn.gelu(values, approximate=True)


def dot(a, b, contract):
    return lax.dot_general(a, b, ((contract[:1], contract[1:]), ((), ())), preferred_element_type=F32)


def project_kernel(seqs, halves, pairs, x_ref, gain_ref, shift_ref, w_ref, *refs):
    out_refs, normed_ref = refs[:pairs], refs[pairs]
    rows = x_ref.shape[0] // seqs

    @pl.when(pl.program_id(0) == 0)
    def _():
        normed_ref[...] = norm_rows(x_ref[...].astype(F32), gain_ref[...], shift_ref[...]).astype(BF16)

    part = jnp.dot(normed_ref[...], w_ref[...], preferred_element_type=F32).astype(BF16)
    for pair in range(pairs):
        for half in range(halves):
            col = (half * pairs + pair) * PAIR
            for seq in range(seqs):
                out_refs[pair][half * seqs + seq] = part[seq * rows : (seq + 1) * rows, col : col + PAIR]


def project(x, gain, shift, w_qkv, halves):
    seqs, rows, width = x.shape
    pairs = width // PAIR // halves
    tokens = seqs * rows
    outs = [jax.ShapeDtypeStruct((halves * seqs, rows, 3 * PAIR), BF16)] * pairs
    whole = lambda g: (0, 0)
    return pl.pallas_call(
        functools.partial(project_kernel, seqs, halves, pairs),
        grid=(3,),
        in_specs=[
            pl.BlockSpec((tokens, width), whole),
            pl.BlockSpec((1, width), whole),
            pl.BlockSpec((1, width), whole),
            pl.BlockSpec((width, width), lambda g: (0, g)),
        ],
        out_specs=[pl.BlockSpec((halves * seqs, rows, PAIR), lambda g: (0, 0, g))] * pairs
        + [pl.BlockSpec((tokens, width), whole)],
        out_shape=outs + [jax.ShapeDtypeStruct((tokens, width), BF16)],
        cost_estimate=pl.CostEstimate(
            flops=6 * tokens * width * width, bytes_accessed=9 * width * width, transcendentals=0
        ),
        name="project",
    )(x.reshape(tokens, width), gain[None], shift[None], w_qkv)


def head_lanes(values, head):
    lane = lax.broadcasted_iota(jnp.int32, values.shape, 1)
    mine = lane < HEAD if head == 0 else lane >= HEAD
    return jnp.where(mine, values, jnp.zeros_like(values))


def gather_rows(place_ref, source_ref, columns, target_ref):
    blocks, rows = source_ref.shape[0], source_ref.shape[1]
    for block in range(blocks):
        at = pl.multiple_of(place_ref[block] * rows, rows)
        target_ref[pl.ds(at, rows), :] = source_ref[block, :, columns]


def scatter_rows(place_ref, source_ref, target_ref, columns):
    blocks, rows = target_ref.shape[0], target_ref.shape[1]
    for block in range(blocks):
        at = pl.multiple_of(place_ref[block] * rows, rows)
        target_ref[block, :, columns] = source_ref[pl.ds(at, rows), :].astype(target_ref.dtype)


def hide_later(magnitude):
    keys = magnitude.shape[0]
    key = lax.broadcasted_iota(jnp.int32, (QTILE, QTILE), 0)
    query = lax.broadcasted_iota(jnp.int32, (QTILE, QTILE), 1)
    last = jnp.where(key <= query, magnitude[keys - QTILE :], HIDDEN)
    return last if keys == QTILE else jnp.concatenate([magnitude[: keys - QTILE], last], axis=0)


def sign_of(scores):
    return jnp.clip(scores * HUGE, -1.0, 1.0)


def attend_kernel(place_ref, x_ref, out_ref, sums_ref, stats_ref, q_sc, k_sc, v_sc, o_sc):
    gather_rows(place_ref, x_ref, slice(0, PAIR), q_sc)
    gather_rows(place_ref, x_ref, slice(PAIR, 2 * PAIR), k_sc)
    gather_rows(place_ref, x_ref, slice(2 * PAIR, 3 * PAIR), v_sc)
    total_rows = q_sc.shape[0]
    v_t = v_sc[...].T
    for tile in range(total_rows // QTILE):
        span = slice(tile * QTILE, (tile + 1) * QTILE)
        keys = (tile + 1) * QTILE
        queries = q_sc[span, :] * SCALE
        for head in range(2):
            scores = dot(k_sc[:keys, :], head_lanes(queries, head).astype(BF16), (1, 1))
            magnitude = hide_later(jnp.abs(scores))
            peak = jnp.max(magnitude, axis=0, keepdims=True)
            exponents = jnp.exp(magnitude - peak)
            total = jnp.sum(exponents, axis=0, keepdims=True)
            weights = (exponents * sign_of(scores)).astype(BF16)
            summed = dot(v_t[head * HEAD : (head + 1) * HEAD, :keys], weights, (1, 0))
            sums_ref[head * HEAD : (head + 1) * HEAD, span] = summed / total
            stats_ref[head : head + 1, span] = peak + jnp.log(total)
        o_sc[span, :] = sums_ref[:, span].T
    scatter_rows(place_ref, o_sc, out_ref, slice(None))


def attend(place, x):
    blocks, rows, _ = x.shape
    length = blocks * rows
    area = length * length
    return pl.pallas_call(
        attend_kernel,
        grid_spec=pltpu.PrefetchScalarGridSpec(
            num_scalar_prefetch=1,
            grid=(1,),
            in_specs=[pl.BlockSpec(x.shape, lambda i, p: (0, 0, 0))],
            out_specs=[
                pl.BlockSpec((blocks, rows, PAIR), lambda i, p: (0, 0, 0)),
                pl.BlockSpec((PAIR, length), lambda i, p: (0, 0)),
                pl.BlockSpec((8, length), lambda i, p: (0, 0)),
            ],
            scratch_shapes=[pltpu.VMEM((length, PAIR), BF16)] * 3 + [pltpu.VMEM((length, PAIR), F32)],
        ),
        out_shape=[
            jax.ShapeDtypeStruct((blocks, rows, PAIR), BF16),
            jax.ShapeDtypeStruct((PAIR, length), F32),
            jax.ShapeDtypeStruct((8, length), F32),
        ],
        cost_estimate=pl.CostEstimate(
            flops=16 * area * HEAD, bytes_accessed=4 * length * PAIR * 4, transcendentals=area
        ),
        name="attend",
    )(place, x)


def attend_back_kernel(
    place_ref, x_ref, g_ref, sums_ref, stats_ref, out_ref, q_sc, k_sc, v_sc, g_sc, dq_sc, dk_sc, dv_sc
):
    gather_rows(place_ref, x_ref, slice(0, PAIR), q_sc)
    gather_rows(place_ref, x_ref, slice(PAIR, 2 * PAIR), k_sc)
    gather_rows(place_ref, x_ref, slice(2 * PAIR, 3 * PAIR), v_sc)
    gather_rows(place_ref, g_ref, slice(0, PAIR), g_sc)
    total_rows = q_sc.shape[0]
    k_t = k_sc[...].T
    g_t = g_sc[...].astype(F32).T
    products = g_t * sums_ref[...]
    deltas = [
        jnp.sum(products[head * HEAD : (head + 1) * HEAD], axis=0, keepdims=True) for head in range(2)
    ]
    dk_sc[...] = jnp.zeros_like(dk_sc)
    dv_sc[...] = jnp.zeros_like(dv_sc)
    for tile in range(total_rows // QTILE):
        span = slice(tile * QTILE, (tile + 1) * QTILE)
        keys = (tile + 1) * QTILE
        queries = q_sc[span, :] * SCALE
        parts = []
        for head in range(2):
            q_head = head_lanes(queries, head).astype(BF16)
            g_head = head_lanes(g_sc[span, :], head)
            scores = dot(k_sc[:keys, :], q_head, (1, 1))
            magnitude = hide_later(jnp.abs(scores))
            sign = sign_of(scores)
            signed = jnp.exp(magnitude - stats_ref[head : head + 1, span]) * sign
            grad_weights = dot(v_sc[:keys, :], g_head, (1, 1))
            grad_scores = (signed * (sign * grad_weights - deltas[head][:, span])).astype(BF16)
            dv_sc[:keys, :] += dot(signed.astype(BF16), g_head, (1, 0))
            dk_sc[:keys, :] += dot(grad_scores, q_head, (1, 0))
            parts.append(dot(k_t[head * HEAD : (head + 1) * HEAD, :keys], grad_scores, (1, 0)))
        dq_sc[span, :] = jnp.concatenate(parts, axis=0).T * SCALE
    scatter_rows(place_ref, dq_sc, out_ref, slice(0, PAIR))
    scatter_rows(place_ref, dk_sc, out_ref, slice(PAIR, 2 * PAIR))
    scatter_rows(place_ref, dv_sc, out_ref, slice(2 * PAIR, 3 * PAIR))


def attend_back(place, x, grad, sums, stats):
    blocks, rows, _ = x.shape
    length = blocks * rows
    area = length * length
    block3 = lambda i, p: (0, 0, 0)
    block2 = lambda i, p: (0, 0)
    return pl.pallas_call(
        attend_back_kernel,
        grid_spec=pltpu.PrefetchScalarGridSpec(
            num_scalar_prefetch=1,
            grid=(1,),
            in_specs=[
                pl.BlockSpec(x.shape, block3),
                pl.BlockSpec(grad.shape, block3),
                pl.BlockSpec(sums.shape, block2),
                pl.BlockSpec(stats.shape, block2),
            ],
            out_specs=pl.BlockSpec(x.shape, block3),
            scratch_shapes=[pltpu.VMEM((length, PAIR), BF16)] * 4 + [pltpu.VMEM((length, PAIR), F32)] * 3,
        ),
        out_shape=jax.ShapeDtypeStruct(x.shape, BF16),
        cost_estimate=pl.CostEstimate(
            flops=40 * area * HEAD, bytes_accessed=8 * length * PAIR * 4, transcendentals=area
        ),
        name="attend_back",
    )(place, x, grad, sums, stats)


def exchange(blocks):
    return lax.all_to_all(blocks, ("pb", "ka"), 0, 0, tiled=True)


def shards(
    inputs,
    block_place,
    ln1_gain,
    ln1_shift,
    w_qkv,
    w_out,
    ln2_gain,
    ln2_shift,
    w_up,
    w_down,
    cotangent,
):
    seqs, rows, width = inputs.shape
    halves = lax.axis_size("pb")
    pairs = width // PAIR // halves
    place = lax.dynamic_index_in_dim(block_place, lax.axis_index("ka"), 0, False)
    *sent, normed1 = project(inputs, ln1_gain, ln1_shift, w_qkv, halves)
    normed1 = normed1.reshape(seqs, rows, width)
    packed = [exchange(s) for s in sent]
    attended, saved = [], []
    for x in packed:
        out, sums, stats = attend(place, x)
        saved.append((sums, stats))
        attended.append(exchange(out))

    def join(pieces):
        stacked = jnp.stack(pieces)
        kinds = stacked.shape[-1] // PAIR
        stacked = stacked.reshape(pairs, halves, seqs, rows, kinds, PAIR)
        return stacked.transpose(2, 3, 4, 1, 0, 5).reshape(seqs, rows, kinds * width)

    def split(whole):
        cut = whole.reshape(seqs, rows, halves, pairs, PAIR).transpose(3, 2, 0, 1, 4)
        return [cut[p].reshape(halves * seqs, rows, PAIR) for p in range(pairs)]

    attended = join(attended)
    source = inputs.astype(jnp.float32)
    residual = source + jnp.einsum(
        "btd,de->bte", attended, w_out, preferred_element_type=jnp.float32
    )
    normed2, second_back = jax.vjp(norm_rows, residual, ln2_gain, ln2_shift)
    normed2 = normed2.astype(jnp.bfloat16)
    pre_act = jnp.einsum("btd,df->btf", normed2, w_up, preferred_element_type=jnp.float32)
    active, gelu_back = jax.vjp(gelu_tanh, pre_act)
    active = active.astype(jnp.bfloat16)
    outputs = (
        residual + jnp.einsum("btf,fd->btd", active, w_down, preferred_element_type=jnp.float32)
    ).astype(jnp.bfloat16)
    grad_down = jnp.einsum("btf,btd->fd", active, cotangent, preferred_element_type=jnp.float32)
    grad_act = jnp.einsum("btd,fd->btf", cotangent, w_down, preferred_element_type=jnp.float32)
    grad_pre = gelu_back(grad_act)[0].astype(jnp.bfloat16)
    grad_up = jnp.einsum("btd,btf->df", normed2, grad_pre, preferred_element_type=jnp.float32)
    grad_normed2 = jnp.einsum("btf,df->btd", grad_pre, w_up, preferred_element_type=jnp.float32)
    grad_res, grad_gain2, grad_shift2 = second_back(grad_normed2)
    grad_res = grad_res + cotangent.astype(jnp.float32)
    grad_z = grad_res.astype(jnp.bfloat16)
    grad_proj = jnp.einsum("btd,bte->de", attended, grad_z, preferred_element_type=jnp.float32)
    grad_att = jnp.einsum("bte,de->btd", grad_z, w_out, preferred_element_type=jnp.float32).astype(
        jnp.bfloat16
    )
    grads = []
    for x, g, (sums, stats) in zip(packed, split(grad_att), saved):
        grads.append(exchange(attend_back(place, x, exchange(g), sums, stats)))
    grad_packed = join(grads)
    grad_qkv = jnp.einsum("btd,bte->de", normed1, grad_packed, preferred_element_type=jnp.float32)
    grad_normed1 = jnp.einsum("bte,de->btd", grad_packed, w_qkv, preferred_element_type=jnp.float32)
    _, first_back = jax.vjp(norm_rows, source, ln1_gain, ln1_shift)
    grad_source, grad_gain1, grad_shift1 = first_back(grad_normed1)
    grad_inputs = (grad_res + grad_source).astype(jnp.bfloat16)
    norm_local = jnp.stack([grad_gain1, grad_shift1, grad_gain2, grad_shift2])

    def scatter(g):
        g = lax.psum_scatter(g.astype(BF16), "batch", scatter_dimension=0, tiled=True)
        return lax.psum_scatter(g, ("pb", "ka"), scatter_dimension=1, tiled=True).astype(F32)

    norm_sum = lax.psum(
        lax.psum_scatter(norm_local, ("pb", "ka"), scatter_dimension=1, tiled=True), "batch"
    )
    return (
        outputs,
        grad_inputs,
        scatter(grad_qkv),
        scatter(grad_proj),
        scatter(grad_up),
        scatter(grad_down),
        norm_sum,
    )


def solution(mesh):
    placed = (
        P("batch", ("pb", "ka"), None),
        P("batch", None),
        P(),
        P(),
        P(),
        P(),
        P(),
        P(),
        P(),
        P(),
        P("batch", ("pb", "ka"), None),
    )
    return jax.shard_map(
        shards,
        mesh=mesh,
        in_specs=placed,
        out_specs=(
            P("batch", ("pb", "ka"), None),
            P("batch", ("pb", "ka"), None),
            P("batch", ("pb", "ka")),
            P("batch", ("pb", "ka")),
            P("batch", ("pb", "ka")),
            P("batch", ("pb", "ka")),
            P(None, ("pb", "ka")),
        ),
        check_vma=False,
    )
```

```python
import functools

import jax
import jax.numpy as jnp
from jax import lax
from jax.experimental import pallas as pl
from jax.experimental.pallas import tpu as pltpu
from jax.sharding import PartitionSpec as P

HEADS = 12
HEAD = 64
PAIR = 2 * HEAD
QTILE = 256
SCALE = HEAD ** (-0.5)
HUGE = 3e38
HIDDEN = -1e30

norm_eps = 1e-05
BF16 = jnp.bfloat16
F32 = jnp.float32


def norm_rows(values, gain_vec, shift_vec):
    average = jnp.mean(values, axis=-1, keepdims=True)
    centred = values - average
    spread = jnp.mean(centred * centred, axis=-1, keepdims=True)
    return centred * lax.rsqrt(spread + norm_eps) * gain_vec + shift_vec


def gelu_tanh(values):
    return jax.nn.gelu(values, approximate=True)


def dot(a, b, contract):
    return lax.dot_general(a, b, ((contract[:1], contract[1:]), ((), ())), preferred_element_type=F32)


def project_kernel(seqs, halves, first, *refs):
    if first:
        x_ref, gain_ref, shift_ref, *w_refs, out_ref, normed_ref = refs
        normed_ref[...] = norm_rows(x_ref[...].astype(F32), gain_ref[...], shift_ref[...]).astype(BF16)
    else:
        normed_ref, *w_refs, out_ref = refs
    rows = normed_ref.shape[0] // seqs
    weights = jnp.concatenate([w[...] for w in w_refs], axis=1)
    part = jnp.dot(normed_ref[...], weights, preferred_element_type=F32).astype(BF16)
    for half in range(halves):
        for seq in range(seqs):
            out_ref[half * seqs + seq] = part[
                seq * rows : (seq + 1) * rows, half * 3 * PAIR : (half + 1) * 3 * PAIR
            ]


def pair_columns(width, halves, pair, order):
    pairs = width // PAIR // halves
    return [
        pl.BlockSpec((width, PAIR), functools.partial(order, kind * (width // PAIR) + half * pairs + pair))
        for half in range(halves)
        for kind in range(3)
    ]


def project(x, gain, shift, w_qkv, halves, pair, normed=None):
    seqs, rows, width = x.shape
    tokens = seqs * rows
    whole = lambda i: (0, 0)
    first = normed is None
    ahead = (
        [x.reshape(tokens, width), gain[None], shift[None]] if first else [normed]
    )
    specs = [pl.BlockSpec(a.shape, whole) for a in ahead]
    columns = pair_columns(width, halves, pair, lambda c, i: (0, c))
    out_shape = [jax.ShapeDtypeStruct((halves * seqs, rows, 3 * PAIR), BF16)]
    out_specs = [pl.BlockSpec(out_shape[0].shape, lambda i: (0, 0, 0))]
    if first:
        out_shape.append(jax.ShapeDtypeStruct((tokens, width), BF16))
        out_specs.append(pl.BlockSpec((tokens, width), whole))
    outs = pl.pallas_call(
        functools.partial(project_kernel, seqs, halves, first),
        grid=(1,),
        in_specs=specs + columns,
        out_specs=out_specs,
        out_shape=out_shape,
        cost_estimate=pl.CostEstimate(
            flops=2 * tokens * width * len(columns) * PAIR, bytes_accessed=5 * width * width, transcendentals=0
        ),
        name="project",
    )(*ahead, *([w_qkv] * len(columns)))
    return outs if first else (outs[0], normed)


def head_lanes(values, head):
    lane = lax.broadcasted_iota(jnp.int32, values.shape, 1)
    mine = lane < HEAD if head == 0 else lane >= HEAD
    return jnp.where(mine, values, jnp.zeros_like(values))


def gather_rows(place_ref, source_ref, columns, target_ref):
    blocks, rows = source_ref.shape[0], source_ref.shape[1]
    for block in range(blocks):
        at = pl.multiple_of(place_ref[block] * rows, rows)
        target_ref[pl.ds(at, rows), :] = source_ref[block, :, columns]


def scatter_rows(place_ref, source_ref, target_ref, columns):
    blocks, rows = target_ref.shape[0], target_ref.shape[1]
    for block in range(blocks):
        at = pl.multiple_of(place_ref[block] * rows, rows)
        target_ref[block, :, columns] = source_ref[pl.ds(at, rows), :].astype(target_ref.dtype)


def hide_later(magnitude):
    keys = magnitude.shape[0]
    key = lax.broadcasted_iota(jnp.int32, (QTILE, QTILE), 0)
    query = lax.broadcasted_iota(jnp.int32, (QTILE, QTILE), 1)
    last = jnp.where(key <= query, magnitude[keys - QTILE :], HIDDEN)
    return last if keys == QTILE else jnp.concatenate([magnitude[: keys - QTILE], last], axis=0)


def sign_of(scores):
    return jnp.clip(scores * HUGE, -1.0, 1.0)


def attend_kernel(place_ref, x_ref, out_ref, sums_ref, stats_ref, q_sc, k_sc, v_sc, o_sc):
    gather_rows(place_ref, x_ref, slice(0, PAIR), q_sc)
    gather_rows(place_ref, x_ref, slice(PAIR, 2 * PAIR), k_sc)
    gather_rows(place_ref, x_ref, slice(2 * PAIR, 3 * PAIR), v_sc)
    total_rows = q_sc.shape[0]
    v_t = v_sc[...].T
    for tile in range(total_rows // QTILE):
        span = slice(tile * QTILE, (tile + 1) * QTILE)
        keys = (tile + 1) * QTILE
        queries = q_sc[span, :] * SCALE
        for head in range(2):
            scores = dot(k_sc[:keys, :], head_lanes(queries, head).astype(BF16), (1, 1))
            magnitude = hide_later(jnp.abs(scores))
            peak = jnp.max(magnitude, axis=0, keepdims=True)
            exponents = jnp.exp(magnitude - peak)
            total = jnp.sum(exponents, axis=0, keepdims=True)
            weights = (exponents * sign_of(scores)).astype(BF16)
            summed = dot(v_t[head * HEAD : (head + 1) * HEAD, :keys], weights, (1, 0))
            sums_ref[head * HEAD : (head + 1) * HEAD, span] = summed / total
            stats_ref[head : head + 1, span] = peak + jnp.log(total)
        o_sc[span, :] = sums_ref[:, span].T
    scatter_rows(place_ref, o_sc, out_ref, slice(None))


def attend(place, x):
    blocks, rows, _ = x.shape
    length = blocks * rows
    area = length * length
    return pl.pallas_call(
        attend_kernel,
        grid_spec=pltpu.PrefetchScalarGridSpec(
            num_scalar_prefetch=1,
            grid=(1,),
            in_specs=[pl.BlockSpec(x.shape, lambda i, p: (0, 0, 0))],
            out_specs=[
                pl.BlockSpec((blocks, rows, PAIR), lambda i, p: (0, 0, 0)),
                pl.BlockSpec((PAIR, length), lambda i, p: (0, 0)),
                pl.BlockSpec((8, length), lambda i, p: (0, 0)),
            ],
            scratch_shapes=[pltpu.VMEM((length, PAIR), BF16)] * 3 + [pltpu.VMEM((length, PAIR), F32)],
        ),
        out_shape=[
            jax.ShapeDtypeStruct((blocks, rows, PAIR), BF16),
            jax.ShapeDtypeStruct((PAIR, length), F32),
            jax.ShapeDtypeStruct((8, length), F32),
        ],
        cost_estimate=pl.CostEstimate(
            flops=16 * area * HEAD, bytes_accessed=4 * length * PAIR * 4, transcendentals=area
        ),
        name="attend",
    )(place, x)


def attend_back_kernel(
    place_ref, x_ref, g_ref, sums_ref, stats_ref, out_ref, q_sc, k_sc, v_sc, g_sc, dq_sc, dk_sc, dv_sc
):
    gather_rows(place_ref, x_ref, slice(0, PAIR), q_sc)
    gather_rows(place_ref, x_ref, slice(PAIR, 2 * PAIR), k_sc)
    gather_rows(place_ref, x_ref, slice(2 * PAIR, 3 * PAIR), v_sc)
    gather_rows(place_ref, g_ref, slice(0, PAIR), g_sc)
    total_rows = q_sc.shape[0]
    k_t = k_sc[...].T
    g_t = g_sc[...].astype(F32).T
    products = g_t * sums_ref[...]
    deltas = [
        jnp.sum(products[head * HEAD : (head + 1) * HEAD], axis=0, keepdims=True) for head in range(2)
    ]
    dk_sc[...] = jnp.zeros_like(dk_sc)
    dv_sc[...] = jnp.zeros_like(dv_sc)
    for tile in range(total_rows // QTILE):
        span = slice(tile * QTILE, (tile + 1) * QTILE)
        keys = (tile + 1) * QTILE
        queries = q_sc[span, :] * SCALE
        parts = []
        for head in range(2):
            q_head = head_lanes(queries, head).astype(BF16)
            g_head = head_lanes(g_sc[span, :], head)
            scores = dot(k_sc[:keys, :], q_head, (1, 1))
            magnitude = hide_later(jnp.abs(scores))
            sign = sign_of(scores)
            signed = jnp.exp(magnitude - stats_ref[head : head + 1, span]) * sign
            grad_weights = dot(v_sc[:keys, :], g_head, (1, 1))
            grad_scores = (signed * (sign * grad_weights - deltas[head][:, span])).astype(BF16)
            dv_sc[:keys, :] += dot(signed.astype(BF16), g_head, (1, 0))
            dk_sc[:keys, :] += dot(grad_scores, q_head, (1, 0))
            parts.append(dot(k_t[head * HEAD : (head + 1) * HEAD, :keys], grad_scores, (1, 0)))
        dq_sc[span, :] = jnp.concatenate(parts, axis=0).T * SCALE
    scatter_rows(place_ref, dq_sc, out_ref, slice(0, PAIR))
    scatter_rows(place_ref, dk_sc, out_ref, slice(PAIR, 2 * PAIR))
    scatter_rows(place_ref, dv_sc, out_ref, slice(2 * PAIR, 3 * PAIR))


def attend_back(place, x, grad, sums, stats):
    blocks, rows, _ = x.shape
    length = blocks * rows
    area = length * length
    block3 = lambda i, p: (0, 0, 0)
    block2 = lambda i, p: (0, 0)
    return pl.pallas_call(
        attend_back_kernel,
        grid_spec=pltpu.PrefetchScalarGridSpec(
            num_scalar_prefetch=1,
            grid=(1,),
            in_specs=[
                pl.BlockSpec(x.shape, block3),
                pl.BlockSpec(grad.shape, block3),
                pl.BlockSpec(sums.shape, block2),
                pl.BlockSpec(stats.shape, block2),
            ],
            out_specs=pl.BlockSpec(x.shape, block3),
            scratch_shapes=[pltpu.VMEM((length, PAIR), BF16)] * 4 + [pltpu.VMEM((length, PAIR), F32)] * 3,
        ),
        out_shape=jax.ShapeDtypeStruct(x.shape, BF16),
        cost_estimate=pl.CostEstimate(
            flops=40 * area * HEAD, bytes_accessed=8 * length * PAIR * 4, transcendentals=area
        ),
        name="attend_back",
    )(place, x, grad, sums, stats)


def gelu_pair(u):
    c = 0.7978845608028654
    square = u * u
    t = jnp.tanh(c * u * (1.0 + 0.044715 * square))
    half = 0.5 * (1.0 + t)
    slope = half + 0.5 * c * u * (1.0 - t * t) * (1.0 + 3.0 * 0.044715 * square)
    return u * half, slope


def norm_back(values, gain_vec, grad):
    average = jnp.mean(values, axis=-1, keepdims=True)
    centred = values - average
    spread = jnp.mean(centred * centred, axis=-1, keepdims=True)
    scale = lax.rsqrt(spread + norm_eps)
    unit = centred * scale
    scaled = grad * gain_vec
    back = scale * (
        scaled
        - jnp.mean(scaled, axis=-1, keepdims=True)
        - unit * jnp.mean(scaled * unit, axis=-1, keepdims=True)
    )
    return back, jnp.sum(grad * unit, axis=0, keepdims=True), jnp.sum(grad, axis=0, keepdims=True)


def ff_kernel(seqs, halves, pairs, plane, *refs):
    me_ref, x_ref, *refs = refs
    att_refs, refs = refs[:pairs], refs[pairs:]
    cot_ref, w_out_ref, gain_ref, shift_ref, up_ref, down_ref, *refs = refs
    out_ref, res_ref, *refs = refs
    ga_refs, refs = refs[:pairs], refs[pairs:]
    norm_ref, gu_send, gu_keep, gd_send, gd_keep, gp_send, gp_keep, *refs = refs
    att_sc, residual_sc, normed_sc, normed_t, turned_sc, acc_out, acc_grad = refs
    step = pl.program_id(0)
    tokens, width = x_ref.shape
    rows = tokens // seqs
    block = width // plane
    near = plane // 2

    def turn(values):
        turned = values.T
        for j in range(plane):
            t = me_ref[0] ^ j
            slot = (1 - (t & 1)) * near + (t >> 1)
            at = pl.multiple_of(slot * block, block)
            turned_sc[pl.ds(at, block), :] = turned[j * block : (j + 1) * block]

    @pl.when(step == 0)
    def _():
        for pair in range(pairs):
            for half in range(halves):
                col = (half * pairs + pair) * PAIR
                for seq in range(seqs):
                    att_sc[seq * rows : (seq + 1) * rows, col : col + PAIR] = att_refs[pair][half * seqs + seq]
        residual = x_ref[...].astype(F32) + jnp.dot(att_sc[...], w_out_ref[...], preferred_element_type=F32)
        residual_sc[...] = residual
        normed = norm_rows(residual, gain_ref[...], shift_ref[...]).astype(BF16)
        normed_sc[...] = normed
        normed_t[...] = normed.T
        turn(cot_ref[...])
        acc_out[...] = jnp.zeros_like(acc_out)
        acc_grad[...] = jnp.zeros_like(acc_grad)

    pre = jnp.dot(normed_sc[...], up_ref[...], preferred_element_type=F32)
    active, slope = gelu_pair(pre)
    active = active.astype(BF16)
    grad_pre = (dot(cot_ref[...], down_ref[...], (1, 1)) * slope).astype(BF16)
    acc_out[...] += jnp.dot(active, down_ref[...], preferred_element_type=F32)
    acc_grad[...] += dot(grad_pre, up_ref[...], (1, 1))
    grad_up = jnp.dot(normed_t[...], grad_pre, preferred_element_type=F32).astype(BF16)
    grad_down = jnp.dot(turned_sc[...], active, preferred_element_type=F32).astype(BF16)
    for slot in range(near):
        gd_send[slot, 0] = grad_down[slot * block : (slot + 1) * block]
        gd_keep[slot, 0] = grad_down[(near + slot) * block : (near + slot + 1) * block]

    @pl.when(step < near)
    def _():
        gu_send[0] = grad_up

    @pl.when(step >= near)
    def _():
        gu_keep[0] = grad_up

    @pl.when(step == plane - 1)
    def _():
        residual = residual_sc[...]
        out_ref[...] = (residual + acc_out[...]).astype(BF16)
        back, gain_grad, shift_grad = norm_back(residual, gain_ref[...], acc_grad[...])
        norm_ref[0:1, :] = gain_grad
        norm_ref[1:2, :] = shift_grad
        grad_res = cot_ref[...].astype(F32) + back
        res_ref[...] = grad_res
        grad_z = grad_res.astype(BF16)
        grad_att = dot(grad_z, w_out_ref[...], (1, 1)).astype(BF16)
        for pair in range(pairs):
            for half in range(halves):
                col = (half * pairs + pair) * PAIR
                for seq in range(seqs):
                    ga_refs[pair][half * seqs + seq] = grad_att[seq * rows : (seq + 1) * rows, col : col + PAIR]
        turn(grad_z)
        grad_proj = jnp.dot(turned_sc[...], att_sc[...], preferred_element_type=F32).astype(BF16)
        for slot in range(near):
            gp_send[slot] = grad_proj[slot * block : (slot + 1) * block]
            gp_keep[slot] = grad_proj[(near + slot) * block : (near + slot + 1) * block]


def feed_forward(me, x, attended, cotangent, w_out, gain, shift, w_up, w_down, halves, plane):
    seqs, rows, width = x.shape
    hidden = w_up.shape[1]
    pairs = len(attended)
    tokens, near, part, block = seqs * rows, plane // 2, hidden // plane, width // plane

    def at(i, me):
        return me[0] ^ (2 * (i % near) + jnp.where(i < near, 1, 0))

    def fixed(shape):
        return pl.BlockSpec(shape, lambda i, me, n=len(shape): (0,) * n)

    piece = (halves * seqs, rows, PAIR)
    outs = [
        ((tokens, width), BF16, fixed((tokens, width))),
        ((tokens, width), F32, fixed((tokens, width))),
        *[(piece, BF16, fixed(piece))] * pairs,
        ((8, width), F32, fixed((8, width))),
        ((near, width, part), BF16, pl.BlockSpec((1, width, part), lambda i, me: (jnp.minimum(i, near - 1), 0, 0))),
        ((near, width, part), BF16, pl.BlockSpec((1, width, part), lambda i, me: (jnp.maximum(i - near, 0), 0, 0))),
        *[
            (
                (near, plane, block, part),
                BF16,
                pl.BlockSpec((near, 1, block, part), lambda i, me: (0, at(i, me), 0, 0)),
            )
        ]
        * 2,
        *[((near, block, width), BF16, fixed((near, block, width)))] * 2,
    ]
    return pl.pallas_call(
        functools.partial(ff_kernel, seqs, halves, pairs, plane),
        grid_spec=pltpu.PrefetchScalarGridSpec(
            num_scalar_prefetch=1,
            grid=(plane,),
            in_specs=[fixed((tokens, width))]
            + [fixed(piece)] * pairs
            + [fixed((tokens, width)), fixed((width, width)), fixed((1, width)), fixed((1, width))]
            + [
                pl.BlockSpec((width, part), lambda i, me: (0, at(i, me))),
                pl.BlockSpec((part, width), lambda i, me: (at(i, me), 0)),
            ],
            out_specs=[o[2] for o in outs],
            scratch_shapes=[
                pltpu.VMEM((tokens, width), BF16),
                pltpu.VMEM((tokens, width), F32),
                pltpu.VMEM((tokens, width), BF16),
                pltpu.VMEM((width, tokens), BF16),
                pltpu.VMEM((width, tokens), BF16),
                pltpu.VMEM((tokens, width), F32),
                pltpu.VMEM((tokens, width), F32),
            ],
        ),
        out_shape=[jax.ShapeDtypeStruct(o[0], o[1]) for o in outs],
        cost_estimate=pl.CostEstimate(
            flops=12 * tokens * width * hidden + 6 * tokens * width * width,
            bytes_accessed=8 * width * hidden,
            transcendentals=tokens * hidden,
        ),
        name="feed_forward",
    )(
        me,
        x.reshape(tokens, width),
        *attended,
        cotangent.reshape(tokens, width),
        w_out,
        gain[None],
        shift[None],
        w_up,
        w_down,
    )


def project_back_kernel(seqs, halves, pairs, first, *refs):
    grad_ref, normed_ref, *refs = refs
    w_refs, refs = refs[: 3 * halves], refs[3 * halves :]
    if first:
        gq_ref, gn_ref = refs
    else:
        _, old_ref, gq_ref, gn_ref = refs
    grad = jnp.concatenate(
        [
            jnp.concatenate([grad_ref[half * seqs + seq] for half in range(halves)], axis=1)
            for seq in range(seqs)
        ],
        axis=0,
    )
    weights = jnp.concatenate([w[...] for w in w_refs], axis=1)
    turned = jnp.dot(grad.T, normed_ref[...], preferred_element_type=F32).astype(BF16)
    for half in range(halves):
        for kind in range(3):
            at = (half * 3 + kind) * PAIR
            gq_ref[kind, half, 0] = turned[at : at + PAIR]
    back = dot(grad, weights, (1, 1))
    gn_ref[...] = back if first else old_ref[...] + back


def project_back(grad, normed, w_qkv, halves, pair, old=None):
    tokens, width = normed.shape
    pairs = width // PAIR // halves
    seqs = grad.shape[0] // halves
    first = old is None
    whole = lambda i: (0, 0)
    columns = pair_columns(width, halves, pair, lambda c, i: (0, c))
    gq_shape = (3, halves, pairs, PAIR, width)
    ahead = [] if first else list(old)
    specs = [] if first else [pl.BlockSpec(memory_space=pl.ANY), pl.BlockSpec((tokens, width), whole)]
    base = 2 + len(columns)
    return pl.pallas_call(
        functools.partial(project_back_kernel, seqs, halves, pairs, first),
        grid=(1,),
        in_specs=[pl.BlockSpec(grad.shape, lambda i: (0, 0, 0)), pl.BlockSpec((tokens, width), whole)]
        + columns
        + specs,
        out_specs=[
            pl.BlockSpec((3, halves, 1, PAIR, width), lambda i: (0, 0, pair, 0, 0)),
            pl.BlockSpec((tokens, width), whole),
        ],
        out_shape=[jax.ShapeDtypeStruct(gq_shape, BF16), jax.ShapeDtypeStruct((tokens, width), F32)],
        input_output_aliases={} if first else {base: 0, base + 1: 1},
        cost_estimate=pl.CostEstimate(
            flops=4 * tokens * width * len(columns) * PAIR, bytes_accessed=10 * width * width, transcendentals=0
        ),
        name="project_back",
    )(grad, normed, *([w_qkv] * len(columns)), *ahead)


def first_norm_kernel(x_ref, gain_ref, grad_ref, res_ref, out_ref, norm_ref):
    back, gain_grad, shift_grad = norm_back(x_ref[...].astype(F32), gain_ref[...], grad_ref[...])
    out_ref[...] = (res_ref[...] + back).astype(BF16)

    @pl.when(pl.program_id(0) == 0)
    def _():
        norm_ref[...] = jnp.zeros_like(norm_ref)

    norm_ref[0:1, :] += gain_grad
    norm_ref[1:2, :] += shift_grad


def first_norm_back(x, gain, grad, grad_res):
    tokens, width = grad.shape
    steps = 4
    row = lambda i: (i, 0)
    one = lambda i: (0, 0)
    return pl.pallas_call(
        first_norm_kernel,
        grid=(steps,),
        in_specs=[
            pl.BlockSpec((tokens // steps, width), row),
            pl.BlockSpec((1, width), one),
            pl.BlockSpec((tokens // steps, width), row),
            pl.BlockSpec((tokens // steps, width), row),
        ],
        out_specs=[pl.BlockSpec((tokens // steps, width), row), pl.BlockSpec((8, width), one)],
        out_shape=[jax.ShapeDtypeStruct((tokens, width), BF16), jax.ShapeDtypeStruct((8, width), F32)],
        cost_estimate=pl.CostEstimate(flops=20 * tokens * width, bytes_accessed=12 * tokens * width, transcendentals=0),
        name="first_norm_back",
    )(x.reshape(tokens, width), gain[None], grad, grad_res)


def exchange(blocks):
    return lax.all_to_all(blocks, ("pb", "ka"), 0, 0, tiled=True)


def swap(values, axes, size, bit):
    return lax.ppermute(values, axes, [(i, i ^ bit) for i in range(size)])


def add_pair_kernel(near, *refs):
    *in_refs, out0, out1, out2, out3 = refs
    outs = (out0, out1, out2, out3)
    step = pl.program_id(0)
    up_a, up_b, down_a, down_b, proj_a, proj_b = in_refs
    width = proj_a.shape[2]
    part = out0.shape[1]

    @pl.when(step < 4)
    def _():
        for k in range(near):
            outs[k][...] = (up_a[k].astype(F32) + up_b[k].astype(F32)).astype(BF16)

    @pl.when((step >= 4) & (step < 8))
    def _():
        for k in range(near):
            outs[k][...] = (down_a[k].astype(F32) + down_b[k].astype(F32)).astype(BF16)

    @pl.when(step == 8)
    def _():
        for k in range(near):
            both = (proj_a[k].astype(F32) + proj_b[k].astype(F32)).astype(BF16)
            outs[k][...] = jnp.concatenate([both[:, :part], both[:, part:]], axis=0)


def add_pair(up, down, proj):
    near, width, part = up[0].shape
    block = proj[0].shape[1]
    tall = width // 4
    down = [d.reshape(near, width, part) for d in down]
    up_spec = pl.BlockSpec((near, tall, part), lambda i: (0, jnp.minimum(i, 3), 0))
    down_spec = pl.BlockSpec((near, tall, part), lambda i: (0, jnp.clip(i - 4, 0, 3), 0))
    proj_spec = pl.BlockSpec((near, block, width), lambda i: (0, 0, 0))
    return pl.pallas_call(
        functools.partial(add_pair_kernel, near),
        grid=(9,),
        in_specs=[up_spec] * 2 + [down_spec] * 2 + [proj_spec] * 2,
        out_specs=[pl.BlockSpec((tall, part), lambda i: (i, 0))] * near,
        out_shape=[jax.ShapeDtypeStruct((9 * tall, part), BF16)] * near,
        cost_estimate=pl.CostEstimate(
            flops=near * 9 * tall * part, bytes_accessed=6 * near * 9 * tall * part, transcendentals=0
        ),
        name="add_pair",
    )(*up, *down, *proj)


def add_all(parts):
    total = parts[0].astype(F32)
    for p in parts[1:]:
        total = total + p.astype(F32)
    return total


def over_batch(stacked):
    size = lax.axis_size("batch")
    mine = lax.axis_index("batch")
    if size > 4:
        return lax.psum_scatter(stacked, "batch", scatter_dimension=0, tiled=True)[0].astype(F32)
    parts = [lax.dynamic_index_in_dim(stacked, mine, 0, False)]
    for bit in range(1, size):
        block = lax.dynamic_index_in_dim(stacked, mine ^ bit, 0, False)
        parts.append(swap(block, "batch", size, bit))
    return add_all(parts)


def over_plane(tiles, plane):
    parts = [tiles[0]]
    for k in range(1, len(tiles)):
        parts.append(swap(tiles[k], ("pb", "ka"), plane, 2 * k))
    return add_all(parts).astype(BF16)


def shards(
    inputs,
    block_place,
    ln1_gain,
    ln1_shift,
    w_qkv,
    w_out,
    ln2_gain,
    ln2_shift,
    w_up,
    w_down,
    cotangent,
):
    seqs, rows, width = inputs.shape
    hidden = w_up.shape[1]
    halves = lax.axis_size("pb")
    plane = halves * lax.axis_size("ka")
    planes = ("pb", "ka")
    batch = lax.axis_size("batch")
    near = plane // 2
    me = lax.axis_index(planes)
    pairs = width // PAIR // halves
    place = lax.dynamic_index_in_dim(block_place, lax.axis_index("ka"), 0, False)
    packed, normed1 = [], None
    for pair in range(pairs):
        sent, normed1 = project(inputs, ln1_gain, ln1_shift, w_qkv, halves, pair, normed1)
        packed.append(exchange(sent))
    attended, saved = [], []
    for x in packed:
        out, sums, stats = attend(place, x)
        saved.append((sums, stats))
        attended.append(exchange(out))
    me_array = me.astype(jnp.int32).reshape(1)
    outputs, grad_res, *rest = feed_forward(
        me_array, inputs, attended, cotangent, w_out, ln2_gain, ln2_shift, w_up, w_down, halves, plane
    )
    grad_att, (norm2, *grads) = rest[:pairs], rest[pairs:]
    state = None
    for pair in range(pairs):
        sums, stats = saved[pair]
        back = attend_back(place, packed[pair], exchange(grad_att[pair]), sums, stats)
        state = project_back(exchange(back), normed1, w_qkv, halves, pair, state)
    up_send, up_keep, down_send, down_keep, proj_send, proj_keep = grads
    tiles = add_pair(
        (up_keep, swap(up_send, planes, plane, 1)),
        (down_keep, swap(down_send, planes, plane, 1)),
        (proj_keep, swap(proj_send, planes, plane, 1)),
    )
    tile = over_plane(tiles, plane)
    part, block = hidden // plane, width // plane
    slab = width // batch
    up_tile = tile[:width].reshape(batch, slab, part)
    down_tile = tile[width : 2 * width].reshape(plane, block, part)
    proj_tile = tile[2 * width :].reshape(2, block, part).transpose(1, 0, 2).reshape(block, batch, slab)
    proj_tile = proj_tile.transpose(1, 0, 2)
    if batch <= plane:
        down_tile = down_tile.reshape(batch, plane // batch * block, part)
    else:
        cut = batch // plane
        down_tile = down_tile.reshape(plane, block, cut, part // cut).transpose(0, 2, 1, 3)
        down_tile = down_tile.reshape(batch, block, part // cut)
    if batch <= 4:
        joined = jnp.concatenate([up_tile, down_tile, proj_tile.reshape(batch, block * slab // part, part)], axis=1)
        summed = over_batch(joined)
        tall = down_tile.shape[1]
        grad_up, grad_down = summed[:slab], summed[slab : slab + tall]
        grad_proj = summed[slab + tall :].reshape(block, slab)
    else:
        grad_up, grad_down, grad_proj = over_batch(up_tile), over_batch(down_tile), over_batch(proj_tile)
    grad_down = grad_down.reshape(-1, block, down_tile.shape[2]).transpose(0, 2, 1).reshape(-1, block)
    grad_proj = grad_proj.T

    grad_qkv, grad_normed1 = state
    grad_inputs, norm1 = first_norm_back(inputs, ln1_gain, grad_normed1, grad_res)
    core = me & 1
    owned = 3 * width // plane
    pieces = grad_qkv.reshape(near, 2, owned, width)
    other = swap(lax.dynamic_index_in_dim(pieces, 1 - core, 1, False), planes, plane, 1)
    pieces = lax.dynamic_index_in_dim(pieces, core, 1, False)
    pieces = (pieces.astype(F32) + other.astype(F32)).astype(BF16)
    tiles = [lax.dynamic_index_in_dim(pieces, (me >> 1) ^ k, 0, False) for k in range(near)]
    tile = over_plane(tiles, plane).reshape(owned, batch, slab).transpose(1, 0, 2)
    grad_qkv = over_batch(tile).T
    norms = lax.psum(jnp.concatenate([norm1[:2], norm2[:2]]), ("batch", *planes))
    norms = lax.dynamic_slice_in_dim(norms, me * block, block, 1)
    return (
        outputs.reshape(inputs.shape),
        grad_inputs.reshape(inputs.shape),
        grad_qkv,
        grad_proj,
        grad_up,
        grad_down,
        norms,
    )


def solution(mesh):
    placed = (
        P("batch", ("pb", "ka"), None),
        P("batch", None),
        P(),
        P(),
        P(),
        P(),
        P(),
        P(),
        P(),
        P(),
        P("batch", ("pb", "ka"), None),
    )
    return jax.shard_map(
        shards,
        mesh=mesh,
        in_specs=placed,
        out_specs=(
            P("batch", ("pb", "ka"), None),
            P("batch", ("pb", "ka"), None),
            P("batch", ("pb", "ka")),
            P("batch", ("pb", "ka")),
            P("batch", ("pb", "ka")),
            P("batch", ("pb", "ka")),
            P(None, ("pb", "ka")),
        ),
        check_vma=False,
    )
```

```python
import functools

import jax
import jax.numpy as jnp
from jax import lax
from jax.experimental import pallas as pl
from jax.experimental.pallas import tpu as pltpu
from jax.sharding import PartitionSpec as P

HEADS = 12
HEAD = 64
PAIR = 2 * HEAD
QTILE = 256
SCALE = HEAD ** (-0.5)
HUGE = 3e38
HIDDEN = -1e30

norm_eps = 1e-05
BF16 = jnp.bfloat16
F32 = jnp.float32


def norm_rows(values, gain_vec, shift_vec):
    average = jnp.mean(values, axis=-1, keepdims=True)
    centred = values - average
    spread = jnp.mean(centred * centred, axis=-1, keepdims=True)
    return centred * lax.rsqrt(spread + norm_eps) * gain_vec + shift_vec


def gelu_tanh(values):
    return jax.nn.gelu(values, approximate=True)


def dot(a, b, contract):
    return lax.dot_general(a, b, ((contract[:1], contract[1:]), ((), ())), preferred_element_type=F32)


def project_kernel(seqs, halves, first, *refs):
    if first:
        x_ref, gain_ref, shift_ref, *w_refs, out_ref, normed_ref = refs
        normed_ref[...] = norm_rows(x_ref[...].astype(F32), gain_ref[...], shift_ref[...]).astype(BF16)
    else:
        normed_ref, *w_refs, out_ref = refs
    rows = normed_ref.shape[0] // seqs
    weights = jnp.concatenate([w[...] for w in w_refs], axis=1)
    part = jnp.dot(normed_ref[...], weights, preferred_element_type=F32).astype(BF16)
    for half in range(halves):
        for seq in range(seqs):
            out_ref[half * seqs + seq] = part[
                seq * rows : (seq + 1) * rows, half * 3 * PAIR : (half + 1) * 3 * PAIR
            ]


def pair_columns(width, halves, pair, order):
    pairs = width // PAIR // halves
    return [
        pl.BlockSpec((width, PAIR), functools.partial(order, kind * (width // PAIR) + half * pairs + pair))
        for half in range(halves)
        for kind in range(3)
    ]


def project(x, gain, shift, w_qkv, halves, pair, normed=None):
    seqs, rows, width = x.shape
    tokens = seqs * rows
    whole = lambda i: (0, 0)
    first = normed is None
    ahead = (
        [x.reshape(tokens, width), gain, shift] if first else [normed]
    )
    specs = [pl.BlockSpec(a.shape, lambda i, n=a.ndim: (0,) * n) for a in ahead]
    columns = pair_columns(width, halves, pair, lambda c, i: (0, c))
    out_shape = [jax.ShapeDtypeStruct((halves * seqs, rows, 3 * PAIR), BF16)]
    out_specs = [pl.BlockSpec(out_shape[0].shape, lambda i: (0, 0, 0))]
    if first:
        out_shape.append(jax.ShapeDtypeStruct((tokens, width), BF16))
        out_specs.append(pl.BlockSpec((tokens, width), whole))
    outs = pl.pallas_call(
        functools.partial(project_kernel, seqs, halves, first),
        grid=(1,),
        in_specs=specs + columns,
        out_specs=out_specs,
        out_shape=out_shape,
        cost_estimate=pl.CostEstimate(
            flops=2 * tokens * width * len(columns) * PAIR, bytes_accessed=5 * width * width, transcendentals=0
        ),
        name="project",
    )(*ahead, *([w_qkv] * len(columns)))
    return outs if first else (outs[0], normed)


def head_lanes(values, head):
    lane = lax.broadcasted_iota(jnp.int32, values.shape, 1)
    mine = lane < HEAD if head == 0 else lane >= HEAD
    return jnp.where(mine, values, jnp.zeros_like(values))


def gather_rows(place_ref, source_ref, columns, target_ref):
    blocks, rows = source_ref.shape[0], source_ref.shape[1]
    for block in range(blocks):
        at = pl.multiple_of(place_ref[block] * rows, rows)
        target_ref[pl.ds(at, rows), :] = source_ref[block, :, columns]


def scatter_rows(place_ref, source_ref, target_ref, columns):
    blocks, rows = target_ref.shape[0], target_ref.shape[1]
    for block in range(blocks):
        at = pl.multiple_of(place_ref[block] * rows, rows)
        target_ref[block, :, columns] = source_ref[pl.ds(at, rows), :].astype(target_ref.dtype)


def hide_later(magnitude):
    keys = magnitude.shape[0]
    key = lax.broadcasted_iota(jnp.int32, (QTILE, QTILE), 0)
    query = lax.broadcasted_iota(jnp.int32, (QTILE, QTILE), 1)
    last = jnp.where(key <= query, magnitude[keys - QTILE :], HIDDEN)
    return last if keys == QTILE else jnp.concatenate([magnitude[: keys - QTILE], last], axis=0)


def sign_of(scores):
    return jnp.clip(scores * HUGE, -1.0, 1.0)


def attend_kernel(place_ref, x_ref, out_ref, sums_ref, stats_ref, q_sc, k_sc, v_sc, o_sc):
    gather_rows(place_ref, x_ref, slice(0, PAIR), q_sc)
    gather_rows(place_ref, x_ref, slice(PAIR, 2 * PAIR), k_sc)
    gather_rows(place_ref, x_ref, slice(2 * PAIR, 3 * PAIR), v_sc)
    total_rows = q_sc.shape[0]
    v_t = v_sc[...].T
    for tile in range(total_rows // QTILE):
        span = slice(tile * QTILE, (tile + 1) * QTILE)
        keys = (tile + 1) * QTILE
        queries = q_sc[span, :] * SCALE
        for head in range(2):
            scores = dot(k_sc[:keys, :], head_lanes(queries, head).astype(BF16), (1, 1))
            magnitude = hide_later(jnp.abs(scores))
            peak = jnp.max(magnitude, axis=0, keepdims=True)
            exponents = jnp.exp(magnitude - peak)
            total = jnp.sum(exponents, axis=0, keepdims=True)
            weights = (exponents * sign_of(scores)).astype(BF16)
            summed = dot(v_t[head * HEAD : (head + 1) * HEAD, :keys], weights, (1, 0))
            sums_ref[head * HEAD : (head + 1) * HEAD, span] = summed / total
            stats_ref[head : head + 1, span] = peak + jnp.log(total)
        o_sc[span, :] = sums_ref[:, span].T
    scatter_rows(place_ref, o_sc, out_ref, slice(None))


def attend(place, x):
    blocks, rows, _ = x.shape
    length = blocks * rows
    area = length * length
    return pl.pallas_call(
        attend_kernel,
        grid_spec=pltpu.PrefetchScalarGridSpec(
            num_scalar_prefetch=1,
            grid=(1,),
            in_specs=[pl.BlockSpec(x.shape, lambda i, p: (0, 0, 0))],
            out_specs=[
                pl.BlockSpec((blocks, rows, PAIR), lambda i, p: (0, 0, 0)),
                pl.BlockSpec((PAIR, length), lambda i, p: (0, 0)),
                pl.BlockSpec((8, length), lambda i, p: (0, 0)),
            ],
            scratch_shapes=[pltpu.VMEM((length, PAIR), BF16)] * 3 + [pltpu.VMEM((length, PAIR), F32)],
        ),
        out_shape=[
            jax.ShapeDtypeStruct((blocks, rows, PAIR), BF16),
            jax.ShapeDtypeStruct((PAIR, length), F32),
            jax.ShapeDtypeStruct((8, length), F32),
        ],
        cost_estimate=pl.CostEstimate(
            flops=16 * area * HEAD, bytes_accessed=4 * length * PAIR * 4, transcendentals=area
        ),
        name="attend",
    )(place, x)


def attend_back_kernel(
    place_ref, x_ref, g_ref, sums_ref, stats_ref, out_ref, q_sc, k_sc, v_sc, g_sc, dq_sc, dk_sc, dv_sc
):
    gather_rows(place_ref, x_ref, slice(0, PAIR), q_sc)
    gather_rows(place_ref, x_ref, slice(PAIR, 2 * PAIR), k_sc)
    gather_rows(place_ref, x_ref, slice(2 * PAIR, 3 * PAIR), v_sc)
    gather_rows(place_ref, g_ref, slice(0, PAIR), g_sc)
    total_rows = q_sc.shape[0]
    k_t = k_sc[...].T
    g_t = g_sc[...].astype(F32).T
    products = g_t * sums_ref[...]
    deltas = [
        jnp.sum(products[head * HEAD : (head + 1) * HEAD], axis=0, keepdims=True) for head in range(2)
    ]
    dk_sc[...] = jnp.zeros_like(dk_sc)
    dv_sc[...] = jnp.zeros_like(dv_sc)
    for tile in range(total_rows // QTILE):
        span = slice(tile * QTILE, (tile + 1) * QTILE)
        keys = (tile + 1) * QTILE
        queries = q_sc[span, :] * SCALE
        parts = []
        for head in range(2):
            q_head = head_lanes(queries, head).astype(BF16)
            g_head = head_lanes(g_sc[span, :], head)
            scores = dot(k_sc[:keys, :], q_head, (1, 1))
            magnitude = hide_later(jnp.abs(scores))
            sign = sign_of(scores)
            signed = jnp.exp(magnitude - stats_ref[head : head + 1, span]) * sign
            grad_weights = dot(v_sc[:keys, :], g_head, (1, 1))
            grad_scores = (signed * (sign * grad_weights - deltas[head][:, span])).astype(BF16)
            dv_sc[:keys, :] += dot(signed.astype(BF16), g_head, (1, 0))
            dk_sc[:keys, :] += dot(grad_scores, q_head, (1, 0))
            parts.append(dot(k_t[head * HEAD : (head + 1) * HEAD, :keys], grad_scores, (1, 0)))
        dq_sc[span, :] = jnp.concatenate(parts, axis=0).T * SCALE
    scatter_rows(place_ref, dq_sc, out_ref, slice(0, PAIR))
    scatter_rows(place_ref, dk_sc, out_ref, slice(PAIR, 2 * PAIR))
    scatter_rows(place_ref, dv_sc, out_ref, slice(2 * PAIR, 3 * PAIR))


def attend_back(place, x, grad, pair, sums, stats):
    blocks, rows, _ = x.shape
    length = blocks * rows
    area = length * length
    block3 = lambda i, p: (0, 0, 0)
    block2 = lambda i, p: (0, 0)
    return pl.pallas_call(
        attend_back_kernel,
        grid_spec=pltpu.PrefetchScalarGridSpec(
            num_scalar_prefetch=1,
            grid=(1,),
            in_specs=[
                pl.BlockSpec(x.shape, block3),
                pl.BlockSpec((blocks, rows, PAIR), lambda i, p: (0, 0, pair)),
                pl.BlockSpec(sums.shape, block2),
                pl.BlockSpec(stats.shape, block2),
            ],
            out_specs=pl.BlockSpec(x.shape, block3),
            scratch_shapes=[pltpu.VMEM((length, PAIR), BF16)] * 4 + [pltpu.VMEM((length, PAIR), F32)] * 3,
        ),
        out_shape=jax.ShapeDtypeStruct(x.shape, BF16),
        cost_estimate=pl.CostEstimate(
            flops=40 * area * HEAD, bytes_accessed=8 * length * PAIR * 4, transcendentals=area
        ),
        name="attend_back",
    )(place, x, grad, sums, stats)


def gelu_pair(u):
    c = 0.7978845608028654
    square = u * u
    t = jnp.tanh(c * u * (1.0 + 0.044715 * square))
    half = 0.5 * (1.0 + t)
    slope = half + 0.5 * c * u * (1.0 - t * t) * (1.0 + 3.0 * 0.044715 * square)
    return u * half, slope


def norm_back(values, gain_vec, grad):
    average = jnp.mean(values, axis=-1, keepdims=True)
    centred = values - average
    spread = jnp.mean(centred * centred, axis=-1, keepdims=True)
    scale = lax.rsqrt(spread + norm_eps)
    unit = centred * scale
    scaled = grad * gain_vec
    back = scale * (
        scaled
        - jnp.mean(scaled, axis=-1, keepdims=True)
        - unit * jnp.mean(scaled * unit, axis=-1, keepdims=True)
    )
    return back, jnp.sum(grad * unit, axis=0, keepdims=True), jnp.sum(grad, axis=0, keepdims=True)


def ff_kernel(seqs, halves, pairs, plane, *refs):
    me_ref, x_ref, *refs = refs
    att_refs, refs = refs[:pairs], refs[pairs:]
    cot_ref, w_out_ref, gain_ref, shift_ref, up_ref, down_ref, *refs = refs
    out_ref, res_ref, *refs = refs
    ga_ref, norm_ref, gu_send, gu_keep, gd_send, gd_keep, gp_send, gp_keep, *refs = refs
    att_sc, residual_sc, normed_sc, normed_t, turned_sc, acc_out, acc_grad = refs
    step = pl.program_id(0)
    tokens, width = x_ref.shape
    rows = tokens // seqs
    block = width // plane
    near = plane // 2

    def turn(values):
        turned = values.T
        for j in range(plane):
            t = me_ref[0] ^ j
            slot = (1 - (t & 1)) * near + (t >> 1)
            at = pl.multiple_of(slot * block, block)
            turned_sc[pl.ds(at, block), :] = turned[j * block : (j + 1) * block]

    @pl.when(step == 0)
    def _():
        for pair in range(pairs):
            for half in range(halves):
                col = (half * pairs + pair) * PAIR
                for seq in range(seqs):
                    att_sc[seq * rows : (seq + 1) * rows, col : col + PAIR] = att_refs[pair][half * seqs + seq]
        residual = x_ref[...].astype(F32) + jnp.dot(att_sc[...], w_out_ref[...], preferred_element_type=F32)
        residual_sc[...] = residual
        normed = norm_rows(residual, gain_ref[...], shift_ref[...]).astype(BF16)
        normed_sc[...] = normed
        normed_t[...] = normed.T
        turn(cot_ref[...])
        acc_out[...] = jnp.zeros_like(acc_out)
        acc_grad[...] = jnp.zeros_like(acc_grad)

    pre = jnp.dot(normed_sc[...], up_ref[...], preferred_element_type=F32)
    active, slope = gelu_pair(pre)
    active = active.astype(BF16)
    grad_pre = (dot(cot_ref[...], down_ref[...], (1, 1)) * slope).astype(BF16)
    acc_out[...] += jnp.dot(active, down_ref[...], preferred_element_type=F32)
    acc_grad[...] += dot(grad_pre, up_ref[...], (1, 1))
    grad_up = jnp.dot(normed_t[...], grad_pre, preferred_element_type=F32).astype(BF16)
    grad_down = jnp.dot(turned_sc[...], active, preferred_element_type=F32).astype(BF16)
    for slot in range(near):
        gd_send[slot, 0] = grad_down[slot * block : (slot + 1) * block]
        gd_keep[slot, 0] = grad_down[(near + slot) * block : (near + slot + 1) * block]

    @pl.when(step < near)
    def _():
        gu_send[0] = grad_up

    @pl.when(step >= near)
    def _():
        gu_keep[0] = grad_up

    @pl.when(step == plane - 1)
    def _():
        residual = residual_sc[...]
        out_ref[...] = (residual + acc_out[...]).astype(BF16)
        back, gain_grad, shift_grad = norm_back(residual, gain_ref[...], acc_grad[...])
        norm_ref[0:1, :] = gain_grad
        norm_ref[1:2, :] = shift_grad
        grad_res = cot_ref[...].astype(F32) + back
        res_ref[...] = grad_res
        grad_z = grad_res.astype(BF16)
        grad_att = dot(grad_z, w_out_ref[...], (1, 1)).astype(BF16)
        for pair in range(pairs):
            for half in range(halves):
                col = (half * pairs + pair) * PAIR
                for seq in range(seqs):
                    ga_ref[half * seqs + seq, :, pair * PAIR : (pair + 1) * PAIR] = grad_att[
                        seq * rows : (seq + 1) * rows, col : col + PAIR
                    ]
        turn(grad_z)
        grad_proj = jnp.dot(turned_sc[...], att_sc[...], preferred_element_type=F32).astype(BF16)
        for slot in range(near):
            gp_send[slot] = grad_proj[slot * block : (slot + 1) * block]
            gp_keep[slot] = grad_proj[(near + slot) * block : (near + slot + 1) * block]


def feed_forward(me, x, attended, cotangent, w_out, gain, shift, w_up, w_down, halves, plane):
    seqs, rows, width = x.shape
    hidden = w_up.shape[1]
    pairs = len(attended)
    tokens, near, part, block = seqs * rows, plane // 2, hidden // plane, width // plane

    def at(i, me):
        return me[0] ^ (2 * (i % near) + jnp.where(i < near, 1, 0))

    def fixed(shape):
        return pl.BlockSpec(shape, lambda i, me, n=len(shape): (0,) * n)

    piece = (halves * seqs, rows, PAIR)
    joined = (halves * seqs, rows, pairs * PAIR)
    outs = [
        ((tokens, width), BF16, fixed((tokens, width))),
        ((tokens, width), F32, fixed((tokens, width))),
        (joined, BF16, fixed(joined)),
        ((8, width), F32, fixed((8, width))),
        ((near, width, part), BF16, pl.BlockSpec((1, width, part), lambda i, me: (jnp.minimum(i, near - 1), 0, 0))),
        ((near, width, part), BF16, pl.BlockSpec((1, width, part), lambda i, me: (jnp.maximum(i - near, 0), 0, 0))),
        *[
            (
                (near, plane, block, part),
                BF16,
                pl.BlockSpec((near, 1, block, part), lambda i, me: (0, at(i, me), 0, 0)),
            )
        ]
        * 2,
        *[((near, block, width), BF16, fixed((near, block, width)))] * 2,
    ]
    return pl.pallas_call(
        functools.partial(ff_kernel, seqs, halves, pairs, plane),
        grid_spec=pltpu.PrefetchScalarGridSpec(
            num_scalar_prefetch=1,
            grid=(plane,),
            in_specs=[fixed((tokens, width))]
            + [fixed(piece)] * pairs
            + [fixed((tokens, width)), fixed((width, width)), fixed((width,)), fixed((width,))]
            + [
                pl.BlockSpec((width, part), lambda i, me: (0, at(i, me))),
                pl.BlockSpec((part, width), lambda i, me: (at(i, me), 0)),
            ],
            out_specs=[o[2] for o in outs],
            scratch_shapes=[
                pltpu.VMEM((tokens, width), BF16),
                pltpu.VMEM((tokens, width), F32),
                pltpu.VMEM((tokens, width), BF16),
                pltpu.VMEM((width, tokens), BF16),
                pltpu.VMEM((width, tokens), BF16),
                pltpu.VMEM((tokens, width), F32),
                pltpu.VMEM((tokens, width), F32),
            ],
        ),
        out_shape=[jax.ShapeDtypeStruct(o[0], o[1]) for o in outs],
        cost_estimate=pl.CostEstimate(
            flops=12 * tokens * width * hidden + 6 * tokens * width * width,
            bytes_accessed=8 * width * hidden,
            transcendentals=tokens * hidden,
        ),
        name="feed_forward",
    )(
        me,
        x.reshape(tokens, width),
        *attended,
        cotangent.reshape(tokens, width),
        w_out,
        gain,
        shift,
        w_up,
        w_down,
    )


def project_back_kernel(seqs, halves, pairs, first, *refs):
    grad_ref, normed_ref, *refs = refs
    w_refs, refs = refs[: 3 * halves], refs[3 * halves :]
    if first:
        gq_ref, gn_ref = refs
    else:
        _, old_ref, gq_ref, gn_ref = refs
    grad = jnp.concatenate(
        [
            jnp.concatenate([grad_ref[half * seqs + seq] for half in range(halves)], axis=1)
            for seq in range(seqs)
        ],
        axis=0,
    )
    weights = jnp.concatenate([w[...] for w in w_refs], axis=1)
    turned = jnp.dot(grad.T, normed_ref[...], preferred_element_type=F32).astype(BF16)
    for half in range(halves):
        for kind in range(3):
            at = (half * 3 + kind) * PAIR
            gq_ref[kind, half, 0] = turned[at : at + PAIR]
    back = dot(grad, weights, (1, 1))
    gn_ref[...] = back if first else old_ref[...] + back


def project_back(grad, normed, w_qkv, halves, pair, old=None):
    tokens, width = normed.shape
    pairs = width // PAIR // halves
    seqs = grad.shape[0] // halves
    first = old is None
    whole = lambda i: (0, 0)
    columns = pair_columns(width, halves, pair, lambda c, i: (0, c))
    gq_shape = (3, halves, pairs, PAIR, width)
    ahead = [] if first else list(old)
    specs = [] if first else [pl.BlockSpec(memory_space=pl.ANY), pl.BlockSpec((tokens, width), whole)]
    base = 2 + len(columns)
    return pl.pallas_call(
        functools.partial(project_back_kernel, seqs, halves, pairs, first),
        grid=(1,),
        in_specs=[pl.BlockSpec(grad.shape, lambda i: (0, 0, 0)), pl.BlockSpec((tokens, width), whole)]
        + columns
        + specs,
        out_specs=[
            pl.BlockSpec((3, halves, 1, PAIR, width), lambda i: (0, 0, pair, 0, 0)),
            pl.BlockSpec((tokens, width), whole),
        ],
        out_shape=[jax.ShapeDtypeStruct(gq_shape, BF16), jax.ShapeDtypeStruct((tokens, width), F32)],
        input_output_aliases={} if first else {base: 0, base + 1: 1},
        cost_estimate=pl.CostEstimate(
            flops=4 * tokens * width * len(columns) * PAIR, bytes_accessed=10 * width * width, transcendentals=0
        ),
        name="project_back",
    )(grad, normed, *([w_qkv] * len(columns)), *ahead)


def first_norm_kernel(x_ref, gain_ref, grad_ref, res_ref, out_ref, norm_ref):
    back, gain_grad, shift_grad = norm_back(x_ref[...].astype(F32), gain_ref[...], grad_ref[...])
    out_ref[...] = (res_ref[...] + back).astype(BF16)

    @pl.when(pl.program_id(0) == 0)
    def _():
        norm_ref[...] = jnp.zeros_like(norm_ref)

    norm_ref[0:1, :] += gain_grad
    norm_ref[1:2, :] += shift_grad


def first_norm_back(x, gain, grad, grad_res):
    tokens, width = grad.shape
    steps = 4
    row = lambda i: (i, 0)
    one = lambda i: (0, 0)
    return pl.pallas_call(
        first_norm_kernel,
        grid=(steps,),
        in_specs=[
            pl.BlockSpec((tokens // steps, width), row),
            pl.BlockSpec((width,), lambda i: (0,)),
            pl.BlockSpec((tokens // steps, width), row),
            pl.BlockSpec((tokens // steps, width), row),
        ],
        out_specs=[pl.BlockSpec((tokens // steps, width), row), pl.BlockSpec((8, width), one)],
        out_shape=[jax.ShapeDtypeStruct((tokens, width), BF16), jax.ShapeDtypeStruct((8, width), F32)],
        cost_estimate=pl.CostEstimate(flops=20 * tokens * width, bytes_accessed=12 * tokens * width, transcendentals=0),
        name="first_norm_back",
    )(x.reshape(tokens, width), gain, grad, grad_res)


def exchange(blocks):
    return lax.all_to_all(blocks, ("pb", "ka"), 0, 0, tiled=True)


def swap(values, axes, size, bit):
    return lax.ppermute(values, axes, [(i, i ^ bit) for i in range(size)])


def add_pair_kernel(near, batch, *refs):
    _, up_a, up_b, down_a, down_b, proj_a, proj_b, *outs = refs
    outs, down_outs = outs[:near], outs[near:]
    step = pl.program_id(0)
    part = outs[0].shape[1]

    def both(a, b):
        return (a.astype(F32) + b.astype(F32)).astype(BF16)

    @pl.when(step < batch)
    def _():
        for k in range(near):
            outs[k][...] = both(up_a[k], up_b[k])

    for far in range(batch):

        @pl.when(step == batch + far)
        def _():
            for k in range(near):
                total = both(down_a[k], down_b[k])
                slab = total.shape[0] * total.shape[1]
                down_outs[far][k * slab : (k + 1) * slab] = total.reshape(slab, part)

    @pl.when(step == 2 * batch)
    def _():
        for k in range(near):
            total = both(proj_a[k], proj_b[k])
            outs[k][...] = jnp.concatenate([total[:, :part], total[:, part:]], axis=0)


def add_pair(mine, up, down, proj, batch):
    near, width, part = up[0].shape
    plane, block = down[0].shape[1:3]
    tall, few = width // batch, plane // batch
    up_spec = pl.BlockSpec((near, tall, part), lambda i, m: (0, jnp.minimum(i, batch - 1), 0))
    down_spec = pl.BlockSpec(
        (near, few, block, part), lambda i, m: (0, m[0] ^ jnp.clip(i - batch, 0, batch - 1), 0, 0)
    )
    proj_spec = pl.BlockSpec((near, block, width), lambda i, m: (0, 0, 0))
    last = lambda i, m: (jnp.where(i < batch, i, jnp.where(i < 2 * batch, batch - 1, batch)), 0)
    down_shape = (near * few * block, part)
    return pl.pallas_call(
        functools.partial(add_pair_kernel, near, batch),
        grid_spec=pltpu.PrefetchScalarGridSpec(
            num_scalar_prefetch=1,
            grid=(2 * batch + 1,),
            in_specs=[up_spec] * 2 + [down_spec] * 2 + [proj_spec] * 2,
            out_specs=[pl.BlockSpec((tall, part), last)] * near
            + [pl.BlockSpec(down_shape, lambda i, m: (0, 0))] * batch,
        ),
        out_shape=[jax.ShapeDtypeStruct((width + tall, part), BF16)] * near
        + [jax.ShapeDtypeStruct(down_shape, BF16)] * batch,
        cost_estimate=pl.CostEstimate(
            flops=near * 9 * tall * part, bytes_accessed=6 * near * 9 * tall * part, transcendentals=0
        ),
        name="add_pair",
    )(mine, *up, *down, *proj)


def tail_kernel(near, me_ref, own_ref, other_ref, norm_ref, norm_other_ref, *refs):
    outs, norm_sc = refs[:near], refs[near]
    step = pl.program_id(0)
    owned = own_ref.shape[1]
    block = norm_ref.shape[1] // (2 * near)

    @pl.when(step == 0)
    def _():
        norms = norm_ref[...] + norm_other_ref[...]
        norm_sc[...] = jnp.zeros_like(norm_sc)
        for j in range(2 * near):
            norm_sc[j, 0:8, 0:block] = norms[:, j * block : (j + 1) * block]

    for k in range(near):

        @pl.when(step == k)
        def _():
            outs[k][:owned] = (own_ref[0].astype(F32) + other_ref[0].astype(F32)).astype(BF16)
            outs[k][owned:] = jnp.zeros_like(outs[k][owned:])
            outs[k][owned:, : norm_sc.shape[2]] = norm_sc[me_ref[0] ^ (2 * k)].astype(BF16)


def tail(me, grad, other, norm, norm_other):
    plane, owned, width = grad.shape
    near = plane // 2
    spec = pl.BlockSpec((1, owned, width), lambda i, m: (m[0] ^ (2 * i), 0, 0))
    fixed = pl.BlockSpec(norm.shape, lambda i, m: (0, 0))
    shape = (owned + 16, width)
    return pl.pallas_call(
        functools.partial(tail_kernel, near),
        grid_spec=pltpu.PrefetchScalarGridSpec(
            num_scalar_prefetch=1,
            grid=(near,),
            in_specs=[spec, spec, fixed, fixed],
            out_specs=[pl.BlockSpec(shape, lambda i, m: (0, 0))] * near,
            scratch_shapes=[pltpu.VMEM((plane, 16, PAIR), F32)],
        ),
        out_shape=[jax.ShapeDtypeStruct(shape, BF16)] * near,
        cost_estimate=pl.CostEstimate(
            flops=plane * owned * width, bytes_accessed=4 * plane * owned * width, transcendentals=0
        ),
        name="tail",
    )(me, grad, other, norm, norm_other)


def add_all(parts):
    total = parts[0].astype(F32)
    for p in parts[1:]:
        total = total + p.astype(F32)
    return total


def over_batch(stacked):
    size = lax.axis_size("batch")
    mine = lax.axis_index("batch")
    if size > 4:
        return lax.psum_scatter(stacked, "batch", scatter_dimension=0, tiled=True)[0].astype(F32)
    parts = [lax.dynamic_index_in_dim(stacked, mine, 0, False)]
    for bit in range(1, size):
        block = lax.dynamic_index_in_dim(stacked, mine ^ bit, 0, False)
        parts.append(swap(block, "batch", size, bit))
    return add_all(parts)


def over_plane(tiles, plane):
    parts = [tiles[0]]
    for k in range(1, len(tiles)):
        parts.append(swap(tiles[k], ("pb", "ka"), plane, 2 * k))
    return add_all(parts)


def shards(
    inputs,
    block_place,
    ln1_gain,
    ln1_shift,
    w_qkv,
    w_out,
    ln2_gain,
    ln2_shift,
    w_up,
    w_down,
    cotangent,
):
    seqs, rows, width = inputs.shape
    hidden = w_up.shape[1]
    halves = lax.axis_size("pb")
    plane = halves * lax.axis_size("ka")
    planes = ("pb", "ka")
    batch = lax.axis_size("batch")
    few = batch <= 4
    near = plane // 2
    me = lax.axis_index(planes)
    me_array = me.astype(jnp.int32).reshape(1)
    pairs = width // PAIR // halves
    part, block, slab = hidden // plane, width // plane, width // batch
    place = lax.dynamic_index_in_dim(block_place, lax.axis_index("ka"), 0, False)
    packed, normed1 = [], None
    for pair in range(pairs):
        sent, normed1 = project(inputs, ln1_gain, ln1_shift, w_qkv, halves, pair, normed1)
        packed.append(exchange(sent))
    attended, saved = [], []
    for x in packed:
        out, sums, stats = attend(place, x)
        saved.append((sums, stats))
        attended.append(exchange(out))
    outputs, grad_res, grad_att, norm2, *grads = feed_forward(
        me_array, inputs, attended, cotangent, w_out, ln2_gain, ln2_shift, w_up, w_down, halves, plane
    )
    grad_att = exchange(grad_att)
    up, down, proj = [(grads[2 * i + 1], swap(grads[2 * i], planes, plane, 1)) for i in range(3)]
    if few:
        mine = lax.axis_index("batch").astype(jnp.int32).reshape(1)
        sums_up = add_pair(mine, up, down, proj, batch)
        grad_att, sums_up = lax.optimization_barrier((grad_att, sums_up))
        tiles, down = sums_up[:near], sums_up[near:]
    else:
        tiles = [
            jnp.concatenate(
                [add_all([t[k] for t in up])]
                + [add_all([t[k] for t in down]).reshape(width, part)]
                + [add_all([t[k] for t in proj]).reshape(block, 2, part).transpose(1, 0, 2).reshape(2 * block, part)]
            ).astype(BF16)
            for k in range(near)
        ]
    tile = over_plane(tiles, plane).astype(BF16)
    if few:
        down_parts = [down[0]] + [swap(down[bit], "batch", batch, bit) for bit in range(1, batch)]
        down_parts = [d.reshape(near, -1, part) for d in down_parts]
        down_tiles = [add_all([d[k] for d in down_parts]).astype(BF16) for k in range(near)]

    state, later = None, None
    for pair in range(pairs):
        sums, stats = saved[pair]
        back = attend_back(place, packed[pair], grad_att, pair, sums, stats)
        state = project_back(exchange(back), normed1, w_qkv, halves, pair, state)

    if few:
        grad_down = over_plane(down_tiles, plane)
    else:
        cut = batch // plane
        down_tile = tile[width : 2 * width].reshape(plane, block, cut, part // cut).transpose(0, 2, 1, 3)
        grad_down = over_batch(down_tile.reshape(batch, block, part // cut))
    proj_tile = tile[-2 * block :].reshape(2, block, part).transpose(1, 0, 2).reshape(block, batch, slab)
    proj_tile = proj_tile.transpose(1, 0, 2)
    up_tile = tile[:width].reshape(batch, slab, part)
    if few:
        joined = jnp.concatenate([up_tile, proj_tile.reshape(batch, block * slab // part, part)], axis=1)
        summed = over_batch(joined)
        grad_up, grad_proj = summed[:slab], summed[slab:].reshape(block, slab)
    else:
        grad_up, grad_proj = over_batch(up_tile), over_batch(proj_tile)
    grad_down = grad_down.reshape(-1, block, min(part, hidden // batch)).transpose(0, 2, 1).reshape(-1, block)
    grad_proj = grad_proj.T

    grad_qkv, grad_normed1 = state
    grad_inputs, norm1 = first_norm_back(inputs, ln1_gain, grad_normed1, grad_res)
    norm = jnp.concatenate([norm1[:2], norm2[:2], jnp.zeros((4, width), F32)])
    owned = 3 * width // plane
    grad_qkv = grad_qkv.reshape(plane, owned, width)
    tiles = tail(me_array, grad_qkv, swap(grad_qkv, planes, plane, 1), norm, swap(norm, planes, plane, 1))
    tile = over_plane(tiles, plane).astype(BF16)
    qkv_tile = tile[:owned].reshape(owned, batch, slab).transpose(1, 0, 2)
    norm_tile = tile[owned:, :PAIR]
    if few:
        norm_tile = jnp.pad(norm_tile, ((0, 0), (0, slab - PAIR)))
        norm_tile = jnp.broadcast_to(norm_tile[None], (batch, *norm_tile.shape))
        summed = over_batch(jnp.concatenate([qkv_tile, norm_tile], axis=1))
        grad_qkv, norms = summed[:owned], summed[owned:]
    else:
        grad_qkv, norms = over_batch(qkv_tile), lax.psum(norm_tile.astype(F32), "batch")
    return (
        outputs.reshape(inputs.shape),
        grad_inputs.reshape(inputs.shape),
        grad_qkv.T,
        grad_proj,
        grad_up,
        grad_down,
        norms[:4, :block],
    )


def solution(mesh):
    placed = (
        P("batch", ("pb", "ka"), None),
        P("batch", None),
        P(),
        P(),
        P(),
        P(),
        P(),
        P(),
        P(),
        P(),
        P("batch", ("pb", "ka"), None),
    )
    return jax.shard_map(
        shards,
        mesh=mesh,
        in_specs=placed,
        out_specs=(
            P("batch", ("pb", "ka"), None),
            P("batch", ("pb", "ka"), None),
            P("batch", ("pb", "ka")),
            P("batch", ("pb", "ka")),
            P("batch", ("pb", "ka")),
            P("batch", ("pb", "ka")),
            P(None, ("pb", "ka")),
        ),
        check_vma=False,
    )
```

```python
import functools

import jax
import jax.numpy as jnp
from jax import lax
from jax.experimental import pallas as pl
from jax.experimental.pallas import tpu as pltpu
from jax.sharding import PartitionSpec as P

HEADS = 12
HEAD = 64
PAIR = 2 * HEAD
QTILE = 256
STRIP = 32
SCALE = HEAD ** (-0.5)
HUGE = 3e38
HIDDEN = -1e30

norm_eps = 1e-05
BF16 = jnp.bfloat16
F32 = jnp.float32


def norm_rows(values, gain_vec, shift_vec):
    average = jnp.mean(values, axis=-1, keepdims=True)
    centred = values - average
    spread = jnp.mean(centred * centred, axis=-1, keepdims=True)
    return centred * lax.rsqrt(spread + norm_eps) * gain_vec + shift_vec


def gelu_tanh(values):
    return jax.nn.gelu(values, approximate=True)


def dot(a, b, contract):
    return lax.dot_general(a, b, ((contract[:1], contract[1:]), ((), ())), preferred_element_type=F32)


def head_lanes(values, head):
    lane = lax.broadcasted_iota(jnp.int32, values.shape, 1)
    mine = lane < HEAD if head == 0 else lane >= HEAD
    return jnp.where(mine, values, jnp.zeros_like(values))


def hide_later(magnitude):
    keys = magnitude.shape[0]
    key = lax.broadcasted_iota(jnp.int32, (QTILE, QTILE), 0)
    query = lax.broadcasted_iota(jnp.int32, (QTILE, QTILE), 1)
    last = jnp.where(key <= query, magnitude[keys - QTILE :], HIDDEN)
    return last if keys == QTILE else jnp.concatenate([magnitude[: keys - QTILE], last], axis=0)


def sign_of(scores):
    return jnp.clip(scores * HUGE, -1.0, 1.0)


def attend_kernel(
    core_ref, place_ref, mine_ref, other_ref, gain_ref, shift_ref, wq_ref, wk_ref, wv_ref,
    out_ref, normed_ref, qkv_ref, sums_ref, stats_ref, o_sc,
):
    blocks, half = mine_ref.shape[0], mine_ref.shape[1]
    rows = 2 * half
    total_rows = normed_ref.shape[0]

    @pl.when(pl.program_id(0) == 0)
    def _():
        @pl.loop(0, blocks)
        def _(block):
            for ref, part in ((mine_ref, core_ref[0]), (other_ref, 1 - core_ref[0])):
                at = pl.multiple_of(place_ref[block] * rows + part * half, half)
                normed = norm_rows(ref[block].astype(F32), gain_ref[...], shift_ref[...])
                normed_ref[pl.ds(at, half), :] = normed.astype(BF16)

    weights = jnp.concatenate([wq_ref[...], wk_ref[...], wv_ref[...]], axis=1)
    qkv_ref[0] = jnp.dot(normed_ref[...], weights, preferred_element_type=F32).astype(BF16)
    v_t = qkv_ref[0, :, 2 * PAIR :].T
    for tile in range(total_rows // QTILE):
        span = slice(tile * QTILE, (tile + 1) * QTILE)
        keys = (tile + 1) * QTILE
        queries = qkv_ref[0, span, :PAIR] * SCALE
        for head in range(2):
            scores = dot(qkv_ref[0, :keys, PAIR : 2 * PAIR], head_lanes(queries, head).astype(BF16), (1, 1))
            magnitude = hide_later(jnp.abs(scores))
            peak = jnp.max(magnitude, axis=0, keepdims=True)
            exponents = jnp.exp(magnitude - peak)
            total = jnp.sum(exponents, axis=0, keepdims=True)
            weights = (exponents * sign_of(scores)).astype(BF16)
            summed = dot(v_t[head * HEAD : (head + 1) * HEAD, :keys], weights, (1, 0))
            sums_ref[0, head * HEAD : (head + 1) * HEAD, span] = summed / total
            stats_ref[0, head : head + 1, span] = peak + jnp.log(total)
        o_sc[span, :] = sums_ref[0, :, span].T
    for block in range(blocks):
        at = pl.multiple_of(place_ref[block] * rows, rows)
        out_ref[block] = o_sc[pl.ds(at, rows), :].astype(BF16)


def columns_of(width, size, kind, pairs):
    return pl.BlockSpec(
        (width, size), lambda i, core, place: (0, kind * (width // size) + core[0] * pairs + jnp.minimum(i, pairs - 1))
    )


def fixed2(shape):
    return pl.BlockSpec(shape, lambda i, *scalars, n=len(shape): (0,) * n)


def attend(core, place, mine, other, gain, shift, w_qkv):
    blocks, half, width = mine.shape
    length, pairs = 2 * half * blocks, width // PAIR // 2
    area = length * length
    return pl.pallas_call(
        attend_kernel,
        grid_spec=pltpu.PrefetchScalarGridSpec(
            num_scalar_prefetch=2,
            grid=(pairs,),
            in_specs=[fixed2(mine.shape), fixed2(mine.shape), fixed2((width,)), fixed2((width,))]
            + [columns_of(width, PAIR, kind, pairs) for kind in range(3)],
            out_specs=[
                pl.BlockSpec((blocks, 2 * half, PAIR), lambda i, c, p: (0, 0, i)),
                fixed2((length, width)),
                pl.BlockSpec((1, length, 3 * PAIR), lambda i, c, p: (i, 0, 0)),
                pl.BlockSpec((1, PAIR, length), lambda i, c, p: (i, 0, 0)),
                pl.BlockSpec((1, 8, length), lambda i, c, p: (i, 0, 0)),
            ],
            scratch_shapes=[pltpu.VMEM((length, PAIR), F32)],
        ),
        out_shape=[
            jax.ShapeDtypeStruct((blocks, 2 * half, pairs * PAIR), BF16),
            jax.ShapeDtypeStruct((length, width), BF16),
            jax.ShapeDtypeStruct((pairs, length, 3 * PAIR), BF16),
            jax.ShapeDtypeStruct((pairs, PAIR, length), F32),
            jax.ShapeDtypeStruct((pairs, 8, length), F32),
        ],
        cost_estimate=pl.CostEstimate(
            flops=pairs * 16 * area * HEAD + 3 * length * width * width,
            bytes_accessed=8 * length * width,
            transcendentals=pairs * area,
        ),
        name="attend",
    )(core, place, mine, other, gain, shift, w_qkv, w_qkv, w_qkv)


def attend_back_kernel(
    core_ref, place_ref, to_ref, qkv_ref, g_ref, sums_ref, stats_ref, normed_ref, out_ref, gq_ref, g_sc, dq_sc, dk_sc, dv_sc
):
    blocks, rows = g_ref.shape[0], g_ref.shape[1]
    for block in range(blocks):
        at = pl.multiple_of(place_ref[block] * rows, rows)
        g_sc[pl.ds(at, rows), :] = g_ref[block]
    total_rows = g_sc.shape[0]
    k_t = qkv_ref[0, :, PAIR : 2 * PAIR].T
    g_t = g_sc[...].astype(F32).T
    products = g_t * sums_ref[0]
    deltas = [
        jnp.sum(products[head * HEAD : (head + 1) * HEAD], axis=0, keepdims=True) for head in range(2)
    ]
    dk_sc[...] = jnp.zeros_like(dk_sc)
    dv_sc[...] = jnp.zeros_like(dv_sc)
    for tile in range(total_rows // QTILE):
        span = slice(tile * QTILE, (tile + 1) * QTILE)
        keys = (tile + 1) * QTILE
        queries = qkv_ref[0, span, :PAIR] * SCALE
        parts = []
        for head in range(2):
            q_head = head_lanes(queries, head).astype(BF16)
            g_head = head_lanes(g_sc[span, :], head)
            scores = dot(qkv_ref[0, :keys, PAIR : 2 * PAIR], q_head, (1, 1))
            magnitude = hide_later(jnp.abs(scores))
            sign = sign_of(scores)
            signed = jnp.exp(magnitude - stats_ref[0, head : head + 1, span]) * sign
            grad_weights = dot(qkv_ref[0, :keys, 2 * PAIR :], g_head, (1, 1))
            grad_scores = (signed * (sign * grad_weights - deltas[head][:, span])).astype(BF16)
            dv_sc[:keys, :] += dot(signed.astype(BF16), g_head, (1, 0))
            dk_sc[:keys, :] += dot(grad_scores, q_head, (1, 0))
            parts.append(dot(k_t[head * HEAD : (head + 1) * HEAD, :keys], grad_scores, (1, 0)))
        dq_sc[span, :] = jnp.concatenate(parts, axis=0).T * SCALE
    for kind, ref in enumerate((dq_sc, dk_sc, dv_sc)):
        grad = ref[...].astype(BF16)
        out_ref[:, kind * PAIR : (kind + 1) * PAIR] = grad
        turned = jnp.dot(grad.T, normed_ref[...], preferred_element_type=F32).astype(BF16)
        for strip in range(PAIR // STRIP):
            at = to_ref[(pl.program_id(0) * 3 + kind) * (PAIR // STRIP) + strip]
            at = pl.multiple_of(at * STRIP, STRIP)
            gq_ref[pl.ds(at, STRIP), :] = turned[strip * STRIP : (strip + 1) * STRIP]


def attend_back(core, place, to, qkv, grad, sums, stats, normed):
    pairs, length, _ = qkv.shape
    blocks, rows, _ = grad.shape
    width = normed.shape[1]
    area = length * length
    one = lambda i, c, p, t: (i, 0, 0)
    return pl.pallas_call(
        attend_back_kernel,
        grid_spec=pltpu.PrefetchScalarGridSpec(
            num_scalar_prefetch=3,
            grid=(pairs,),
            in_specs=[
                pl.BlockSpec((1, length, 3 * PAIR), one),
                pl.BlockSpec((blocks, rows, PAIR), lambda i, c, p, t: (0, 0, i)),
                pl.BlockSpec((1, PAIR, length), one),
                pl.BlockSpec((1, 8, length), one),
                fixed2(normed.shape),
            ],
            out_specs=[
                pl.BlockSpec((length, 3 * PAIR), lambda i, c, p, t: (0, i)),
                fixed2((pairs * 3 * PAIR, width)),
            ],
            scratch_shapes=[pltpu.VMEM((length, PAIR), BF16)] + [pltpu.VMEM((length, PAIR), F32)] * 3,
        ),
        out_shape=[
            jax.ShapeDtypeStruct((length, pairs * 3 * PAIR), BF16),
            jax.ShapeDtypeStruct((pairs * 3 * PAIR, width), BF16),
        ],
        cost_estimate=pl.CostEstimate(
            flops=pairs * 40 * area * HEAD + 3 * length * width * width,
            bytes_accessed=8 * length * width,
            transcendentals=pairs * area,
        ),
        name="attend_back",
    )(core, place, to, qkv, grad, sums, stats, normed)


def normed_back_kernel(
    core_ref, place_ref, back_ref, grad_ref, mine_ref, other_ref, norm_ref, wq_ref, wk_ref, wv_ref,
    keep_ref, send_ref, sums_ref, w_sc,
):
    step = pl.program_id(0)
    half = mine_ref.shape[1]
    pairs = wq_ref.shape[1] // PAIR

    @pl.when(step == 0)
    def _():
        sums_ref[...] = norm_ref[...]
        for pair in range(pairs):
            for kind, ref in enumerate((wq_ref, wk_ref, wv_ref)):
                w_sc[:, (pair * 3 + kind) * PAIR : (pair * 3 + kind + 1) * PAIR] = ref[
                    :, pair * PAIR : (pair + 1) * PAIR
                ]

    back = dot(grad_ref[...], w_sc[...], (1, 1))
    for at in range(grad_ref.shape[0] // (2 * half)):
        block = back_ref[step * (grad_ref.shape[0] // (2 * half)) + at]
        low = back[2 * at * half : (2 * at + 1) * half]
        high = back[(2 * at + 1) * half : (2 * at + 2) * half]
        first = core_ref[0] == 0
        mine, other = jnp.where(first, low, high), jnp.where(first, high, low)
        keep_ref[block] = mine
        send_ref[block] = other.astype(BF16)
        for grad, ref in ((mine, mine_ref), (other, other_ref)):
            x = ref[block].astype(F32)
            centred = x - jnp.mean(x, axis=-1, keepdims=True)
            unit = centred * lax.rsqrt(jnp.mean(centred * centred, axis=-1, keepdims=True) + norm_eps)
            sums_ref[0:1, :] += jnp.sum(grad * unit, axis=0, keepdims=True)
            sums_ref[1:2, :] += jnp.sum(grad, axis=0, keepdims=True)


def normed_back(core, place, back, grad, mine, other, norm, w_qkv):
    length, size = grad.shape
    blocks, half, width = mine.shape
    steps = 4
    columns = [
        pl.BlockSpec((width, size // 3), lambda i, core, p, b, kind=kind: (0, kind * 2 + core[0])) for kind in range(3)
    ]
    return pl.pallas_call(
        normed_back_kernel,
        grid_spec=pltpu.PrefetchScalarGridSpec(
            num_scalar_prefetch=3,
            grid=(steps,),
            in_specs=[
                pl.BlockSpec((length // steps, size), lambda i, c, p, b: (i, 0)),
                fixed2(mine.shape),
                fixed2(mine.shape),
                fixed2(norm.shape),
                *columns,
            ],
            out_specs=[fixed2(mine.shape), fixed2(mine.shape), fixed2(norm.shape)],
            scratch_shapes=[pltpu.VMEM((width, size), BF16)],
        ),
        out_shape=[
            jax.ShapeDtypeStruct(mine.shape, F32),
            jax.ShapeDtypeStruct(mine.shape, BF16),
            jax.ShapeDtypeStruct(norm.shape, F32),
        ],
        cost_estimate=pl.CostEstimate(
            flops=2 * length * width * size, bytes_accessed=8 * length * width, transcendentals=0
        ),
        name="normed_back",
    )(core, place, back, grad, mine, other, norm, w_qkv, w_qkv, w_qkv)


def merge_kernel(keep_ref, other_ref, norm_ref, out_ref):
    half = keep_ref.shape[1]
    block = norm_ref.shape[1] // keep_ref.shape[0]
    norms = norm_ref[...].astype(BF16)
    for at in range(keep_ref.shape[0]):
        out_ref[at, :half] = (keep_ref[at] + other_ref[at].astype(F32)).astype(BF16)
        out_ref[at, half:] = jnp.zeros_like(out_ref[at, half:])
        out_ref[at, half:, :block] = norms[:, at * block : (at + 1) * block]


def merge(keep, other, norm):
    blocks, half, width = keep.shape
    return pl.pallas_call(
        merge_kernel,
        grid=(1,),
        in_specs=[fixed2(keep.shape), fixed2(keep.shape), fixed2(norm.shape)],
        out_specs=fixed2((blocks, half + norm.shape[0], width)),
        out_shape=jax.ShapeDtypeStruct((blocks, half + norm.shape[0], width), BF16),
        cost_estimate=pl.CostEstimate(
            flops=blocks * half * width, bytes_accessed=8 * blocks * half * width, transcendentals=0
        ),
        name="merge",
    )(keep, other, norm)


@functools.lru_cache
def strips(width, plane):
    near, owned = plane // 2, 3 * width // plane // STRIP
    side, pair = width // 2 // STRIP, PAIR // STRIP
    slots = []
    for core in range(2):
        slot, count = {}, [0, 0]
        for col in range(2 * near * owned):
            if col % (2 * side) // side == core:
                away = (col // owned % 2) ^ core
                slot[col] = (away, count[away])
                count[away] += 1
        assert count == [near * owned // 2] * 2
        slots.append(slot)
    stay = near * owned // 2
    to, found = [], []
    for core in range(2):
        order = [
            kind * 2 * side + core * side + p * pair + strip
            for p in range(side // pair)
            for kind in range(3)
            for strip in range(pair)
        ]
        to.append([slots[core][col][0] * stay + slots[core][col][1] for col in order])
        row = []
        for chip in range(near):
            for strip in range(owned):
                col = (2 * chip + core) * owned + strip
                row.append(slots[core][col][1] if col in slots[core] else stay + slots[1 - core][col][1])
        found.append(row)
    return to, found


def tiles_kernel(near, owned, chip_ref, found_ref, keep_ref, given_ref, *outs):
    step = pl.program_id(0)
    stay = keep_ref.shape[0] // STRIP
    for k in range(near):

        @pl.when(step == k)
        def _():
            for strip in range(owned):
                at = found_ref[(chip_ref[0] ^ k) * owned + strip]
                here = pl.multiple_of(jnp.minimum(at, stay - 1) * STRIP, STRIP)
                there = pl.multiple_of(jnp.maximum(at - stay, 0) * STRIP, STRIP)
                outs[k][strip * STRIP : (strip + 1) * STRIP, :] = jnp.where(
                    at < stay, keep_ref[pl.ds(here, STRIP), :], given_ref[pl.ds(there, STRIP), :]
                )


def qkv_tiles(chip, found, keep, given, near):
    size, width = keep.shape
    owned = 2 * size // near // STRIP
    shape = (owned * STRIP, width)
    return pl.pallas_call(
        functools.partial(tiles_kernel, near, owned),
        grid_spec=pltpu.PrefetchScalarGridSpec(
            num_scalar_prefetch=2,
            grid=(near,),
            in_specs=[fixed2(keep.shape), fixed2(keep.shape)],
            out_specs=[fixed2(shape)] * near,
        ),
        out_shape=[jax.ShapeDtypeStruct(shape, BF16)] * near,
        cost_estimate=pl.CostEstimate(flops=size * width, bytes_accessed=8 * size * width, transcendentals=0),
        name="qkv_tiles",
    )(chip, found, keep, given)


def gelu_pair(u):
    c = 0.7978845608028654
    square = u * u
    t = jnp.tanh(c * u * (1.0 + 0.044715 * square))
    half = 0.5 * (1.0 + t)
    slope = half + 0.5 * c * u * (1.0 - t * t) * (1.0 + 3.0 * 0.044715 * square)
    return u * half, slope


def norm_back(values, gain_vec, grad):
    average = jnp.mean(values, axis=-1, keepdims=True)
    centred = values - average
    spread = jnp.mean(centred * centred, axis=-1, keepdims=True)
    scale = lax.rsqrt(spread + norm_eps)
    unit = centred * scale
    scaled = grad * gain_vec
    back = scale * (
        scaled
        - jnp.mean(scaled, axis=-1, keepdims=True)
        - unit * jnp.mean(scaled * unit, axis=-1, keepdims=True)
    )
    return back, jnp.sum(grad * unit, axis=0, keepdims=True), jnp.sum(grad, axis=0, keepdims=True)


def ff_kernel(seqs, plane, *refs):
    me_ref, x_ref, att_ref, cot_ref, w_out_ref, gain_ref, shift_ref, up_ref, down_ref, *refs = refs
    out_ref, res_ref, *refs = refs
    ga_ref, norm_ref, gu_send, gu_keep, gd_send, gd_keep, gp_send, gp_keep, *refs = refs
    att_sc, residual_sc, normed_sc, normed_t, turned_sc, acc_out, acc_grad = refs
    step = pl.program_id(0)
    tokens, width = x_ref.shape
    rows = tokens // seqs
    block = width // plane
    near = plane // 2

    def turn(values):
        turned = values.T
        for j in range(plane):
            t = me_ref[0] ^ j
            slot = (1 - (t & 1)) * near + (t >> 1)
            at = pl.multiple_of(slot * block, block)
            turned_sc[pl.ds(at, block), :] = turned[j * block : (j + 1) * block]

    @pl.when(step == 0)
    def _():
        for seq in range(seqs):
            for core in range(2):
                cols = slice(core * width // 2, (core + 1) * width // 2)
                att_sc[seq * rows : (seq + 1) * rows, cols] = att_ref[seq * 2 + core]
        residual = x_ref[...].astype(F32) + jnp.dot(att_sc[...], w_out_ref[...], preferred_element_type=F32)
        residual_sc[...] = residual
        normed = norm_rows(residual, gain_ref[...], shift_ref[...]).astype(BF16)
        normed_sc[...] = normed
        normed_t[...] = normed.T
        turn(cot_ref[...])
        acc_out[...] = jnp.zeros_like(acc_out)
        acc_grad[...] = jnp.zeros_like(acc_grad)

    pre = jnp.dot(normed_sc[...], up_ref[...], preferred_element_type=F32)
    active, slope = gelu_pair(pre)
    active = active.astype(BF16)
    grad_pre = (dot(cot_ref[...], down_ref[...], (1, 1)) * slope).astype(BF16)
    acc_out[...] += jnp.dot(active, down_ref[...], preferred_element_type=F32)
    acc_grad[...] += dot(grad_pre, up_ref[...], (1, 1))
    grad_up = jnp.dot(normed_t[...], grad_pre, preferred_element_type=F32).astype(BF16)
    grad_down = jnp.dot(turned_sc[...], active, preferred_element_type=F32).astype(BF16)
    for slot in range(near):
        gd_send[slot, 0] = grad_down[slot * block : (slot + 1) * block]
        gd_keep[slot, 0] = grad_down[(near + slot) * block : (near + slot + 1) * block]

    @pl.when(step < near)
    def _():
        gu_send[0] = grad_up

    @pl.when(step >= near)
    def _():
        gu_keep[0] = grad_up

    @pl.when(step == plane - 1)
    def _():
        residual = residual_sc[...]
        out_ref[...] = (residual + acc_out[...]).astype(BF16)
        back, gain_grad, shift_grad = norm_back(residual, gain_ref[...], acc_grad[...])
        norm_ref[...] = jnp.zeros_like(norm_ref)
        norm_ref[2:3, :] = gain_grad
        norm_ref[3:4, :] = shift_grad
        grad_res = cot_ref[...].astype(F32) + back
        res_ref[...] = grad_res
        grad_z = grad_res.astype(BF16)
        grad_att = dot(grad_z, w_out_ref[...], (1, 1)).astype(BF16)
        for seq in range(seqs):
            for core in range(2):
                cols = slice(core * width // 2, (core + 1) * width // 2)
                ga_ref[seq * 2 + core] = grad_att[seq * rows : (seq + 1) * rows, cols]
        turn(grad_z)
        grad_proj = jnp.dot(turned_sc[...], att_sc[...], preferred_element_type=F32).astype(BF16)
        for slot in range(near):
            gp_send[slot] = grad_proj[slot * block : (slot + 1) * block]
            gp_keep[slot] = grad_proj[(near + slot) * block : (near + slot + 1) * block]


def feed_forward(me, x, attended, cotangent, w_out, gain, shift, w_up, w_down, plane):
    seqs, rows, width = x.shape
    hidden = w_up.shape[1]
    tokens, near, part, block = seqs * rows, plane // 2, hidden // plane, width // plane

    def at(i, me):
        return me[0] ^ (2 * (i % near) + jnp.where(i < near, 1, 0))

    def fixed(shape):
        return pl.BlockSpec(shape, lambda i, me, n=len(shape): (0,) * n)

    joined = attended.shape
    outs = [
        ((tokens, width), BF16, fixed((tokens, width))),
        ((tokens, width), F32, fixed((tokens, width))),
        (joined, BF16, fixed(joined)),
        ((8, width), F32, fixed((8, width))),
        ((near, width, part), BF16, pl.BlockSpec((1, width, part), lambda i, me: (jnp.minimum(i, near - 1), 0, 0))),
        ((near, width, part), BF16, pl.BlockSpec((1, width, part), lambda i, me: (jnp.maximum(i - near, 0), 0, 0))),
        *[
            (
                (near, plane, block, part),
                BF16,
                pl.BlockSpec((near, 1, block, part), lambda i, me: (0, at(i, me), 0, 0)),
            )
        ]
        * 2,
        *[((near, block, width), BF16, fixed((near, block, width)))] * 2,
    ]
    return pl.pallas_call(
        functools.partial(ff_kernel, seqs, plane),
        grid_spec=pltpu.PrefetchScalarGridSpec(
            num_scalar_prefetch=1,
            grid=(plane,),
            in_specs=[fixed((tokens, width))]
            + [fixed(joined), fixed((tokens, width)), fixed((width, width)), fixed((width,)), fixed((width,))]
            + [
                pl.BlockSpec((width, part), lambda i, me: (0, at(i, me))),
                pl.BlockSpec((part, width), lambda i, me: (at(i, me), 0)),
            ],
            out_specs=[o[2] for o in outs],
            scratch_shapes=[
                pltpu.VMEM((tokens, width), BF16),
                pltpu.VMEM((tokens, width), F32),
                pltpu.VMEM((tokens, width), BF16),
                pltpu.VMEM((width, tokens), BF16),
                pltpu.VMEM((width, tokens), BF16),
                pltpu.VMEM((tokens, width), F32),
                pltpu.VMEM((tokens, width), F32),
            ],
        ),
        out_shape=[jax.ShapeDtypeStruct(o[0], o[1]) for o in outs],
        cost_estimate=pl.CostEstimate(
            flops=12 * tokens * width * hidden + 6 * tokens * width * width,
            bytes_accessed=8 * width * hidden,
            transcendentals=tokens * hidden,
        ),
        name="feed_forward",
    )(
        me,
        x.reshape(tokens, width),
        attended,
        cotangent.reshape(tokens, width),
        w_out,
        gain,
        shift,
        w_up,
        w_down,
    )


def first_norm_kernel(seqs, x_ref, gain_ref, grad_ref, res_ref, out_ref, norm_ref):
    half = x_ref.shape[0] // seqs // 2
    for piece in range(2 * seqs):
        at = slice(piece * half, (piece + 1) * half)
        values = x_ref[at].astype(F32)
        centred = values - jnp.mean(values, axis=-1, keepdims=True)
        scale = lax.rsqrt(jnp.mean(centred * centred, axis=-1, keepdims=True) + norm_eps)
        unit = centred * scale
        scaled = grad_ref[piece, :half].astype(F32) * gain_ref[...]
        back = scale * (
            scaled
            - jnp.mean(scaled, axis=-1, keepdims=True)
            - unit * jnp.mean(scaled * unit, axis=-1, keepdims=True)
        )
        out_ref[at] = (res_ref[at] + back).astype(BF16)
    norms = grad_ref[0, half:, :PAIR].astype(F32)
    for piece in range(1, 2 * seqs):
        norms = norms + grad_ref[piece, half:, :PAIR].astype(F32)
    norm_ref[...] = norms


def first_norm_back(x, gain, grad, grad_res):
    seqs, rows, width = x.shape
    tokens = seqs * rows
    return pl.pallas_call(
        functools.partial(first_norm_kernel, seqs),
        grid=(1,),
        in_specs=[fixed2((tokens, width)), fixed2((width,)), fixed2(grad.shape), fixed2((tokens, width))],
        out_specs=[fixed2((tokens, width)), fixed2((8, PAIR))],
        out_shape=[jax.ShapeDtypeStruct((tokens, width), BF16), jax.ShapeDtypeStruct((8, PAIR), F32)],
        cost_estimate=pl.CostEstimate(flops=20 * tokens * width, bytes_accessed=12 * tokens * width, transcendentals=0),
        name="first_norm_back",
    )(x.reshape(tokens, width), gain, grad, grad_res)


def exchange(blocks):
    return lax.all_to_all(blocks, ("pb", "ka"), 0, 0, tiled=True)


def swap(values, axes, size, bit):
    return lax.ppermute(values, axes, [(i, i ^ bit) for i in range(size)])


def add_pair_kernel(near, batch, *refs):
    _, up_a, up_b, down_a, down_b, proj_a, proj_b, *outs = refs
    outs, down_outs = outs[:near], outs[near:]
    step = pl.program_id(0)
    part = outs[0].shape[1]

    def both(a, b):
        return (a.astype(F32) + b.astype(F32)).astype(BF16)

    @pl.when(step < batch)
    def _():
        for k in range(near):
            outs[k][...] = both(up_a[k], up_b[k])

    for far in range(batch):

        @pl.when(step == batch + far)
        def _():
            for k in range(near):
                total = both(down_a[k], down_b[k])
                slab = total.shape[0] * total.shape[1]
                down_outs[far][k * slab : (k + 1) * slab] = total.reshape(slab, part)

    @pl.when(step == 2 * batch)
    def _():
        for k in range(near):
            total = both(proj_a[k], proj_b[k])
            outs[k][...] = jnp.concatenate([total[:, :part], total[:, part:]], axis=0)


def add_pair(mine, up, down, proj, batch):
    near, width, part = up[0].shape
    plane, block = down[0].shape[1:3]
    tall, few = width // batch, plane // batch
    up_spec = pl.BlockSpec((near, tall, part), lambda i, m: (0, jnp.minimum(i, batch - 1), 0))
    down_spec = pl.BlockSpec(
        (near, few, block, part), lambda i, m: (0, m[0] ^ jnp.clip(i - batch, 0, batch - 1), 0, 0)
    )
    proj_spec = pl.BlockSpec((near, block, width), lambda i, m: (0, 0, 0))
    last = lambda i, m: (jnp.where(i < batch, i, jnp.where(i < 2 * batch, batch - 1, batch)), 0)
    down_shape = (near * few * block, part)
    return pl.pallas_call(
        functools.partial(add_pair_kernel, near, batch),
        grid_spec=pltpu.PrefetchScalarGridSpec(
            num_scalar_prefetch=1,
            grid=(2 * batch + 1,),
            in_specs=[up_spec] * 2 + [down_spec] * 2 + [proj_spec] * 2,
            out_specs=[pl.BlockSpec((tall, part), last)] * near
            + [pl.BlockSpec(down_shape, lambda i, m: (0, 0))] * batch,
        ),
        out_shape=[jax.ShapeDtypeStruct((width + tall, part), BF16)] * near
        + [jax.ShapeDtypeStruct(down_shape, BF16)] * batch,
        cost_estimate=pl.CostEstimate(
            flops=near * 9 * tall * part, bytes_accessed=6 * near * 9 * tall * part, transcendentals=0
        ),
        name="add_pair",
    )(mine, *up, *down, *proj)


def add_all(parts):
    total = parts[0].astype(F32)
    for p in parts[1:]:
        total = total + p.astype(F32)
    return total


def over_batch(stacked):
    size = lax.axis_size("batch")
    mine = lax.axis_index("batch")
    if size > 4:
        return lax.psum_scatter(stacked, "batch", scatter_dimension=0, tiled=True)[0].astype(F32)
    parts = [lax.dynamic_index_in_dim(stacked, mine, 0, False)]
    for bit in range(1, size):
        block = lax.dynamic_index_in_dim(stacked, mine ^ bit, 0, False)
        parts.append(swap(block, "batch", size, bit))
    return add_all(parts)


def over_plane(tiles, plane):
    parts = [tiles[0]]
    for k in range(1, len(tiles)):
        parts.append(swap(tiles[k], ("pb", "ka"), plane, 2 * k))
    return add_all(parts)


def shards(
    inputs,
    block_place,
    ln1_gain,
    ln1_shift,
    w_qkv,
    w_out,
    ln2_gain,
    ln2_shift,
    w_up,
    w_down,
    cotangent,
):
    seqs, rows, width = inputs.shape
    hidden = w_up.shape[1]
    plane = lax.axis_size("pb") * lax.axis_size("ka")
    planes = ("pb", "ka")
    batch = lax.axis_size("batch")
    near = plane // 2
    few = batch <= 4
    me = lax.axis_index(planes)
    scalar = lambda value: value.astype(jnp.int32).reshape(1)
    core, chip = scalar(me & 1), scalar(me >> 1)
    part, block, slab = hidden // plane, width // plane, width // batch
    place = lax.dynamic_index_in_dim(block_place, me >> 1, 0, False)
    spots = jnp.arange(plane, dtype=jnp.int32)
    back = jnp.sum(jnp.where(place[None] == spots[:, None], spots[None], 0), axis=1)
    to, found = [jnp.where(core == 0, *(jnp.array(t, jnp.int32) for t in both)) for both in strips(width, plane)]

    mine = exchange(inputs.reshape(plane, seqs * rows // plane, width))
    other = swap(mine, planes, plane, 1)
    attended, normed1, packed, sums, stats = attend(core, place, mine, other, ln1_gain, ln1_shift, w_qkv)
    outputs, grad_res, grad_att, norm2, *grads = feed_forward(
        scalar(me), inputs, exchange(attended), cotangent, w_out, ln2_gain, ln2_shift, w_up, w_down, plane
    )
    grad_att = exchange(grad_att)
    up, down, proj = [(grads[2 * i + 1], swap(grads[2 * i], planes, plane, 1)) for i in range(3)]
    if few:
        sums_up = add_pair(scalar(lax.axis_index("batch")), up, down, proj, batch)
        grad_att, sums_up = lax.optimization_barrier((grad_att, sums_up))
        tiles, down = sums_up[:near], sums_up[near:]
    else:
        tiles = [
            jnp.concatenate(
                [add_all([t[k] for t in up])]
                + [add_all([t[k] for t in down]).reshape(width, part)]
                + [add_all([t[k] for t in proj]).reshape(block, 2, part).transpose(1, 0, 2).reshape(2 * block, part)]
            ).astype(BF16)
            for k in range(near)
        ]
    tile = over_plane(tiles, plane).astype(BF16)
    if few:
        down_parts = [down[0]] + [swap(down[bit], "batch", batch, bit) for bit in range(1, batch)]
        down_parts = [d.reshape(near, -1, part) for d in down_parts]
        down_tiles = [add_all([d[k] for d in down_parts]).astype(BF16) for k in range(near)]

    grad_packed, grad_qkv = attend_back(core, place, to, packed, grad_att, sums, stats, normed1)
    grad_packed, tile = lax.optimization_barrier((grad_packed, tile))
    stay = grad_qkv.shape[0] // 2
    given = swap(grad_qkv[stay:], planes, plane, 1)
    keep, send, norm = normed_back(
        core, place, back, grad_packed, mine, other, norm2, w_qkv
    )
    tiles = qkv_tiles(chip, found, grad_qkv[:stay], given, near)
    returned = exchange(merge(keep, swap(send, planes, plane, 1), norm))
    if few:
        returned, down_tiles = lax.optimization_barrier((returned, down_tiles))
    grad_inputs, norm = first_norm_back(inputs, ln1_gain, returned, grad_res)

    if few:
        grad_down = over_plane(down_tiles, plane)
    else:
        cut = batch // plane
        down_tile = tile[width : 2 * width].reshape(plane, block, cut, part // cut).transpose(0, 2, 1, 3)
        grad_down = over_batch(down_tile.reshape(batch, block, part // cut))
    proj_tile = tile[-2 * block :].reshape(2, block, part).transpose(1, 0, 2).reshape(block, batch, slab)
    proj_tile = proj_tile.transpose(1, 0, 2)
    up_tile = tile[:width].reshape(batch, slab, part)
    if few:
        joined = jnp.concatenate([up_tile, proj_tile.reshape(batch, block * slab // part, part)], axis=1)
        summed = over_batch(joined)
        grad_up, grad_proj = summed[:slab], summed[slab:].reshape(block, slab)
    else:
        grad_up, grad_proj = over_batch(up_tile), over_batch(proj_tile)
    grad_down = grad_down.reshape(-1, block, min(part, hidden // batch)).transpose(0, 2, 1).reshape(-1, block)
    grad_proj = grad_proj.T

    owned = 3 * width // plane
    tile = over_plane(tiles, plane).astype(BF16)
    qkv_tile = tile.reshape(owned, batch, slab).transpose(1, 0, 2)
    if few:
        norm_tile = jnp.pad(norm.astype(BF16), ((0, 8), (0, slab - PAIR)))
        norm_tile = jnp.broadcast_to(norm_tile[None], (batch, *norm_tile.shape))
        summed = over_batch(jnp.concatenate([qkv_tile, norm_tile], axis=1))
        grad_qkv, norms = summed[:owned], summed[owned:]
    else:
        grad_qkv, norms = over_batch(qkv_tile), lax.psum(norm, "batch")
    return (
        outputs.reshape(inputs.shape),
        grad_inputs.reshape(inputs.shape),
        grad_qkv.T,
        grad_proj,
        grad_up,
        grad_down,
        norms[:4, :block],
    )


def solution(mesh):
    placed = (
        P("batch", ("pb", "ka"), None),
        P("batch", None),
        P(),
        P(),
        P(),
        P(),
        P(),
        P(),
        P(),
        P(),
        P("batch", ("pb", "ka"), None),
    )
    return jax.shard_map(
        shards,
        mesh=mesh,
        in_specs=placed,
        out_specs=(
            P("batch", ("pb", "ka"), None),
            P("batch", ("pb", "ka"), None),
            P("batch", ("pb", "ka")),
            P("batch", ("pb", "ka")),
            P("batch", ("pb", "ka")),
            P("batch", ("pb", "ka")),
            P(None, ("pb", "ka")),
        ),
        check_vma=False,
    )
```

```python
import functools

import jax
import jax.numpy as jnp
from jax import lax
from jax.experimental import pallas as pl
from jax.experimental.pallas import tpu as pltpu
from jax.sharding import PartitionSpec as P

HEADS = 12
HEAD = 64
PAIR = 2 * HEAD
QTILE = 256
STRIP = 32
SCALE = HEAD ** (-0.5)
HUGE = 3e38
HIDDEN = -1e30

norm_eps = 1e-05
BF16 = jnp.bfloat16
F32 = jnp.float32


def norm_rows(values, gain_vec, shift_vec):
    average = jnp.mean(values, axis=-1, keepdims=True)
    centred = values - average
    spread = jnp.mean(centred * centred, axis=-1, keepdims=True)
    return centred * lax.rsqrt(spread + norm_eps) * gain_vec + shift_vec


def gelu_tanh(values):
    return jax.nn.gelu(values, approximate=True)


def dot(a, b, contract):
    return lax.dot_general(a, b, ((contract[:1], contract[1:]), ((), ())), preferred_element_type=F32)


def head_lanes(values, head):
    lane = lax.broadcasted_iota(jnp.int32, values.shape, 1)
    mine = lane < HEAD if head == 0 else lane >= HEAD
    return jnp.where(mine, values, jnp.zeros_like(values))


def hide_later(magnitude):
    keys = magnitude.shape[0]
    key = lax.broadcasted_iota(jnp.int32, (QTILE, QTILE), 0)
    query = lax.broadcasted_iota(jnp.int32, (QTILE, QTILE), 1)
    last = jnp.where(key <= query, magnitude[keys - QTILE :], HIDDEN)
    return last if keys == QTILE else jnp.concatenate([magnitude[: keys - QTILE], last], axis=0)


def sign_of(scores):
    return jnp.clip(scores * HUGE, -1.0, 1.0)


def attend_kernel(
    core_ref, place_ref, mine_ref, other_ref, gain_ref, shift_ref, wq_ref, wk_ref, wv_ref,
    out_ref, normed_ref, qkv_ref, sums_ref, stats_ref, o_sc,
):
    blocks, half = mine_ref.shape[0], mine_ref.shape[1]
    rows = 2 * half
    total_rows = normed_ref.shape[0]

    @pl.when(pl.program_id(0) == 0)
    def _():
        @pl.loop(0, blocks)
        def _(block):
            for ref, part in ((mine_ref, core_ref[0]), (other_ref, 1 - core_ref[0])):
                at = pl.multiple_of(place_ref[block] * rows + part * half, half)
                normed = norm_rows(ref[block].astype(F32), gain_ref[...], shift_ref[...])
                normed_ref[pl.ds(at, half), :] = normed.astype(BF16)

    weights = jnp.concatenate([wq_ref[...], wk_ref[...], wv_ref[...]], axis=1)
    qkv_ref[0] = jnp.dot(normed_ref[...], weights, preferred_element_type=F32).astype(BF16)
    v_t = qkv_ref[0, :, 2 * PAIR :].T
    for tile in range(total_rows // QTILE):
        span = slice(tile * QTILE, (tile + 1) * QTILE)
        keys = (tile + 1) * QTILE
        queries = qkv_ref[0, span, :PAIR] * SCALE
        for head in range(2):
            scores = dot(qkv_ref[0, :keys, PAIR : 2 * PAIR], head_lanes(queries, head).astype(BF16), (1, 1))
            magnitude = hide_later(jnp.abs(scores))
            peak = jnp.max(magnitude, axis=0, keepdims=True)
            exponents = jnp.exp(magnitude - peak)
            total = jnp.sum(exponents, axis=0, keepdims=True)
            weights = (exponents * sign_of(scores)).astype(BF16)
            summed = dot(v_t[head * HEAD : (head + 1) * HEAD, :keys], weights, (1, 0))
            sums_ref[0, head * HEAD : (head + 1) * HEAD, span] = summed / total
            stats_ref[0, head : head + 1, span] = peak + jnp.log(total)
        o_sc[span, :] = sums_ref[0, :, span].T
    for block in range(blocks):
        at = pl.multiple_of(place_ref[block] * rows, rows)
        out_ref[block] = o_sc[pl.ds(at, rows), :].astype(BF16)


def columns_of(width, size, kind, pairs):
    return pl.BlockSpec(
        (width, size), lambda i, core, place: (0, kind * (width // size) + core[0] * pairs + jnp.minimum(i, pairs - 1))
    )


def fixed2(shape):
    return pl.BlockSpec(shape, lambda i, *scalars, n=len(shape): (0,) * n)


def attend(core, place, mine, other, gain, shift, w_qkv):
    blocks, half, width = mine.shape
    length, pairs = 2 * half * blocks, width // PAIR // 2
    area = length * length
    return pl.pallas_call(
        attend_kernel,
        grid_spec=pltpu.PrefetchScalarGridSpec(
            num_scalar_prefetch=2,
            grid=(pairs,),
            in_specs=[fixed2(mine.shape), fixed2(mine.shape), fixed2((width,)), fixed2((width,))]
            + [columns_of(width, PAIR, kind, pairs) for kind in range(3)],
            out_specs=[
                pl.BlockSpec((blocks, 2 * half, PAIR), lambda i, c, p: (0, 0, i)),
                fixed2((length, width)),
                pl.BlockSpec((1, length, 3 * PAIR), lambda i, c, p: (i, 0, 0)),
                pl.BlockSpec((1, PAIR, length), lambda i, c, p: (i, 0, 0)),
                pl.BlockSpec((1, 8, length), lambda i, c, p: (i, 0, 0)),
            ],
            scratch_shapes=[pltpu.VMEM((length, PAIR), F32)],
        ),
        out_shape=[
            jax.ShapeDtypeStruct((blocks, 2 * half, pairs * PAIR), BF16),
            jax.ShapeDtypeStruct((length, width), BF16),
            jax.ShapeDtypeStruct((pairs, length, 3 * PAIR), BF16),
            jax.ShapeDtypeStruct((pairs, PAIR, length), F32),
            jax.ShapeDtypeStruct((pairs, 8, length), F32),
        ],
        cost_estimate=pl.CostEstimate(
            flops=pairs * 16 * area * HEAD + 3 * length * width * width,
            bytes_accessed=8 * length * width,
            transcendentals=pairs * area,
        ),
        name="attend",
    )(core, place, mine, other, gain, shift, w_qkv, w_qkv, w_qkv)


def attend_back_kernel(
    core_ref, place_ref, to_ref, qkv_ref, g_ref, sums_ref, stats_ref, normed_ref, mine_ref, other_ref, norm_ref,
    wq_ref, wk_ref, wv_ref, gq_ref, keep_ref, send_ref, norms_ref, g_sc, dq_sc, dk_sc, dv_sc, packed_sc, back_sc,
):
    blocks, rows = g_ref.shape[0], g_ref.shape[1]
    for block in range(blocks):
        at = pl.multiple_of(place_ref[block] * rows, rows)
        g_sc[pl.ds(at, rows), :] = g_ref[block]
    total_rows = g_sc.shape[0]
    k_t = qkv_ref[0, :, PAIR : 2 * PAIR].T
    g_t = g_sc[...].astype(F32).T
    products = g_t * sums_ref[0]
    deltas = [
        jnp.sum(products[head * HEAD : (head + 1) * HEAD], axis=0, keepdims=True) for head in range(2)
    ]
    dk_sc[...] = jnp.zeros_like(dk_sc)
    dv_sc[...] = jnp.zeros_like(dv_sc)
    for tile in range(total_rows // QTILE):
        span = slice(tile * QTILE, (tile + 1) * QTILE)
        keys = (tile + 1) * QTILE
        queries = qkv_ref[0, span, :PAIR] * SCALE
        parts = []
        for head in range(2):
            q_head = head_lanes(queries, head).astype(BF16)
            g_head = head_lanes(g_sc[span, :], head)
            scores = dot(qkv_ref[0, :keys, PAIR : 2 * PAIR], q_head, (1, 1))
            magnitude = hide_later(jnp.abs(scores))
            sign = sign_of(scores)
            signed = jnp.exp(magnitude - stats_ref[0, head : head + 1, span]) * sign
            grad_weights = dot(qkv_ref[0, :keys, 2 * PAIR :], g_head, (1, 1))
            grad_scores = (signed * (sign * grad_weights - deltas[head][:, span])).astype(BF16)
            dv_sc[:keys, :] += dot(signed.astype(BF16), g_head, (1, 0))
            dk_sc[:keys, :] += dot(grad_scores, q_head, (1, 0))
            parts.append(dot(k_t[head * HEAD : (head + 1) * HEAD, :keys], grad_scores, (1, 0)))
        dq_sc[span, :] = jnp.concatenate(parts, axis=0).T * SCALE
    for kind, ref in enumerate((dq_sc, dk_sc, dv_sc)):
        grad = ref[...].astype(BF16)
        packed_sc[:, kind * PAIR : (kind + 1) * PAIR] = grad
        turned = jnp.dot(grad.T, normed_ref[...], preferred_element_type=F32).astype(BF16)
        for strip in range(PAIR // STRIP):
            at = to_ref[(pl.program_id(0) * 3 + kind) * (PAIR // STRIP) + strip]
            at = pl.multiple_of(at * STRIP, STRIP)
            gq_ref[pl.ds(at, STRIP), :] = turned[strip * STRIP : (strip + 1) * STRIP]

    step, half = pl.program_id(0), mine_ref.shape[1]
    weights = jnp.concatenate([wq_ref[...], wk_ref[...], wv_ref[...]], axis=1)
    back = dot(packed_sc[...], weights, (1, 1))

    @pl.when(step == 0)
    def _():
        back_sc[...] = back

    @pl.when(step > 0)
    def _():
        back_sc[...] += back

    @pl.when(step == pl.num_programs(0) - 1)
    def _():
        norms_ref[...] = norm_ref[...]

        @pl.loop(0, blocks)
        def _(block):
            for ref, out_ref, part in ((mine_ref, keep_ref, core_ref[0]), (other_ref, send_ref, 1 - core_ref[0])):
                at = pl.multiple_of(place_ref[block] * rows + part * half, half)
                grad = back_sc[pl.ds(at, half), :]
                out_ref[block] = grad.astype(out_ref.dtype)
                x = ref[block].astype(F32)
                centred = x - jnp.mean(x, axis=-1, keepdims=True)
                unit = centred * lax.rsqrt(jnp.mean(centred * centred, axis=-1, keepdims=True) + norm_eps)
                norms_ref[0:1, :] += jnp.sum(grad * unit, axis=0, keepdims=True)
                norms_ref[1:2, :] += jnp.sum(grad, axis=0, keepdims=True)


def attend_back(core, place, to, qkv, grad, sums, stats, normed, mine, other, norm, w_qkv):
    pairs, length, _ = qkv.shape
    blocks, rows, _ = grad.shape
    width = normed.shape[1]
    area = length * length
    one = lambda i, c, p, t: (i, 0, 0)

    def columns(kind):
        size = width // PAIR
        return pl.BlockSpec((width, PAIR), lambda i, core, p, t: (0, kind * size + core[0] * pairs + i))

    return pl.pallas_call(
        attend_back_kernel,
        grid_spec=pltpu.PrefetchScalarGridSpec(
            num_scalar_prefetch=3,
            grid=(pairs,),
            in_specs=[
                pl.BlockSpec((1, length, 3 * PAIR), one),
                pl.BlockSpec((blocks, rows, PAIR), lambda i, c, p, t: (0, 0, i)),
                pl.BlockSpec((1, PAIR, length), one),
                pl.BlockSpec((1, 8, length), one),
                fixed2(normed.shape),
                fixed2(mine.shape),
                fixed2(mine.shape),
                fixed2(norm.shape),
                *(columns(kind) for kind in range(3)),
            ],
            out_specs=[
                fixed2((pairs * 3 * PAIR, width)),
                fixed2(mine.shape),
                fixed2(mine.shape),
                fixed2(norm.shape),
            ],
            scratch_shapes=[
                pltpu.VMEM((length, PAIR), BF16),
                *[pltpu.VMEM((length, PAIR), F32)] * 3,
                pltpu.VMEM((length, 3 * PAIR), BF16),
                pltpu.VMEM((length, width), F32),
            ],
        ),
        out_shape=[
            jax.ShapeDtypeStruct((pairs * 3 * PAIR, width), BF16),
            jax.ShapeDtypeStruct(mine.shape, F32),
            jax.ShapeDtypeStruct(mine.shape, BF16),
            jax.ShapeDtypeStruct(norm.shape, F32),
        ],
        cost_estimate=pl.CostEstimate(
            flops=pairs * 40 * area * HEAD + 6 * length * width * width,
            bytes_accessed=8 * length * width,
            transcendentals=pairs * area,
        ),
        name="attend_back",
    )(core, place, to, qkv, grad, sums, stats, normed, mine, other, norm, w_qkv, w_qkv, w_qkv)


def merge_kernel(keep_ref, other_ref, norm_ref, out_ref):
    half = keep_ref.shape[1]
    block = norm_ref.shape[1] // keep_ref.shape[0]
    norms = norm_ref[...].astype(BF16)
    for at in range(keep_ref.shape[0]):
        out_ref[at, :half] = (keep_ref[at] + other_ref[at].astype(F32)).astype(BF16)
        out_ref[at, half:] = jnp.zeros_like(out_ref[at, half:])
        out_ref[at, half:, :block] = norms[:, at * block : (at + 1) * block]


def merge(keep, other, norm):
    blocks, half, width = keep.shape
    return pl.pallas_call(
        merge_kernel,
        grid=(1,),
        in_specs=[fixed2(keep.shape), fixed2(keep.shape), fixed2(norm.shape)],
        out_specs=fixed2((blocks, half + norm.shape[0], width)),
        out_shape=jax.ShapeDtypeStruct((blocks, half + norm.shape[0], width), BF16),
        cost_estimate=pl.CostEstimate(
            flops=blocks * half * width, bytes_accessed=8 * blocks * half * width, transcendentals=0
        ),
        name="merge",
    )(keep, other, norm)


@functools.lru_cache
def strips(width, plane):
    near, owned = plane // 2, 3 * width // plane // STRIP
    side, pair = width // 2 // STRIP, PAIR // STRIP
    slots = []
    for core in range(2):
        slot, count = {}, [0, 0]
        for col in range(2 * near * owned):
            if col % (2 * side) // side == core:
                away = (col // owned % 2) ^ core
                slot[col] = (away, count[away])
                count[away] += 1
        assert count == [near * owned // 2] * 2
        slots.append(slot)
    stay = near * owned // 2
    to, found = [], []
    for core in range(2):
        order = [
            kind * 2 * side + core * side + p * pair + strip
            for p in range(side // pair)
            for kind in range(3)
            for strip in range(pair)
        ]
        to.append([slots[core][col][0] * stay + slots[core][col][1] for col in order])
        row = []
        for chip in range(near):
            for strip in range(owned):
                col = (2 * chip + core) * owned + strip
                row.append(slots[core][col][1] if col in slots[core] else stay + slots[1 - core][col][1])
        found.append(row)
    return to, found


def tiles_kernel(near, owned, chip_ref, found_ref, keep_ref, given_ref, *outs):
    step = pl.program_id(0)
    stay = keep_ref.shape[0] // STRIP
    for k in range(near):

        @pl.when(step == k)
        def _():
            for strip in range(owned):
                at = found_ref[(chip_ref[0] ^ k) * owned + strip]
                here = pl.multiple_of(jnp.minimum(at, stay - 1) * STRIP, STRIP)
                there = pl.multiple_of(jnp.maximum(at - stay, 0) * STRIP, STRIP)
                outs[k][strip * STRIP : (strip + 1) * STRIP, :] = jnp.where(
                    at < stay, keep_ref[pl.ds(here, STRIP), :], given_ref[pl.ds(there, STRIP), :]
                )


def qkv_tiles(chip, found, grad, given, near):
    size, width = given.shape
    owned = 2 * size // near // STRIP
    shape = (owned * STRIP, width)
    return pl.pallas_call(
        functools.partial(tiles_kernel, near, owned),
        grid_spec=pltpu.PrefetchScalarGridSpec(
            num_scalar_prefetch=2,
            grid=(near,),
            in_specs=[fixed2(given.shape), fixed2(given.shape)],
            out_specs=[fixed2(shape)] * near,
        ),
        out_shape=[jax.ShapeDtypeStruct(shape, BF16)] * near,
        cost_estimate=pl.CostEstimate(flops=size * width, bytes_accessed=size * width, transcendentals=0),
        name="qkv_tiles",
    )(chip, found, grad, given)


def gelu_pair(u):
    c = 0.7978845608028654
    square = u * u
    t = jnp.tanh(c * u * (1.0 + 0.044715 * square))
    half = 0.5 * (1.0 + t)
    slope = half + 0.5 * c * u * (1.0 - t * t) * (1.0 + 3.0 * 0.044715 * square)
    return u * half, slope


def norm_back(values, gain_vec, grad):
    average = jnp.mean(values, axis=-1, keepdims=True)
    centred = values - average
    spread = jnp.mean(centred * centred, axis=-1, keepdims=True)
    scale = lax.rsqrt(spread + norm_eps)
    unit = centred * scale
    scaled = grad * gain_vec
    back = scale * (
        scaled
        - jnp.mean(scaled, axis=-1, keepdims=True)
        - unit * jnp.mean(scaled * unit, axis=-1, keepdims=True)
    )
    return back, jnp.sum(grad * unit, axis=0, keepdims=True), jnp.sum(grad, axis=0, keepdims=True)


def ff_kernel(seqs, plane, *refs):
    me_ref, x_ref, att_ref, cot_ref, w_out_ref, gain_ref, shift_ref, up_ref, down_ref, *refs = refs
    out_ref, res_ref, *refs = refs
    ga_ref, norm_ref, gu_send, gu_keep, gd_send, gd_keep, gp_send, gp_keep, *refs = refs
    att_sc, residual_sc, normed_sc, normed_t, turned_sc, acc_out, acc_grad = refs
    step = pl.program_id(0)
    tokens, width = x_ref.shape
    rows = tokens // seqs
    block = width // plane
    near = plane // 2

    def turn(values):
        turned = values.T
        for j in range(plane):
            t = me_ref[0] ^ j
            slot = (1 - (t & 1)) * near + (t >> 1)
            at = pl.multiple_of(slot * block, block)
            turned_sc[pl.ds(at, block), :] = turned[j * block : (j + 1) * block]

    @pl.when(step == 0)
    def _():
        for seq in range(seqs):
            for core in range(2):
                cols = slice(core * width // 2, (core + 1) * width // 2)
                att_sc[seq * rows : (seq + 1) * rows, cols] = att_ref[seq * 2 + core]
        residual = x_ref[...].astype(F32) + jnp.dot(att_sc[...], w_out_ref[...], preferred_element_type=F32)
        residual_sc[...] = residual
        normed = norm_rows(residual, gain_ref[...], shift_ref[...]).astype(BF16)
        normed_sc[...] = normed
        normed_t[...] = normed.T
        turn(cot_ref[...])
        acc_out[...] = jnp.zeros_like(acc_out)
        acc_grad[...] = jnp.zeros_like(acc_grad)

    pre = jnp.dot(normed_sc[...], up_ref[...], preferred_element_type=F32)
    active, slope = gelu_pair(pre)
    active = active.astype(BF16)
    grad_pre = (dot(cot_ref[...], down_ref[...], (1, 1)) * slope).astype(BF16)
    acc_out[...] += jnp.dot(active, down_ref[...], preferred_element_type=F32)
    acc_grad[...] += dot(grad_pre, up_ref[...], (1, 1))
    grad_up = jnp.dot(normed_t[...], grad_pre, preferred_element_type=F32).astype(BF16)
    grad_down = jnp.dot(turned_sc[...], active, preferred_element_type=F32).astype(BF16)
    for slot in range(near):
        gd_send[slot, 0] = grad_down[slot * block : (slot + 1) * block]
        gd_keep[slot, 0] = grad_down[(near + slot) * block : (near + slot + 1) * block]

    @pl.when(step < near)
    def _():
        gu_send[0] = grad_up

    @pl.when(step >= near)
    def _():
        gu_keep[0] = grad_up

    @pl.when(step == plane - 1)
    def _():
        residual = residual_sc[...]
        out_ref[...] = (residual + acc_out[...]).astype(BF16)
        back, gain_grad, shift_grad = norm_back(residual, gain_ref[...], acc_grad[...])
        norm_ref[...] = jnp.zeros_like(norm_ref)
        norm_ref[2:3, :] = gain_grad
        norm_ref[3:4, :] = shift_grad
        grad_res = cot_ref[...].astype(F32) + back
        res_ref[...] = grad_res
        grad_z = grad_res.astype(BF16)
        grad_att = dot(grad_z, w_out_ref[...], (1, 1)).astype(BF16)
        for seq in range(seqs):
            for core in range(2):
                cols = slice(core * width // 2, (core + 1) * width // 2)
                ga_ref[seq * 2 + core] = grad_att[seq * rows : (seq + 1) * rows, cols]
        turn(grad_z)
        grad_proj = jnp.dot(turned_sc[...], att_sc[...], preferred_element_type=F32).astype(BF16)
        for slot in range(near):
            gp_send[slot] = grad_proj[slot * block : (slot + 1) * block]
            gp_keep[slot] = grad_proj[(near + slot) * block : (near + slot + 1) * block]


def feed_forward(me, x, attended, cotangent, w_out, gain, shift, w_up, w_down, plane):
    seqs, rows, width = x.shape
    hidden = w_up.shape[1]
    tokens, near, part, block = seqs * rows, plane // 2, hidden // plane, width // plane

    def at(i, me):
        return me[0] ^ (2 * (i % near) + jnp.where(i < near, 1, 0))

    def fixed(shape):
        return pl.BlockSpec(shape, lambda i, me, n=len(shape): (0,) * n)

    joined = attended.shape
    outs = [
        ((tokens, width), BF16, fixed((tokens, width))),
        ((tokens, width), F32, fixed((tokens, width))),
        (joined, BF16, fixed(joined)),
        ((8, width), F32, fixed((8, width))),
        ((near, width, part), BF16, pl.BlockSpec((1, width, part), lambda i, me: (jnp.minimum(i, near - 1), 0, 0))),
        ((near, width, part), BF16, pl.BlockSpec((1, width, part), lambda i, me: (jnp.maximum(i - near, 0), 0, 0))),
        *[
            (
                (near, plane, block, part),
                BF16,
                pl.BlockSpec((near, 1, block, part), lambda i, me: (0, at(i, me), 0, 0)),
            )
        ]
        * 2,
        *[((near, block, width), BF16, fixed((near, block, width)))] * 2,
    ]
    return pl.pallas_call(
        functools.partial(ff_kernel, seqs, plane),
        grid_spec=pltpu.PrefetchScalarGridSpec(
            num_scalar_prefetch=1,
            grid=(plane,),
            in_specs=[fixed((tokens, width))]
            + [fixed(joined), fixed((tokens, width)), fixed((width, width)), fixed((width,)), fixed((width,))]
            + [
                pl.BlockSpec((width, part), lambda i, me: (0, at(i, me))),
                pl.BlockSpec((part, width), lambda i, me: (at(i, me), 0)),
            ],
            out_specs=[o[2] for o in outs],
            scratch_shapes=[
                pltpu.VMEM((tokens, width), BF16),
                pltpu.VMEM((tokens, width), F32),
                pltpu.VMEM((tokens, width), BF16),
                pltpu.VMEM((width, tokens), BF16),
                pltpu.VMEM((width, tokens), BF16),
                pltpu.VMEM((tokens, width), F32),
                pltpu.VMEM((tokens, width), F32),
            ],
        ),
        out_shape=[jax.ShapeDtypeStruct(o[0], o[1]) for o in outs],
        cost_estimate=pl.CostEstimate(
            flops=12 * tokens * width * hidden + 6 * tokens * width * width,
            bytes_accessed=8 * width * hidden,
            transcendentals=tokens * hidden,
        ),
        name="feed_forward",
    )(
        me,
        x.reshape(tokens, width),
        attended,
        cotangent.reshape(tokens, width),
        w_out,
        gain,
        shift,
        w_up,
        w_down,
    )


def first_norm_kernel(seqs, x_ref, gain_ref, grad_ref, res_ref, out_ref, norm_ref):
    half = x_ref.shape[0] // seqs // 2
    for piece in range(2 * seqs):
        at = slice(piece * half, (piece + 1) * half)
        values = x_ref[at].astype(F32)
        centred = values - jnp.mean(values, axis=-1, keepdims=True)
        scale = lax.rsqrt(jnp.mean(centred * centred, axis=-1, keepdims=True) + norm_eps)
        unit = centred * scale
        scaled = grad_ref[piece, :half].astype(F32) * gain_ref[...]
        back = scale * (
            scaled
            - jnp.mean(scaled, axis=-1, keepdims=True)
            - unit * jnp.mean(scaled * unit, axis=-1, keepdims=True)
        )
        out_ref[at] = (res_ref[at] + back).astype(BF16)
    norms = grad_ref[0, half:, :PAIR].astype(F32)
    for piece in range(1, 2 * seqs):
        norms = norms + grad_ref[piece, half:, :PAIR].astype(F32)
    norm_ref[...] = norms


def first_norm_back(x, gain, grad, grad_res):
    seqs, rows, width = x.shape
    tokens = seqs * rows
    return pl.pallas_call(
        functools.partial(first_norm_kernel, seqs),
        grid=(1,),
        in_specs=[fixed2((tokens, width)), fixed2((width,)), fixed2(grad.shape), fixed2((tokens, width))],
        out_specs=[fixed2((tokens, width)), fixed2((8, PAIR))],
        out_shape=[jax.ShapeDtypeStruct((tokens, width), BF16), jax.ShapeDtypeStruct((8, PAIR), F32)],
        cost_estimate=pl.CostEstimate(flops=20 * tokens * width, bytes_accessed=12 * tokens * width, transcendentals=0),
        name="first_norm_back",
    )(x.reshape(tokens, width), gain, grad, grad_res)


def exchange(blocks):
    return lax.all_to_all(blocks, ("pb", "ka"), 0, 0, tiled=True)


def swap(values, axes, size, bit):
    return lax.ppermute(values, axes, [(i, i ^ bit) for i in range(size)])


def add_pair_kernel(near, batch, *refs):
    _, up_a, up_b, down_a, down_b, proj_a, proj_b, *outs = refs
    outs, down_outs = outs[:near], outs[near:]
    step = pl.program_id(0)
    part = outs[0].shape[1]

    def both(a, b):
        return (a.astype(F32) + b.astype(F32)).astype(BF16)

    @pl.when(step < batch)
    def _():
        for k in range(near):
            outs[k][...] = both(up_a[k], up_b[k])

    for far in range(batch):

        @pl.when(step == batch + far)
        def _():
            for k in range(near):
                total = both(down_a[k], down_b[k])
                slab = total.shape[0] * total.shape[1]
                target, at = down_outs[far in (1, 2)], (far > 1) * near * slab + k * slab
                target[at : at + slab] = total.reshape(slab, part)

    @pl.when(step == 2 * batch)
    def _():
        for k in range(near):
            total = both(proj_a[k], proj_b[k])
            outs[k][...] = jnp.concatenate([total[:, :part], total[:, part:]], axis=0)


def add_pair(mine, up, down, proj, batch):
    near, width, part = up[0].shape
    plane, block = down[0].shape[1:3]
    tall, few = width // batch, plane // batch
    up_spec = pl.BlockSpec((near, tall, part), lambda i, m: (0, jnp.minimum(i, batch - 1), 0))
    down_spec = pl.BlockSpec(
        (near, few, block, part), lambda i, m: (0, m[0] ^ jnp.clip(i - batch, 0, batch - 1), 0, 0)
    )
    proj_spec = pl.BlockSpec((near, block, width), lambda i, m: (0, 0, 0))
    last = lambda i, m: (jnp.where(i < batch, i, jnp.where(i < 2 * batch, batch - 1, batch)), 0)
    down_shape = (2 * near * few * block, part)
    return pl.pallas_call(
        functools.partial(add_pair_kernel, near, batch),
        grid_spec=pltpu.PrefetchScalarGridSpec(
            num_scalar_prefetch=1,
            grid=(2 * batch + 1,),
            in_specs=[up_spec] * 2 + [down_spec] * 2 + [proj_spec] * 2,
            out_specs=[pl.BlockSpec((tall, part), last)] * near
            + [pl.BlockSpec(down_shape, lambda i, m: (0, 0))] * 2,
        ),
        out_shape=[jax.ShapeDtypeStruct((width + tall, part), BF16)] * near
        + [jax.ShapeDtypeStruct(down_shape, BF16)] * 2,
        cost_estimate=pl.CostEstimate(
            flops=near * 9 * tall * part, bytes_accessed=6 * near * 9 * tall * part, transcendentals=0
        ),
        name="add_pair",
    )(mine, *up, *down, *proj)


def add_all(parts):
    total = parts[0].astype(F32)
    for p in parts[1:]:
        total = total + p.astype(F32)
    return total


def over_batch(stacked):
    size = lax.axis_size("batch")
    mine = lax.axis_index("batch")
    if size > 4:
        return lax.psum_scatter(stacked, "batch", scatter_dimension=0, tiled=True)[0].astype(F32)
    parts = [lax.dynamic_index_in_dim(stacked, mine, 0, False)]
    for bit in range(1, size):
        block = lax.dynamic_index_in_dim(stacked, mine ^ bit, 0, False)
        parts.append(swap(block, "batch", size, bit))
    return add_all(parts)


def over_plane(tiles, plane):
    parts = [tiles[0]]
    for k in range(1, len(tiles)):
        parts.append(swap(tiles[k], ("pb", "ka"), plane, 2 * k))
    return add_all(parts)


def shards(
    inputs,
    block_place,
    ln1_gain,
    ln1_shift,
    w_qkv,
    w_out,
    ln2_gain,
    ln2_shift,
    w_up,
    w_down,
    cotangent,
):
    seqs, rows, width = inputs.shape
    hidden = w_up.shape[1]
    plane = lax.axis_size("pb") * lax.axis_size("ka")
    planes = ("pb", "ka")
    batch = lax.axis_size("batch")
    near = plane // 2
    few = batch == 4
    me = lax.axis_index(planes)
    scalar = lambda value: value.astype(jnp.int32).reshape(1)
    core, chip = scalar(me & 1), scalar(me >> 1)
    part, block, slab = hidden // plane, width // plane, width // batch
    place = lax.dynamic_index_in_dim(block_place, me >> 1, 0, False)
    to, found = [], []
    for core in range(2):
        order = [
            kind * 2 * side + core * side + p * pair + strip
            for p in range(side // pair)
            for kind in range(3)
            for strip in range(pair)
        ]
        to.append([slots[core][col][0] * stay + slots[core][col][1] for col in order])
        row = []
        for chip in range(near):
            for strip in range(owned):
                col = (2 * chip + core) * owned + strip
                row.append(slots[core][col][1] if col in slots[core] else stay + slots[1 - core][col][1])
        found.append(row)
    return to, found


def tiles_kernel(near, owned, chip_ref, found_ref, keep_ref, given_ref, *outs):
    step = pl.program_id(0)
    stay = keep_ref.shape[0] // STRIP
    for k in range(near):

        @pl.when(step == k)
        def _():
            for strip in range(owned):
                at = found_ref[(chip_ref[0] ^ k) * owned + strip]
                here = pl.multiple_of(jnp.minimum(at, stay - 1) * STRIP, STRIP)
                there = pl.multiple_of(jnp.maximum(at - stay, 0) * STRIP, STRIP)
                outs[k][strip * STRIP : (strip + 1) * STRIP, :] = jnp.where(
                    at < stay, keep_ref[pl.ds(here, STRIP), :], given_ref[pl.ds(there, STRIP), :]
                )


def qkv_tiles(chip, found, grad, given, near):
    size, width = given.shape
    owned = 2 * size // near // STRIP
    shape = (owned * STRIP, width)
    return pl.pallas_call(
        functools.partial(tiles_kernel, near, owned),
        grid_spec=pltpu.PrefetchScalarGridSpec(
            num_scalar_prefetch=2,
            grid=(near,),
            in_specs=[fixed2(given.shape), fixed2(given.shape)],
            out_specs=[fixed2(shape)] * near,
        ),
        out_shape=[jax.ShapeDtypeStruct(shape, BF16)] * near,
        cost_estimate=pl.CostEstimate(flops=size * width, bytes_accessed=size * width, transcendentals=0),
        name="qkv_tiles",
    )(chip, found, grad, given)


def gelu_pair(u):
    c = 0.7978845608028654
    square = u * u
    t = jnp.tanh(c * u * (1.0 + 0.044715 * square))
    half = 0.5 * (1.0 + t)
    slope = half + 0.5 * c * u * (1.0 - t * t) * (1.0 + 3.0 * 0.044715 * square)
    return u * half, slope


def norm_back(values, gain_vec, grad):
    average = jnp.mean(values, axis=-1, keepdims=True)
    centred = values - average
    spread = jnp.mean(centred * centred, axis=-1, keepdims=True)
    scale = lax.rsqrt(spread + norm_eps)
    unit = centred * scale
    scaled = grad * gain_vec
    back = scale * (
        scaled
        - jnp.mean(scaled, axis=-1, keepdims=True)
        - unit * jnp.mean(scaled * unit, axis=-1, keepdims=True)
    )
    return back, jnp.sum(grad * unit, axis=0, keepdims=True), jnp.sum(grad, axis=0, keepdims=True)


def ff_kernel(seqs, plane, *refs):
    me_ref, x_ref, att_ref, cot_ref, w_out_ref, gain_ref, shift_ref, up_ref, down_ref, *refs = refs
    out_ref, res_ref, *refs = refs
    ga_ref, norm_ref, gu_send, gu_keep, gd_send, gd_keep, gp_send, gp_keep, *refs = refs
    att_sc, residual_sc, normed_sc, normed_t, turned_sc, acc_out, acc_grad = refs
    step = pl.program_id(0)
    tokens, width = x_ref.shape
    rows = tokens // seqs
    block = width // plane
    near = plane // 2

    def turn(values):
        turned = values.T
        for j in range(plane):
            t = me_ref[0] ^ j
            slot = (1 - (t & 1)) * near + (t >> 1)
            at = pl.multiple_of(slot * block, block)
            turned_sc[pl.ds(at, block), :] = turned[j * block : (j + 1) * block]

    @pl.when(step == 0)
    def _():
        for seq in range(seqs):
            for core in range(2):
                cols = slice(core * width // 2, (core + 1) * width // 2)
                att_sc[seq * rows : (seq + 1) * rows, cols] = att_ref[seq * 2 + core]
        residual = x_ref[...].astype(F32) + jnp.dot(att_sc[...], w_out_ref[...], preferred_element_type=F32)
        residual_sc[...] = residual
        normed = norm_rows(residual, gain_ref[...], shift_ref[...]).astype(BF16)
        normed_sc[...] = normed
        normed_t[...] = normed.T
        turn(cot_ref[...])
        acc_out[...] = jnp.zeros_like(acc_out)
        acc_grad[...] = jnp.zeros_like(acc_grad)

    pre = jnp.dot(normed_sc[...], up_ref[...], preferred_element_type=F32)
    active, slope = gelu_pair(pre)
    active = active.astype(BF16)
    grad_pre = (dot(cot_ref[...], down_ref[...], (1, 1)) * slope).astype(BF16)
    acc_out[...] += jnp.dot(active, down_ref[...], preferred_element_type=F32)
    acc_grad[...] += dot(grad_pre, up_ref[...], (1, 1))
    grad_up = jnp.dot(normed_t[...], grad_pre, preferred_element_type=F32).astype(BF16)
    grad_down = jnp.dot(turned_sc[...], active, preferred_element_type=F32).astype(BF16)
    for slot in range(near):
        gd_send[slot, 0] = grad_down[slot * block : (slot + 1) * block]
        gd_keep[slot, 0] = grad_down[(near + slot) * block : (near + slot + 1) * block]

    @pl.when(step < near)
    def _():
        gu_send[0] = grad_up

    @pl.when(step >= near)
    def _():
        gu_keep[0] = grad_up

    @pl.when(step == plane - 1)
    def _():
        residual = residual_sc[...]
        out_ref[...] = (residual + acc_out[...]).astype(BF16)
        back, gain_grad, shift_grad = norm_back(residual, gain_ref[...], acc_grad[...])
        norm_ref[...] = jnp.zeros_like(norm_ref)
        norm_ref[2:3, :] = gain_grad
        norm_ref[3:4, :] = shift_grad
        grad_res = cot_ref[...].astype(F32) + back
        res_ref[...] = grad_res
        grad_z = grad_res.astype(BF16)
        grad_att = dot(grad_z, w_out_ref[...], (1, 1)).astype(BF16)
        for seq in range(seqs):
            for core in range(2):
                cols = slice(core * width // 2, (core + 1) * width // 2)
                ga_ref[seq * 2 + core] = grad_att[seq * rows : (seq + 1) * rows, cols]
        turn(grad_z)
        grad_proj = jnp.dot(turned_sc[...], att_sc[...], preferred_element_type=F32).astype(BF16)
        for slot in range(near):
            gp_send[slot] = grad_proj[slot * block : (slot + 1) * block]
            gp_keep[slot] = grad_proj[(near + slot) * block : (near + slot + 1) * block]


def feed_forward(me, x, attended, cotangent, w_out, gain, shift, w_up, w_down, plane):
    seqs, rows, width = x.shape
    hidden = w_up.shape[1]
    tokens, near, part, block = seqs * rows, plane // 2, hidden // plane, width // plane

    def at(i, me):
        return me[0] ^ (2 * (i % near) + jnp.where(i < near, 1, 0))

    def fixed(shape):
        return pl.BlockSpec(shape, lambda i, me, n=len(shape): (0,) * n)

    joined = attended.shape
    outs = [
        ((tokens, width), BF16, fixed((tokens, width))),
        ((tokens, width), F32, fixed((tokens, width))),
        (joined, BF16, fixed(joined)),
        ((8, width), F32, fixed((8, width))),
        ((near, width, part), BF16, pl.BlockSpec((1, width, part), lambda i, me: (jnp.minimum(i, near - 1), 0, 0))),
        ((near, width, part), BF16, pl.BlockSpec((1, width, part), lambda i, me: (jnp.maximum(i - near, 0), 0, 0))),
        *[
            (
                (near, plane, block, part),
                BF16,
                pl.BlockSpec((near, 1, block, part), lambda i, me: (0, at(i, me), 0, 0)),
            )
        ]
        * 2,
        *[((near, block, width), BF16, fixed((near, block, width)))] * 2,
    ]
    return pl.pallas_call(
        functools.partial(ff_kernel, seqs, plane),
        grid_spec=pltpu.PrefetchScalarGridSpec(
            num_scalar_prefetch=1,
            grid=(plane,),
            in_specs=[fixed((tokens, width))]
            + [fixed(joined), fixed((tokens, width)), fixed((width, width)), fixed((width,)), fixed((width,))]
            + [
                pl.BlockSpec((width, part), lambda i, me: (0, at(i, me))),
                pl.BlockSpec((part, width), lambda i, me: (at(i, me), 0)),
            ],
            out_specs=[o[2] for o in outs],
            scratch_shapes=[
                pltpu.VMEM((tokens, width), BF16),
                pltpu.VMEM((tokens, width), F32),
                pltpu.VMEM((tokens, width), BF16),
                pltpu.VMEM((width, tokens), BF16),
                pltpu.VMEM((width, tokens), BF16),
                pltpu.VMEM((tokens, width), F32),
                pltpu.VMEM((tokens, width), F32),
            ],
        ),
        out_shape=[jax.ShapeDtypeStruct(o[0], o[1]) for o in outs],
        cost_estimate=pl.CostEstimate(
            flops=12 * tokens * width * hidden + 6 * tokens * width * width,
            bytes_accessed=8 * width * hidden,
            transcendentals=tokens * hidden,
        ),
        name="feed_forward",
    )(
        me,
        x.reshape(tokens, width),
        attended,
        cotangent.reshape(tokens, width),
        w_out,
        gain,
        shift,
        w_up,
        w_down,
    )


def first_norm_kernel(seqs, x_ref, gain_ref, grad_ref, res_ref, out_ref, norm_ref):
    half = x_ref.shape[0] // seqs // 2
    for piece in range(2 * seqs):
        at = slice(piece * half, (piece + 1) * half)
        values = x_ref[at].astype(F32)
        centred = values - jnp.mean(values, axis=-1, keepdims=True)
        scale = lax.rsqrt(jnp.mean(centred * centred, axis=-1, keepdims=True) + norm_eps)
        unit = centred * scale
        scaled = grad_ref[piece, :half].astype(F32) * gain_ref[...]
        back = scale * (
            scaled
            - jnp.mean(scaled, axis=-1, keepdims=True)
            - unit * jnp.mean(scaled * unit, axis=-1, keepdims=True)
        )
        out_ref[at] = (res_ref[at] + back).astype(BF16)
    norms = grad_ref[0, half:, :PAIR].astype(F32)
    for piece in range(1, 2 * seqs):
        norms = norms + grad_ref[piece, half:, :PAIR].astype(F32)
    norm_ref[...] = norms


def first_norm_back(x, gain, grad, grad_res):
    seqs, rows, width = x.shape
    tokens = seqs * rows
    return pl.pallas_call(
        functools.partial(first_norm_kernel, seqs),
        grid=(1,),
        in_specs=[fixed2((tokens, width)), fixed2((width,)), fixed2(grad.shape), fixed2((tokens, width))],
        out_specs=[fixed2((tokens, width)), fixed2((8, PAIR))],
        out_shape=[jax.ShapeDtypeStruct((tokens, width), BF16), jax.ShapeDtypeStruct((8, PAIR), F32)],
        cost_estimate=pl.CostEstimate(flops=20 * tokens * width, bytes_accessed=12 * tokens * width, transcendentals=0),
        name="first_norm_back",
    )(x.reshape(tokens, width), gain, grad, grad_res)


def exchange(blocks):
    return lax.all_to_all(blocks, ("pb", "ka"), 0, 0, tiled=True)


def swap(values, axes, size, bit):
    return lax.ppermute(values, axes, [(i, i ^ bit) for i in range(size)])


def add_pair_kernel(near, batch, *refs):
    _, up_a, up_b, down_a, down_b, proj_a, proj_b, *outs = refs
    outs, down_outs = outs[:near], outs[near:]
    step = pl.program_id(0)
    part = outs[0].shape[1]

    def both(a, b):
        return (a.astype(F32) + b.astype(F32)).astype(BF16)

    @pl.when(step < batch)
    def _():
        for k in range(near):
            outs[k][...] = both(up_a[k], up_b[k])

    for far in range(batch):

        @pl.when(step == batch + far)
        def _():
            for k in range(near):
                total = both(down_a[k], down_b[k])
                slab = total.shape[0] * total.shape[1]
                target, at = down_outs[far in (1, 2)], (far > 1) * near * slab + k * slab
                target[at : at + slab] = total.reshape(slab, part)

    @pl.when(step == 2 * batch)
    def _():
        for k in range(near):
            total = both(proj_a[k], proj_b[k])
            outs[k][...] = jnp.concatenate([total[:, :part], total[:, part:]], axis=0)


def add_pair(mine, up, down, proj, batch):
    near, width, part = up[0].shape
    plane, block = down[0].shape[1:3]
    tall, few = width // batch, plane // batch
    up_spec = pl.BlockSpec((near, tall, part), lambda i, m: (0, jnp.minimum(i, batch - 1), 0))
    down_spec = pl.BlockSpec(
        (near, few, block, part), lambda i, m: (0, m[0] ^ jnp.clip(i - batch, 0, batch - 1), 0, 0)
    )
    proj_spec = pl.BlockSpec((near, block, width), lambda i, m: (0, 0, 0))
    last = lambda i, m: (jnp.where(i < batch, i, jnp.where(i < 2 * batch, batch - 1, batch)), 0)
    down_shape = (2 * near * few * block, part)
    return pl.pallas_call(
        functools.partial(add_pair_kernel, near, batch),
        grid_spec=pltpu.PrefetchScalarGridSpec(
            num_scalar_prefetch=1,
            grid=(2 * batch + 1,),
            in_specs=[up_spec] * 2 + [down_spec] * 2 + [proj_spec] * 2,
            out_specs=[pl.BlockSpec((tall, part), last)] * near
            + [pl.BlockSpec(down_shape, lambda i, m: (0, 0))] * 2,
        ),
        out_shape=[jax.ShapeDtypeStruct((width + tall, part), BF16)] * near
        + [jax.ShapeDtypeStruct(down_shape, BF16)] * 2,
        cost_estimate=pl.CostEstimate(
            flops=near * 9 * tall * part, bytes_accessed=6 * near * 9 * tall * part, transcendentals=0
        ),
        name="add_pair",
    )(mine, *up, *down, *proj)


def add_all(parts):
    total = parts[0].astype(F32)
    for p in parts[1:]:
        total = total + p.astype(F32)
    return total


def over_batch(stacked):
    size = lax.axis_size("batch")
    mine = lax.axis_index("batch")
    if size > 4:
        return lax.psum_scatter(stacked, "batch", scatter_dimension=0, tiled=True)[0].astype(F32)
    parts = [lax.dynamic_index_in_dim(stacked, mine, 0, False)]
    for bit in range(1, size):
        block = lax.dynamic_index_in_dim(stacked, mine ^ bit, 0, False)
        parts.append(swap(block, "batch", size, bit))
    return add_all(parts)


def over_plane(tiles, plane):
    parts = [tiles[0]]
    for k in range(1, len(tiles)):
        parts.append(swap(tiles[k], ("pb", "ka"), plane, 2 * k))
    return add_all(parts)


def shards(
    inputs,
    block_place,
    ln1_gain,
    ln1_shift,
    w_qkv,
    w_out,
    ln2_gain,
    ln2_shift,
    w_up,
    w_down,
    cotangent,
):
    seqs, rows, width = inputs.shape
    hidden = w_up.shape[1]
    plane = lax.axis_size("pb") * lax.axis_size("ka")
    planes = ("pb", "ka")
    batch = lax.axis_size("batch")
    near = plane // 2
    few = batch == 4
    me = lax.axis_index(planes)
    scalar = lambda value: value.astype(jnp.int32).reshape(1)
    core, chip = scalar(me & 1), scalar(me >> 1)
    part, block, slab = hidden // plane, width // plane, width // batch
    place = lax.dynamic_index_in_dim(block_place, me >> 1, 0, False)
    spots = jnp.arange(plane, dtype=jnp.int32)
    back = jnp.sum(jnp.where(place[None] == spots[:, None], spots[None], 0), axis=1)
    to, found = [jnp.where(core == 0, *(jnp.array(t, jnp.int32) for t in both)) for both in strips(width, plane)]

    mine = exchange(inputs.reshape(plane, seqs * rows // plane, width))
    other = swap(mine, planes, plane, 1)
    attended, normed1, packed, sums, stats = attend(core, place, mine, other, ln1_gain, ln1_shift, w_qkv)
    outputs, grad_res, grad_att, norm2, *grads = feed_forward(
        scalar(me), inputs, exchange(attended), cotangent, w_out, ln2_gain, ln2_shift, w_up, w_down, plane
    )
    grad_att = exchange(grad_att)
    up, down, proj = [(grads[2 * i + 1], swap(grads[2 * i], planes, plane, 1)) for i in range(3)]
    if few:
        sums_up = add_pair(scalar(lax.axis_index("batch")), up, down, proj, batch)
        grad_att, sums_up = lax.optimization_barrier((grad_att, sums_up))
        tiles, down = sums_up[:near], sums_up[near:]
    else:
        tiles = [
            jnp.concatenate(
                [add_all([t[k] for t in up])]
                + [add_all([t[k] for t in down]).reshape(width, part)]
                + [add_all([t[k] for t in proj]).reshape(block, 2, part).transpose(1, 0, 2).reshape(2 * block, part)]
            ).astype(BF16)
            for k in range(near)
        ]
    tile = over_plane(tiles, plane).astype(BF16)
    if few:
        down = add_all([down[0], swap(down[1], "batch", batch, 1)]).astype(BF16)

    grad_qkv, keep, send, norm = attend_back(
        core, place, to, packed, grad_att, sums, stats, normed1, mine, other, norm2, w_qkv
    )
    given = swap(grad_qkv[grad_qkv.shape[0] // 2 :], planes, plane, 1)
    if few:
        given, tile, down = lax.optimization_barrier((given, tile, down))
        down = jnp.split(down, 2)
        down[1] = swap(down[1], "batch", batch, 3)
    late = qkv_tiles(chip, found, grad_qkv, given, near)
    keep, late = lax.optimization_barrier((keep, late))
    returned = exchange(merge(keep, swap(send, planes, plane, 1), norm))
    if few:
        returned, down = lax.optimization_barrier((returned, add_all(down).astype(BF16)))
        grad_down = over_plane(jnp.split(down, near), plane)
    else:
        cut = batch // plane
        down_tile = tile[width : 2 * width].reshape(plane, block, cut, part // cut).transpose(0, 2, 1, 3)
        grad_down = over_batch(down_tile.reshape(batch, block, part // cut))
    grad_down = grad_down.reshape(-1, block, min(part, hidden // batch)).transpose(0, 2, 1).reshape(-1, block)

    proj_tile = tile[-2 * block :].reshape(2, block, part).transpose(1, 0, 2).reshape(block, batch, slab)
    proj_tile = proj_tile.transpose(1, 0, 2)
    up_tile = tile[:width].reshape(batch, slab, part)
    owned = 3 * width // plane
    qkv_tile = over_plane(late, plane).astype(BF16).reshape(owned, batch, slab).transpose(1, 0, 2)
    grad_inputs, norms = first_norm_back(inputs, ln1_gain, returned, grad_res)
    if few:
        joined = [t.reshape(batch, -1, part) for t in (up_tile, proj_tile, qkv_tile)]
        summed = over_batch(jnp.concatenate(joined, axis=1))
        grad_up, grad_proj, grad_qkv = jnp.split(summed, (slab, slab + block * slab // part))
        grad_proj, grad_qkv = grad_proj.reshape(block, slab), grad_qkv.reshape(owned, slab)
        for bit in (1, 2):
            norms = norms + swap(norms, "batch", batch, bit)
    else:
        grad_up, grad_proj, grad_qkv = over_batch(up_tile), over_batch(proj_tile), over_batch(qkv_tile)
        norms = lax.psum(norms, "batch")
    grad_proj = grad_proj.T
    return (
        outputs.reshape(inputs.shape),
        grad_inputs.reshape(inputs.shape),
        grad_qkv.T,
        grad_proj,
        grad_up,
        grad_down,
        norms[:4, :block],
    )


def solution(mesh):
    placed = (
        P("batch", ("pb", "ka"), None),
        P("batch", None),
        P(),
        P(),
        P(),
        P(),
        P(),
        P(),
        P(),
        P(),
        P("batch", ("pb", "ka"), None),
    )
    return jax.shard_map(
        shards,
        mesh=mesh,
        in_specs=placed,
        out_specs=(
            P("batch", ("pb", "ka"), None),
            P("batch", ("pb", "ka"), None),
            P("batch", ("pb", "ka")),
            P("batch", ("pb", "ka")),
            P("batch", ("pb", "ka")),
            P("batch", ("pb", "ka")),
            P(None, ("pb", "ka")),
        ),
        check_vma=False,
    )
```

```python
import functools

import jax
import jax.numpy as jnp
from jax import lax
from jax.experimental import pallas as pl
from jax.experimental.pallas import tpu as pltpu
from jax.sharding import PartitionSpec as P

HEADS = 12
HEAD = 64
PAIR = 2 * HEAD
QTILE = 256
STRIP = 32
SCALE = HEAD ** (-0.5)
HUGE = 3e38
HIDDEN = -1e30

norm_eps = 1e-05
BF16 = jnp.bfloat16
F32 = jnp.float32


def norm_rows(values, gain_vec, shift_vec):
    average = jnp.mean(values, axis=-1, keepdims=True)
    centred = values - average
    spread = jnp.mean(centred * centred, axis=-1, keepdims=True)
    return centred * lax.rsqrt(spread + norm_eps) * gain_vec + shift_vec


def gelu_tanh(values):
    return jax.nn.gelu(values, approximate=True)


def dot(a, b, contract):
    return lax.dot_general(a, b, ((contract[:1], contract[1:]), ((), ())), preferred_element_type=F32)


def head_lanes(values, head):
    lane = lax.broadcasted_iota(jnp.int32, values.shape, 1)
    mine = lane < HEAD if head == 0 else lane >= HEAD
    return jnp.where(mine, values, jnp.zeros_like(values))


def hide_later(magnitude):
    keys = magnitude.shape[0]
    key = lax.broadcasted_iota(jnp.int32, (QTILE, QTILE), 0)
    query = lax.broadcasted_iota(jnp.int32, (QTILE, QTILE), 1)
    last = jnp.where(key <= query, magnitude[keys - QTILE :], HIDDEN)
    return last if keys == QTILE else jnp.concatenate([magnitude[: keys - QTILE], last], axis=0)


def sign_of(scores):
    return jnp.clip(scores * HUGE, -1.0, 1.0)


def attend_kernel(
    core_ref, place_ref, mine_ref, other_ref, gain_ref, shift_ref, wq_ref, wk_ref, wv_ref,
    out_ref, normed_ref, qkv_ref, sums_ref, stats_ref, o_sc,
):
    blocks, half = mine_ref.shape[0], mine_ref.shape[1]
    rows = 2 * half
    total_rows = normed_ref.shape[0]

    @pl.when(pl.program_id(0) == 0)
    def _():
        @pl.loop(0, blocks)
        def _(block):
            for ref, part in ((mine_ref, core_ref[0]), (other_ref, 1 - core_ref[0])):
                at = pl.multiple_of(place_ref[block] * rows + part * half, half)
                normed = norm_rows(ref[block].astype(F32), gain_ref[...], shift_ref[...])
                normed_ref[pl.ds(at, half), :] = normed.astype(BF16)

    weights = jnp.concatenate([wq_ref[...], wk_ref[...], wv_ref[...]], axis=1)
    qkv_ref[0] = jnp.dot(normed_ref[...], weights, preferred_element_type=F32).astype(BF16)
    v_t = qkv_ref[0, :, 2 * PAIR :].T
    for tile in range(total_rows // QTILE):
        span = slice(tile * QTILE, (tile + 1) * QTILE)
        keys = (tile + 1) * QTILE
        queries = qkv_ref[0, span, :PAIR] * SCALE
        for head in range(2):
            scores = dot(qkv_ref[0, :keys, PAIR : 2 * PAIR], head_lanes(queries, head).astype(BF16), (1, 1))
            magnitude = hide_later(jnp.abs(scores))
            peak = jnp.max(magnitude, axis=0, keepdims=True)
            exponents = jnp.exp(magnitude - peak)
            total = jnp.sum(exponents, axis=0, keepdims=True)
            weights = (exponents * sign_of(scores)).astype(BF16)
            summed = dot(v_t[head * HEAD : (head + 1) * HEAD, :keys], weights, (1, 0))
            sums_ref[0, head * HEAD : (head + 1) * HEAD, span] = summed / total
            stats_ref[0, head : head + 1, span] = peak + jnp.log(total)
        o_sc[span, :] = sums_ref[0, :, span].T
    for block in range(blocks):
        at = pl.multiple_of(place_ref[block] * rows, rows)
        out_ref[block] = o_sc[pl.ds(at, rows), :].astype(BF16)


def columns_of(width, size, kind, pairs):
    return pl.BlockSpec(
        (width, size), lambda i, core, place: (0, kind * (width // size) + core[0] * pairs + jnp.minimum(i, pairs - 1))
    )


def fixed2(shape):
    return pl.BlockSpec(shape, lambda i, *scalars, n=len(shape): (0,) * n)


def attend(core, place, mine, other, gain, shift, w_qkv):
    blocks, half, width = mine.shape
    length, pairs = 2 * half * blocks, width // PAIR // 2
    area = length * length
    return pl.pallas_call(
        attend_kernel,
        grid_spec=pltpu.PrefetchScalarGridSpec(
            num_scalar_prefetch=2,
            grid=(pairs,),
            in_specs=[fixed2(mine.shape), fixed2(mine.shape), fixed2((width,)), fixed2((width,))]
            + [columns_of(width, PAIR, kind, pairs) for kind in range(3)],
            out_specs=[
                pl.BlockSpec((blocks, 2 * half, PAIR), lambda i, c, p: (0, 0, i)),
                fixed2((length, width)),
                pl.BlockSpec((1, length, 3 * PAIR), lambda i, c, p: (i, 0, 0)),
                pl.BlockSpec((1, PAIR, length), lambda i, c, p: (i, 0, 0)),
                pl.BlockSpec((1, 8, length), lambda i, c, p: (i, 0, 0)),
            ],
            scratch_shapes=[pltpu.VMEM((length, PAIR), F32)],
        ),
        out_shape=[
            jax.ShapeDtypeStruct((blocks, 2 * half, pairs * PAIR), BF16),
            jax.ShapeDtypeStruct((length, width), BF16),
            jax.ShapeDtypeStruct((pairs, length, 3 * PAIR), BF16),
            jax.ShapeDtypeStruct((pairs, PAIR, length), F32),
            jax.ShapeDtypeStruct((pairs, 8, length), F32),
        ],
        cost_estimate=pl.CostEstimate(
            flops=pairs * 16 * area * HEAD + 3 * length * width * width,
            bytes_accessed=8 * length * width,
            transcendentals=pairs * area,
        ),
        name="attend",
    )(core, place, mine, other, gain, shift, w_qkv, w_qkv, w_qkv)


def attend_back_kernel(
    core_ref, place_ref, to_ref, qkv_ref, g_ref, sums_ref, stats_ref, normed_ref, mine_ref, other_ref, norm_ref,
    wq_ref, wk_ref, wv_ref, gq_ref, keep_ref, send_ref, norms_ref, g_sc, dq_sc, dk_sc, dv_sc, packed_sc, back_sc,
):
    blocks, rows = g_ref.shape[0], g_ref.shape[1]
    for block in range(blocks):
        at = pl.multiple_of(place_ref[block] * rows, rows)
        g_sc[pl.ds(at, rows), :] = g_ref[block]
    total_rows = g_sc.shape[0]
    k_t = qkv_ref[0, :, PAIR : 2 * PAIR].T
    g_t = g_sc[...].astype(F32).T
    products = g_t * sums_ref[0]
    deltas = [
        jnp.sum(products[head * HEAD : (head + 1) * HEAD], axis=0, keepdims=True) for head in range(2)
    ]
    dk_sc[...] = jnp.zeros_like(dk_sc)
    dv_sc[...] = jnp.zeros_like(dv_sc)
    for tile in range(total_rows // QTILE):
        span = slice(tile * QTILE, (tile + 1) * QTILE)
        keys = (tile + 1) * QTILE
        queries = qkv_ref[0, span, :PAIR] * SCALE
        parts = []
        for head in range(2):
            q_head = head_lanes(queries, head).astype(BF16)
            g_head = head_lanes(g_sc[span, :], head)
            scores = dot(qkv_ref[0, :keys, PAIR : 2 * PAIR], q_head, (1, 1))
            magnitude = hide_later(jnp.abs(scores))
            sign = sign_of(scores)
            signed = jnp.exp(magnitude - stats_ref[0, head : head + 1, span]) * sign
            grad_weights = dot(qkv_ref[0, :keys, 2 * PAIR :], g_head, (1, 1))
            grad_scores = (signed * (sign * grad_weights - deltas[head][:, span])).astype(BF16)
            dv_sc[:keys, :] += dot(signed.astype(BF16), g_head, (1, 0))
            dk_sc[:keys, :] += dot(grad_scores, q_head, (1, 0))
            parts.append(dot(k_t[head * HEAD : (head + 1) * HEAD, :keys], grad_scores, (1, 0)))
        dq_sc[span, :] = jnp.concatenate(parts, axis=0).T * SCALE
    for kind, ref in enumerate((dq_sc, dk_sc, dv_sc)):
        grad = ref[...].astype(BF16)
        packed_sc[:, kind * PAIR : (kind + 1) * PAIR] = grad
        turned = jnp.dot(grad.T, normed_ref[...], preferred_element_type=F32).astype(BF16)
        for strip in range(PAIR // STRIP):
            at = to_ref[(pl.program_id(0) * 3 + kind) * (PAIR // STRIP) + strip]
            at = pl.multiple_of(at * STRIP, STRIP)
            gq_ref[pl.ds(at, STRIP), :] = turned[strip * STRIP : (strip + 1) * STRIP]

    step, half = pl.program_id(0), mine_ref.shape[1]
    weights = jnp.concatenate([wq_ref[...], wk_ref[...], wv_ref[...]], axis=1)
    back = dot(packed_sc[...], weights, (1, 1))

    @pl.when(step == 0)
    def _():
        back_sc[...] = back

    @pl.when(step > 0)
    def _():
        back_sc[...] += back

    @pl.when(step == pl.num_programs(0) - 1)
    def _():
        norms_ref[...] = norm_ref[...]

        @pl.loop(0, blocks)
        def _(block):
            for ref, out_ref, part in ((mine_ref, keep_ref, core_ref[0]), (other_ref, send_ref, 1 - core_ref[0])):
                at = pl.multiple_of(place_ref[block] * rows + part * half, half)
                grad = back_sc[pl.ds(at, half), :]
                out_ref[block] = grad.astype(out_ref.dtype)
                x = ref[block].astype(F32)
                centred = x - jnp.mean(x, axis=-1, keepdims=True)
                unit = centred * lax.rsqrt(jnp.mean(centred * centred, axis=-1, keepdims=True) + norm_eps)
                norms_ref[0:1, :] += jnp.sum(grad * unit, axis=0, keepdims=True)
                norms_ref[1:2, :] += jnp.sum(grad, axis=0, keepdims=True)


def attend_back(core, place, to, qkv, grad, sums, stats, normed, mine, other, norm, w_qkv):
    pairs, length, _ = qkv.shape
    blocks, rows, _ = grad.shape
    width = normed.shape[1]
    area = length * length
    one = lambda i, c, p, t: (i, 0, 0)

    def columns(kind):
        size = width // PAIR
        return pl.BlockSpec((width, PAIR), lambda i, core, p, t: (0, kind * size + core[0] * pairs + i))

    return pl.pallas_call(
        attend_back_kernel,
        grid_spec=pltpu.PrefetchScalarGridSpec(
            num_scalar_prefetch=3,
            grid=(pairs,),
            in_specs=[
                pl.BlockSpec((1, length, 3 * PAIR), one),
                pl.BlockSpec((blocks, rows, PAIR), lambda i, c, p, t: (0, 0, i)),
                pl.BlockSpec((1, PAIR, length), one),
                pl.BlockSpec((1, 8, length), one),
                fixed2(normed.shape),
                fixed2(mine.shape),
                fixed2(mine.shape),
                fixed2(norm.shape),
                *(columns(kind) for kind in range(3)),
            ],
            out_specs=[
                fixed2((pairs * 3 * PAIR, width)),
                fixed2(mine.shape),
                fixed2(mine.shape),
                fixed2(norm.shape),
            ],
            scratch_shapes=[
                pltpu.VMEM((length, PAIR), BF16),
                *[pltpu.VMEM((length, PAIR), F32)] * 3,
                pltpu.VMEM((length, 3 * PAIR), BF16),
                pltpu.VMEM((length, width), F32),
            ],
        ),
        out_shape=[
            jax.ShapeDtypeStruct((pairs * 3 * PAIR, width), BF16),
            jax.ShapeDtypeStruct(mine.shape, F32),
            jax.ShapeDtypeStruct(mine.shape, BF16),
            jax.ShapeDtypeStruct(norm.shape, F32),
        ],
        cost_estimate=pl.CostEstimate(
            flops=pairs * 40 * area * HEAD + 6 * length * width * width,
            bytes_accessed=8 * length * width,
            transcendentals=pairs * area,
        ),
        name="attend_back",
    )(core, place, to, qkv, grad, sums, stats, normed, mine, other, norm, w_qkv, w_qkv, w_qkv)


def merge_kernel(keep_ref, other_ref, norm_ref, out_ref):
    half = keep_ref.shape[1]
    block = norm_ref.shape[1] // keep_ref.shape[0]
    norms = norm_ref[...].astype(BF16)
    for at in range(keep_ref.shape[0]):
        out_ref[at, :half] = (keep_ref[at] + other_ref[at].astype(F32)).astype(BF16)
        out_ref[at, half:] = jnp.zeros_like(out_ref[at, half:])
        out_ref[at, half:, :block] = norms[:, at * block : (at + 1) * block]


def merge(keep, other, norm):
    blocks, half, width = keep.shape
    return pl.pallas_call(
        merge_kernel,
        grid=(1,),
        in_specs=[fixed2(keep.shape), fixed2(keep.shape), fixed2(norm.shape)],
        out_specs=fixed2((blocks, half + norm.shape[0], width)),
        out_shape=jax.ShapeDtypeStruct((blocks, half + norm.shape[0], width), BF16),
        cost_estimate=pl.CostEstimate(
            flops=blocks * half * width, bytes_accessed=8 * blocks * half * width, transcendentals=0
        ),
        name="merge",
    )(keep, other, norm)


@functools.lru_cache
def strips(width, plane):
    near, owned = plane // 2, 3 * width // plane // STRIP
    side, pair = width // 2 // STRIP, PAIR // STRIP
    slots = []
    for core in range(2):
        slot, count = {}, [0, 0]
        for col in range(2 * near * owned):
            if col % (2 * side) // side == core:
                away = (col // owned % 2) ^ core
                slot[col] = (away, count[away])
                count[away] += 1
        assert count == [near * owned // 2] * 2
        slots.append(slot)
    stay = near * owned // 2
    to, found = [], []
    for core in range(2):
        order = [
            kind * 2 * side + core * side + p * pair + strip
            for p in range(side // pair)
            for kind in range(3)
            for strip in range(pair)
        ]
        to.append([slots[core][col][0] * stay + slots[core][col][1] for col in order])
        row = []
        for chip in range(near):
            for strip in range(owned):
                col = (2 * chip + core) * owned + strip
                row.append(slots[core][col][1] if col in slots[core] else stay + slots[1 - core][col][1])
        found.append(row)
    return to, found


def tiles_kernel(near, owned, chip_ref, found_ref, keep_ref, given_ref, *outs):
    step = pl.program_id(0)
    stay = keep_ref.shape[0] // STRIP
    for k in range(near):

        @pl.when(step == k)
        def _():
            for strip in range(owned):
                at = found_ref[(chip_ref[0] ^ k) * owned + strip]
                here = pl.multiple_of(jnp.minimum(at, stay - 1) * STRIP, STRIP)
                there = pl.multiple_of(jnp.maximum(at - stay, 0) * STRIP, STRIP)
                outs[k][strip * STRIP : (strip + 1) * STRIP, :] = jnp.where(
                    at < stay, keep_ref[pl.ds(here, STRIP), :], given_ref[pl.ds(there, STRIP), :]
                )


def qkv_tiles(chip, found, grad, given, near):
    size, width = given.shape
    owned = 2 * size // near // STRIP
    shape = (owned * STRIP, width)
    return pl.pallas_call(
        functools.partial(tiles_kernel, near, owned),
        grid_spec=pltpu.PrefetchScalarGridSpec(
            num_scalar_prefetch=2,
            grid=(near,),
            in_specs=[fixed2(given.shape), fixed2(given.shape)],
            out_specs=[fixed2(shape)] * near,
        ),
        out_shape=[jax.ShapeDtypeStruct(shape, BF16)] * near,
        cost_estimate=pl.CostEstimate(flops=size * width, bytes_accessed=size * width, transcendentals=0),
        name="qkv_tiles",
    )(chip, found, grad, given)


def gelu_pair(u):
    c = 0.7978845608028654
    square = u * u
    t = jnp.tanh(c * u * (1.0 + 0.044715 * square))
    half = 0.5 * (1.0 + t)
    slope = half + 0.5 * c * u * (1.0 - t * t) * (1.0 + 3.0 * 0.044715 * square)
    return u * half, slope


def norm_back(values, gain_vec, grad):
    average = jnp.mean(values, axis=-1, keepdims=True)
    centred = values - average
    spread = jnp.mean(centred * centred, axis=-1, keepdims=True)
    scale = lax.rsqrt(spread + norm_eps)
    unit = centred * scale
    scaled = grad * gain_vec
    back = scale * (
        scaled
        - jnp.mean(scaled, axis=-1, keepdims=True)
        - unit * jnp.mean(scaled * unit, axis=-1, keepdims=True)
    )
    return back, jnp.sum(grad * unit, axis=0, keepdims=True), jnp.sum(grad, axis=0, keepdims=True)


def ff_kernel(seqs, plane, *refs):
    me_ref, x_ref, att_ref, cot_ref, w_out_ref, gain_ref, shift_ref, *refs = refs
    ups, downs, refs = refs[:2], refs[2:4], refs[4:]
    out_ref, res_ref, *refs = refs
    ga_ref, norm_ref, gu_send, gu_keep, gd_send, gd_keep, gp_send, gp_keep, *refs = refs
    att_sc, residual_sc, normed_sc, normed_t, turned_sc, acc_out, acc_grad = refs
    step = pl.program_id(0)
    tokens, width = x_ref.shape
    rows = tokens // seqs
    block = width // plane
    near = plane // 2

    def turn(values):
        turned = values.T
        for j in range(plane):
            t = me_ref[0] ^ j
            slot = (1 - (t & 1)) * near + (t >> 1)
            at = pl.multiple_of(slot * block, block)
            turned_sc[pl.ds(at, block), :] = turned[j * block : (j + 1) * block]

    @pl.when(step == 0)
    def _():
        for seq in range(seqs):
            for core in range(2):
                cols = slice(core * width // 2, (core + 1) * width // 2)
                att_sc[seq * rows : (seq + 1) * rows, cols] = att_ref[seq * 2 + core]
        residual = x_ref[...].astype(F32) + jnp.dot(att_sc[...], w_out_ref[...], preferred_element_type=F32)
        residual_sc[...] = residual
        normed = norm_rows(residual, gain_ref[...], shift_ref[...]).astype(BF16)
        normed_sc[...] = normed
        normed_t[...] = normed.T
        turn(cot_ref[...])
        acc_out[...] = jnp.zeros_like(acc_out)
        acc_grad[...] = jnp.zeros_like(acc_grad)

    up = jnp.concatenate([r[...] for r in ups], axis=1)
    down = jnp.concatenate([r[...] for r in downs], axis=0)
    pre = jnp.dot(normed_sc[...], up, preferred_element_type=F32)
    active, slope = gelu_pair(pre)
    active = active.astype(BF16)
    grad_pre = (dot(cot_ref[...], down, (1, 1)) * slope).astype(BF16)
    acc_out[...] += jnp.dot(active, down, preferred_element_type=F32)
    acc_grad[...] += dot(grad_pre, up, (1, 1))
    grad_up = jnp.dot(normed_t[...], grad_pre, preferred_element_type=F32).astype(BF16)
    grad_down = jnp.dot(turned_sc[...], active, preferred_element_type=F32).astype(BF16)
    part = ups[0].shape[1]
    for half in range(2):
        spot = ((me_ref[0] >> 1) ^ half) & 1
        cols = slice(half * part, (half + 1) * part)
        for slot in range(near):
            gd_send[slot, 0, spot, 0] = grad_down[slot * block : (slot + 1) * block, cols]
            gd_keep[slot, 0, spot, 0] = grad_down[(near + slot) * block : (near + slot + 1) * block, cols]

        @pl.when(step < near // 2)
        def _():
            gu_send[half] = grad_up[:, cols]

        @pl.when(step >= near // 2)
        def _():
            gu_keep[half] = grad_up[:, cols]

    @pl.when(step == near - 1)
    def _():
        residual = residual_sc[...]
        out_ref[...] = (residual + acc_out[...]).astype(BF16)
        back, gain_grad, shift_grad = norm_back(residual, gain_ref[...], acc_grad[...])
        norm_ref[...] = jnp.zeros_like(norm_ref)
        norm_ref[2:3, :] = gain_grad
        norm_ref[3:4, :] = shift_grad
        grad_res = cot_ref[...].astype(F32) + back
        res_ref[...] = grad_res
        grad_z = grad_res.astype(BF16)
        grad_att = dot(grad_z, w_out_ref[...], (1, 1)).astype(BF16)
        for seq in range(seqs):
            for core in range(2):
                cols = slice(core * width // 2, (core + 1) * width // 2)
                ga_ref[seq * 2 + core] = grad_att[seq * rows : (seq + 1) * rows, cols]
        turn(grad_z)
        grad_proj = jnp.dot(turned_sc[...], att_sc[...], preferred_element_type=F32).astype(BF16)
        for slot in range(near):
            gp_send[slot] = grad_proj[slot * block : (slot + 1) * block]
            gp_keep[slot] = grad_proj[(near + slot) * block : (near + slot + 1) * block]


def feed_forward(me, x, attended, cotangent, w_out, gain, shift, w_up, w_down, plane):
    seqs, rows, width = x.shape
    hidden = w_up.shape[1]
    tokens, near, part, block = seqs * rows, plane // 2, hidden // plane, width // plane

    def at(i, me, half=0):
        return me[0] ^ (4 * (i % (near // 2)) + 2 * half + jnp.where(i < near // 2, 1, 0))

    def fixed(shape):
        return pl.BlockSpec(shape, lambda i, me, n=len(shape): (0,) * n)

    joined = attended.shape
    outs = [
        ((tokens, width), BF16, fixed((tokens, width))),
        ((tokens, width), F32, fixed((tokens, width))),
        (joined, BF16, fixed(joined)),
        ((8, width), F32, fixed((8, width))),
        ((near, width, part), BF16, pl.BlockSpec((2, width, part), lambda i, me: (jnp.minimum(i, near // 2 - 1), 0, 0))),
        ((near, width, part), BF16, pl.BlockSpec((2, width, part), lambda i, me: (jnp.maximum(i - near // 2, 0), 0, 0))),
        *[
            (
                (near, plane // 4, 2, 2, block, part),
                BF16,
                pl.BlockSpec(
                    (near, 1, 2, 1, block, part), lambda i, me: (0, at(i, me) >> 2, 0, at(i, me) & 1, 0, 0)
                ),
            )
        ]
        * 2,
        *[((near, block, width), BF16, fixed((near, block, width)))] * 2,
    ]
    return pl.pallas_call(
        functools.partial(ff_kernel, seqs, plane),
        grid_spec=pltpu.PrefetchScalarGridSpec(
            num_scalar_prefetch=1,
            grid=(near,),
            in_specs=[fixed((tokens, width))]
            + [fixed(joined), fixed((tokens, width)), fixed((width, width)), fixed((width,)), fixed((width,))]
            + [
                pl.BlockSpec((width, part), lambda i, me: (0, at(i, me))),
                pl.BlockSpec((width, part), lambda i, me: (0, at(i, me, 1))),
                pl.BlockSpec((part, width), lambda i, me: (at(i, me), 0)),
                pl.BlockSpec((part, width), lambda i, me: (at(i, me, 1), 0)),
            ],
            out_specs=[o[2] for o in outs],
            scratch_shapes=[
                pltpu.VMEM((tokens, width), BF16),
                pltpu.VMEM((tokens, width), F32),
                pltpu.VMEM((tokens, width), BF16),
                pltpu.VMEM((width, tokens), BF16),
                pltpu.VMEM((width, tokens), BF16),
                pltpu.VMEM((tokens, width), F32),
                pltpu.VMEM((tokens, width), F32),
            ],
        ),
        out_shape=[jax.ShapeDtypeStruct(o[0], o[1]) for o in outs],
        cost_estimate=pl.CostEstimate(
            flops=12 * tokens * width * hidden + 6 * tokens * width * width,
            bytes_accessed=8 * width * hidden,
            transcendentals=tokens * hidden,
        ),
        name="feed_forward",
    )(
        me,
        x.reshape(tokens, width),
        attended,
        cotangent.reshape(tokens, width),
        w_out,
        gain,
        shift,
        w_up,
        w_up,
        w_down,
        w_down,
    )


def first_norm_kernel(seqs, x_ref, gain_ref, grad_ref, res_ref, out_ref, norm_ref):
    half = x_ref.shape[0] // seqs // 2
    for piece in range(2 * seqs):
        at = slice(piece * half, (piece + 1) * half)
        values = x_ref[at].astype(F32)
        centred = values - jnp.mean(values, axis=-1, keepdims=True)
        scale = lax.rsqrt(jnp.mean(centred * centred, axis=-1, keepdims=True) + norm_eps)
        unit = centred * scale
        scaled = grad_ref[piece, :half].astype(F32) * gain_ref[...]
        back = scale * (
            scaled
            - jnp.mean(scaled, axis=-1, keepdims=True)
            - unit * jnp.mean(scaled * unit, axis=-1, keepdims=True)
        )
        out_ref[at] = (res_ref[at] + back).astype(BF16)
    norms = grad_ref[0, half:, :PAIR].astype(F32)
    for piece in range(1, 2 * seqs):
        norms = norms + grad_ref[piece, half:, :PAIR].astype(F32)
    norm_ref[...] = norms


def first_norm_back(x, gain, grad, grad_res):
    seqs, rows, width = x.shape
    tokens = seqs * rows
    return pl.pallas_call(
        functools.partial(first_norm_kernel, seqs),
        grid=(1,),
        in_specs=[fixed2((tokens, width)), fixed2((width,)), fixed2(grad.shape), fixed2((tokens, width))],
        out_specs=[fixed2((tokens, width)), fixed2((8, PAIR))],
        out_shape=[jax.ShapeDtypeStruct((tokens, width), BF16), jax.ShapeDtypeStruct((8, PAIR), F32)],
        cost_estimate=pl.CostEstimate(flops=20 * tokens * width, bytes_accessed=12 * tokens * width, transcendentals=0),
        name="first_norm_back",
    )(x.reshape(tokens, width), gain, grad, grad_res)


def exchange(blocks):
    return lax.all_to_all(blocks, ("pb", "ka"), 0, 0, tiled=True)


def swap(values, axes, size, bit):
    return lax.ppermute(values, axes, [(i, i ^ bit) for i in range(size)])


def add_pair_kernel(near, batch, *refs):
    _, up_a, up_b, down_a, down_b, proj_a, proj_b, *outs = refs
    outs, down_outs = outs[:near], outs[near:]
    step = pl.program_id(0)
    part = outs[0].shape[1]

    def both(a, b):
        return a + b

    @pl.when(step < batch)
    def _():
        for k in range(near):
            outs[k][...] = both(up_a[k], up_b[k])

    for far in range(batch):

        @pl.when(step == batch + far)
        def _():
            for k in range(near):
                total = both(down_a[k], down_b[k])
                slab = total.shape[0] * total.shape[1]
                target, at = down_outs[far in (1, 2)], (far > 1) * near * slab + k * slab
                target[at : at + slab] = total.reshape(slab, part)

    @pl.when(step == 2 * batch)
    def _():
        for k in range(near):
            total = both(proj_a[k], proj_b[k])
            outs[k][...] = jnp.concatenate([total[:, :part], total[:, part:]], axis=0)


def add_pair(mine, up, down, proj, batch):
    near, width, part = up[0].shape
    plane, block = down[0].shape[1:3]
    tall, few = width // batch, plane // batch
    up_spec = pl.BlockSpec((near, tall, part), lambda i, m: (0, jnp.minimum(i, batch - 1), 0))
    down_spec = pl.BlockSpec(
        (near, few, block, part), lambda i, m: (0, m[0] ^ jnp.clip(i - batch, 0, batch - 1), 0, 0)
    )
    proj_spec = pl.BlockSpec((near, block, width), lambda i, m: (0, 0, 0))
    last = lambda i, m: (jnp.where(i < batch, i, jnp.where(i < 2 * batch, batch - 1, batch)), 0)
    down_shape = (2 * near * few * block, part)
    return pl.pallas_call(
        functools.partial(add_pair_kernel, near, batch),
        grid_spec=pltpu.PrefetchScalarGridSpec(
            num_scalar_prefetch=1,
            grid=(2 * batch + 1,),
            in_specs=[up_spec] * 2 + [down_spec] * 2 + [proj_spec] * 2,
            out_specs=[pl.BlockSpec((tall, part), last)] * near
            + [pl.BlockSpec(down_shape, lambda i, m: (0, 0))] * 2,
        ),
        out_shape=[jax.ShapeDtypeStruct((width + tall, part), BF16)] * near
        + [jax.ShapeDtypeStruct(down_shape, BF16)] * 2,
        cost_estimate=pl.CostEstimate(
            flops=near * 9 * tall * part, bytes_accessed=6 * near * 9 * tall * part, transcendentals=0
        ),
        name="add_pair",
    )(mine, *up, *down, *proj)


def add_all(parts):
    total = parts[0].astype(F32)
    for p in parts[1:]:
        total = total + p.astype(F32)
    return total


def over_batch(stacked):
    return lax.psum_scatter(stacked, "batch", scatter_dimension=0, tiled=True)[0].astype(F32)


def over_plane(tiles, plane):
    return [tiles[0]] + [swap(tiles[k], ("pb", "ka"), plane, 2 * k) for k in range(1, len(tiles))]


def pack_kernel(batch, mine_ref, *refs):
    early_ref, late_ref, *outs, side_sc = refs
    width, slab = side_sc.shape[0], outs[0].shape[0] // 2
    block = (early_ref.shape[0] - width) // 2
    proj = jnp.concatenate([early_ref[width : width + block], early_ref[width + block :]], axis=1)
    side_sc[...] = jnp.concatenate([late_ref[...], proj], axis=0).T
    for far in range(batch):
        at = pl.multiple_of((mine_ref[0] ^ far) * slab, slab)
        outs[far][:slab] = early_ref[pl.ds(at, slab), :]
        outs[far][slab:] = side_sc[pl.ds(at, slab), :]


def pack(mine, early, late, batch):
    width, part = late.shape[1], early.shape[1]
    shape = (2 * width // batch, part)
    return pl.pallas_call(
        functools.partial(pack_kernel, batch),
        grid_spec=pltpu.PrefetchScalarGridSpec(
            num_scalar_prefetch=1,
            grid=(1,),
            in_specs=[fixed2(early.shape), fixed2(late.shape)],
            out_specs=[fixed2(shape)] * batch,
            scratch_shapes=[pltpu.VMEM((width, part), BF16)],
        ),
        out_shape=[jax.ShapeDtypeStruct(shape, BF16)] * batch,
        cost_estimate=pl.CostEstimate(flops=8 * width * part, bytes_accessed=20 * width * part, transcendentals=0),
        name="pack",
    )(mine, early, late)


def finish_kernel(*refs):
    parts, (up_ref, qkv_ref, proj_ref) = refs[:-3], refs[-3:]
    slab, owned = qkv_ref.shape
    total = add_all([r[...] for r in parts])
    up_ref[...] = total[:slab]
    qkv_ref[...] = total[slab:, :owned]
    proj_ref[...] = total[slab:, owned:]


def finish_down_kernel(*refs):
    parts, down_ref = refs[:-1], refs[-1]
    total = add_all([r[...] for r in parts])
    block, part = down_ref.shape[1], total.shape[1]
    for at in range(total.shape[0] // block):
        down_ref[at * part : (at + 1) * part] = total[at * block : (at + 1) * block].T


def finish(kernel, parts, shapes):
    rows, part = parts[0].shape
    return pl.pallas_call(
        kernel,
        grid=(1,),
        in_specs=[fixed2(a.shape) for a in parts],
        out_specs=[fixed2(s) for s in shapes],
        out_shape=[jax.ShapeDtypeStruct(s, F32) for s in shapes],
        cost_estimate=pl.CostEstimate(flops=8 * rows * part, bytes_accessed=16 * rows * part, transcendentals=0),
        name="finish",
    )(*parts)


def shards(
    inputs,
    block_place,
    ln1_gain,
    ln1_shift,
    w_qkv,
    w_out,
    ln2_gain,
    ln2_shift,
    w_up,
    w_down,
    cotangent,
):
    seqs, rows, width = inputs.shape
    hidden = w_up.shape[1]
    plane = lax.axis_size("pb") * lax.axis_size("ka")
    planes = ("pb", "ka")
    batch = lax.axis_size("batch")
    near = plane // 2
    few = batch == 4
    me = lax.axis_index(planes)
    scalar = lambda value: value.astype(jnp.int32).reshape(1)
    core, chip = scalar(me & 1), scalar(me >> 1)
    part, block, slab = hidden // plane, width // plane, width // batch
    place = lax.dynamic_index_in_dim(block_place, me >> 1, 0, False)
    to, found = [jnp.where(core == 0, *(jnp.array(t, jnp.int32) for t in both)) for both in strips(width, plane)]

    mine = exchange(inputs.reshape(plane, seqs * rows // plane, width))
    other = swap(mine, planes, plane, 1)
    attended, normed1, packed, sums, stats = attend(core, place, mine, other, ln1_gain, ln1_shift, w_qkv)
    outputs, grad_res, grad_att, norm2, *grads = feed_forward(
        scalar(me), inputs, exchange(attended), cotangent, w_out, ln2_gain, ln2_shift, w_up, w_down, plane
    )
    grad_att = exchange(grad_att)
    grads[2:4] = [g.reshape(near, plane, block, part) for g in grads[2:4]]
    up, down, proj = [(grads[2 * i + 1], swap(grads[2 * i], planes, plane, 1)) for i in range(3)]
    if few:
        sums_up = add_pair(scalar(lax.axis_index("batch")), up, down, proj, batch)
        grad_att, sums_up = lax.optimization_barrier((grad_att, sums_up))
        tiles, down = sums_up[:near], sums_up[near:]
    else:
        tiles = [
            jnp.concatenate(
                [add_all([t[k] for t in up])]
                + [add_all([t[k] for t in down]).reshape(width, part)]
                + [add_all([t[k] for t in proj]).reshape(block, 2, part).transpose(1, 0, 2).reshape(2 * block, part)]
            ).astype(BF16)
            for k in range(near)
        ]
    early = add_all(over_plane(tiles, plane)).astype(BF16)
    if few:
        down = add_all([down[0], swap(down[1], "batch", batch, 1)]).astype(BF16)

    grad_qkv, keep, send, norm = attend_back(
        core, place, to, packed, grad_att, sums, stats, normed1, mine, other, norm2, w_qkv
    )
    given = swap(grad_qkv[grad_qkv.shape[0] // 2 :], planes, plane, 1)
    if few:
        given, early, down = lax.optimization_barrier((given, early, down))
        down = jnp.split(down, 2)
        down[1] = swap(down[1], "batch", batch, 3)
    late = qkv_tiles(chip, found, grad_qkv, given, near)
    keep, late = lax.optimization_barrier((keep, late))
    returned = exchange(merge(keep, swap(send, planes, plane, 1), norm))
    late = add_all(over_plane(late, plane)).astype(BF16)
    owned = 3 * width // plane
    if few:
        along = scalar(lax.axis_index("batch"))
        sums = pack(along, early, late, batch)
        sums = [sums[0]] + [swap(sums[bit], "batch", batch, bit) for bit in range(1, batch)]
        returned, down = lax.optimization_barrier((returned, add_all(down).astype(BF16)))
        down = over_plane(jnp.split(down, near), plane)
    grad_inputs, norms = first_norm_back(inputs, ln1_gain, returned, grad_res)
    if few:
        for bit in (1, 2):
            norms = norms + swap(norms, "batch", batch, bit)
        grad_up, grad_qkv, grad_proj = finish(finish_kernel, sums, [(slab, part), (slab, owned), (slab, block)])
        (grad_down,) = finish(finish_down_kernel, down, [(hidden // batch, block)])
    else:
        tile, cut = early, batch // plane
        down_tile = tile[width : 2 * width].reshape(plane, block, cut, part // cut).transpose(0, 2, 1, 3)
        grad_down = over_batch(down_tile.reshape(batch, block, part // cut)).T
        proj_tile = tile[-2 * block :].reshape(2, block, part).transpose(1, 0, 2).reshape(block, batch, slab)
        grad_proj = over_batch(proj_tile.transpose(1, 0, 2)).T
        grad_up = over_batch(tile[:width].reshape(batch, slab, part))
        grad_qkv = over_batch(late.reshape(owned, batch, slab).transpose(1, 0, 2)).T
        norms = lax.psum(norms, "batch")
    return (
        outputs.reshape(inputs.shape),
        grad_inputs.reshape(inputs.shape),
        grad_qkv,
        grad_proj,
        grad_up,
        grad_down,
        norms[:4, :block],
    )


def solution(mesh):
    placed = (
        P("batch", ("pb", "ka"), None),
        P("batch", None),
        P(),
        P(),
        P(),
        P(),
        P(),
        P(),
        P(),
        P(),
        P("batch", ("pb", "ka"), None),
    )
    return jax.shard_map(
        shards,
        mesh=mesh,
        in_specs=placed,
        out_specs=(
            P("batch", ("pb", "ka"), None),
            P("batch", ("pb", "ka"), None),
            P("batch", ("pb", "ka")),
            P("batch", ("pb", "ka")),
            P("batch", ("pb", "ka")),
            P("batch", ("pb", "ka")),
            P(None, ("pb", "ka")),
        ),
        check_vma=False,
    )
```

```python
import functools

import jax
import jax.numpy as jnp
from jax import lax
from jax.experimental import pallas as pl
from jax.experimental.pallas import tpu as pltpu
from jax.sharding import PartitionSpec as P

HEADS = 12
HEAD = 64
PAIR = 2 * HEAD
QTILE = 256
STRIP = 32
SCALE = HEAD ** (-0.5)
HUGE = 3e38
HIDDEN = -1e30

norm_eps = 1e-05
BF16 = jnp.bfloat16
F32 = jnp.float32


def norm_rows(values, gain_vec, shift_vec):
    average = jnp.mean(values, axis=-1, keepdims=True)
    centred = values - average
    spread = jnp.mean(centred * centred, axis=-1, keepdims=True)
    return centred * lax.rsqrt(spread + norm_eps) * gain_vec + shift_vec


def gelu_tanh(values):
    return jax.nn.gelu(values, approximate=True)


def dot(a, b, contract):
    return lax.dot_general(a, b, ((contract[:1], contract[1:]), ((), ())), preferred_element_type=F32)


def head_lanes(values, head):
    lane = lax.broadcasted_iota(jnp.int32, values.shape, 1)
    mine = lane < HEAD if head == 0 else lane >= HEAD
    return jnp.where(mine, values, jnp.zeros_like(values))


def hide_later(magnitude):
    keys = magnitude.shape[0]
    key = lax.broadcasted_iota(jnp.int32, (QTILE, QTILE), 0)
    query = lax.broadcasted_iota(jnp.int32, (QTILE, QTILE), 1)
    last = jnp.where(key <= query, magnitude[keys - QTILE :], HIDDEN)
    return last if keys == QTILE else jnp.concatenate([magnitude[: keys - QTILE], last], axis=0)


def sign_of(scores):
    return jnp.clip(scores * HUGE, -1.0, 1.0)


def attend_kernel(
    core_ref, place_ref, mine_ref, other_ref, gain_ref, shift_ref, wq_ref, wk_ref, wv_ref,
    out_ref, normed_ref, qkv_ref, sums_ref, stats_ref, o_sc,
):
    blocks, half = mine_ref.shape[0], mine_ref.shape[1]
    rows = 2 * half
    total_rows = normed_ref.shape[0]

    @pl.when(pl.program_id(0) == 0)
    def _():
        @pl.loop(0, blocks)
        def _(block):
            for ref, part in ((mine_ref, core_ref[0]), (other_ref, 1 - core_ref[0])):
                at = pl.multiple_of(place_ref[block] * rows + part * half, half)
                normed = norm_rows(ref[block].astype(F32), gain_ref[...], shift_ref[...])
                normed_ref[pl.ds(at, half), :] = normed.astype(BF16)

    weights = jnp.concatenate([wq_ref[...], wk_ref[...], wv_ref[...]], axis=1)
    qkv_ref[0] = jnp.dot(normed_ref[...], weights, preferred_element_type=F32).astype(BF16)
    v_t = qkv_ref[0, :, 2 * PAIR :].T
    for tile in range(total_rows // QTILE):
        span = slice(tile * QTILE, (tile + 1) * QTILE)
        keys = (tile + 1) * QTILE
        queries = qkv_ref[0, span, :PAIR] * SCALE
        for head in range(2):
            scores = dot(qkv_ref[0, :keys, PAIR : 2 * PAIR], head_lanes(queries, head).astype(BF16), (1, 1))
            magnitude = hide_later(jnp.abs(scores))
            peak = jnp.max(magnitude, axis=0, keepdims=True)
            exponents = jnp.exp(magnitude - peak)
            total = jnp.sum(exponents, axis=0, keepdims=True)
            weights = (exponents * sign_of(scores)).astype(BF16)
            summed = dot(v_t[head * HEAD : (head + 1) * HEAD, :keys], weights, (1, 0))
            sums_ref[0, head * HEAD : (head + 1) * HEAD, span] = summed / total
            stats_ref[0, head : head + 1, span] = peak + jnp.log(total)
        o_sc[span, :] = sums_ref[0, :, span].T
    for block in range(blocks):
        at = pl.multiple_of(place_ref[block] * rows, rows)
        out_ref[block] = o_sc[pl.ds(at, rows), :].astype(BF16)


def columns_of(width, size, kind, pairs):
    return pl.BlockSpec(
        (width, size), lambda i, core, place: (0, kind * (width // size) + core[0] * pairs + jnp.minimum(i, pairs - 1))
    )


def fixed2(shape):
    return pl.BlockSpec(shape, lambda i, *scalars, n=len(shape): (0,) * n)


def attend(core, place, mine, other, gain, shift, w_qkv):
    blocks, half, width = mine.shape
    length, pairs = 2 * half * blocks, width // PAIR // 2
    area = length * length
    return pl.pallas_call(
        attend_kernel,
        grid_spec=pltpu.PrefetchScalarGridSpec(
            num_scalar_prefetch=2,
            grid=(pairs,),
            in_specs=[fixed2(mine.shape), fixed2(mine.shape), fixed2((width,)), fixed2((width,))]
            + [columns_of(width, PAIR, kind, pairs) for kind in range(3)],
            out_specs=[
                pl.BlockSpec((blocks, 2 * half, PAIR), lambda i, c, p: (0, 0, i)),
                fixed2((length, width)),
                pl.BlockSpec((1, length, 3 * PAIR), lambda i, c, p: (i, 0, 0)),
                pl.BlockSpec((1, PAIR, length), lambda i, c, p: (i, 0, 0)),
                pl.BlockSpec((1, 8, length), lambda i, c, p: (i, 0, 0)),
            ],
            scratch_shapes=[pltpu.VMEM((length, PAIR), F32)],
        ),
        out_shape=[
            jax.ShapeDtypeStruct((blocks, 2 * half, pairs * PAIR), BF16),
            jax.ShapeDtypeStruct((length, width), BF16),
            jax.ShapeDtypeStruct((pairs, length, 3 * PAIR), BF16),
            jax.ShapeDtypeStruct((pairs, PAIR, length), F32),
            jax.ShapeDtypeStruct((pairs, 8, length), F32),
        ],
        cost_estimate=pl.CostEstimate(
            flops=pairs * 16 * area * HEAD + 3 * length * width * width,
            bytes_accessed=8 * length * width,
            transcendentals=pairs * area,
        ),
        name="attend",
    )(core, place, mine, other, gain, shift, w_qkv, w_qkv, w_qkv)


def attend_back_kernel(
    core_ref, place_ref, to_ref, qkv_ref, g_ref, sums_ref, stats_ref, normed_ref, mine_ref, other_ref, norm_ref,
    wq_ref, wk_ref, wv_ref, gq_ref, keep_ref, send_ref, norms_ref, g_sc, dq_sc, dk_sc, dv_sc, packed_sc, back_sc,
):
    blocks, rows = g_ref.shape[0], g_ref.shape[1]
    for block in range(blocks):
        at = pl.multiple_of(place_ref[block] * rows, rows)
        g_sc[pl.ds(at, rows), :] = g_ref[block]
    total_rows = g_sc.shape[0]
    k_t = qkv_ref[0, :, PAIR : 2 * PAIR].T
    g_t = g_sc[...].astype(F32).T
    products = g_t * sums_ref[0]
    deltas = [
        jnp.sum(products[head * HEAD : (head + 1) * HEAD], axis=0, keepdims=True) for head in range(2)
    ]
    dk_sc[...] = jnp.zeros_like(dk_sc)
    dv_sc[...] = jnp.zeros_like(dv_sc)
    for tile in range(total_rows // QTILE):
        span = slice(tile * QTILE, (tile + 1) * QTILE)
        keys = (tile + 1) * QTILE
        queries = qkv_ref[0, span, :PAIR] * SCALE
        parts = []
        for head in range(2):
            q_head = head_lanes(queries, head).astype(BF16)
            g_head = head_lanes(g_sc[span, :], head)
            scores = dot(qkv_ref[0, :keys, PAIR : 2 * PAIR], q_head, (1, 1))
            magnitude = hide_later(jnp.abs(scores))
            sign = sign_of(scores)
            signed = jnp.exp(magnitude - stats_ref[0, head : head + 1, span]) * sign
            grad_weights = dot(qkv_ref[0, :keys, 2 * PAIR :], g_head, (1, 1))
            grad_scores = (signed * (sign * grad_weights - deltas[head][:, span])).astype(BF16)
            dv_sc[:keys, :] += dot(signed.astype(BF16), g_head, (1, 0))
            dk_sc[:keys, :] += dot(grad_scores, q_head, (1, 0))
            parts.append(dot(k_t[head * HEAD : (head + 1) * HEAD, :keys], grad_scores, (1, 0)))
        dq_sc[span, :] = jnp.concatenate(parts, axis=0).T * SCALE
    for kind, ref in enumerate((dq_sc, dk_sc, dv_sc)):
        grad = ref[...].astype(BF16)
        packed_sc[:, kind * PAIR : (kind + 1) * PAIR] = grad
        turned = jnp.dot(grad.T, normed_ref[...], preferred_element_type=F32).astype(BF16)
        for strip in range(PAIR // STRIP):
            at = to_ref[(pl.program_id(0) * 3 + kind) * (PAIR // STRIP) + strip]
            at = pl.multiple_of(at * STRIP, STRIP)
            gq_ref[pl.ds(at, STRIP), :] = turned[strip * STRIP : (strip + 1) * STRIP]

    step, half = pl.program_id(0), mine_ref.shape[1]
    weights = jnp.concatenate([wq_ref[...], wk_ref[...], wv_ref[...]], axis=1)
    back = dot(packed_sc[...], weights, (1, 1))

    @pl.when(step == 0)
    def _():
        back_sc[...] = back

    @pl.when(step > 0)
    def _():
        back_sc[...] += back

    @pl.when(step == pl.num_programs(0) - 1)
    def _():
        norms_ref[...] = norm_ref[...]

        @pl.loop(0, blocks)
        def _(block):
            for ref, out_ref, part in ((mine_ref, keep_ref, core_ref[0]), (other_ref, send_ref, 1 - core_ref[0])):
                at = pl.multiple_of(place_ref[block] * rows + part * half, half)
                grad = back_sc[pl.ds(at, half), :]
                out_ref[block] = grad.astype(out_ref.dtype)
                x = ref[block].astype(F32)
                centred = x - jnp.mean(x, axis=-1, keepdims=True)
                unit = centred * lax.rsqrt(jnp.mean(centred * centred, axis=-1, keepdims=True) + norm_eps)
                norms_ref[0:1, :] += jnp.sum(grad * unit, axis=0, keepdims=True)
                norms_ref[1:2, :] += jnp.sum(grad, axis=0, keepdims=True)


def attend_back(core, place, to, qkv, grad, sums, stats, normed, mine, other, norm, w_qkv):
    pairs, length, _ = qkv.shape
    blocks, rows, _ = grad.shape
    width = normed.shape[1]
    area = length * length
    one = lambda i, c, p, t: (i, 0, 0)

    def columns(kind):
        size = width // PAIR
        return pl.BlockSpec((width, PAIR), lambda i, core, p, t: (0, kind * size + core[0] * pairs + i))

    return pl.pallas_call(
        attend_back_kernel,
        grid_spec=pltpu.PrefetchScalarGridSpec(
            num_scalar_prefetch=3,
            grid=(pairs,),
            in_specs=[
                pl.BlockSpec((1, length, 3 * PAIR), one),
                pl.BlockSpec((blocks, rows, PAIR), lambda i, c, p, t: (0, 0, i)),
                pl.BlockSpec((1, PAIR, length), one),
                pl.BlockSpec((1, 8, length), one),
                fixed2(normed.shape),
                fixed2(mine.shape),
                fixed2(mine.shape),
                fixed2(norm.shape),
                *(columns(kind) for kind in range(3)),
            ],
            out_specs=[
                fixed2((pairs * 3 * PAIR, width)),
                fixed2(mine.shape),
                fixed2(mine.shape),
                fixed2(norm.shape),
            ],
            scratch_shapes=[
                pltpu.VMEM((length, PAIR), BF16),
                *[pltpu.VMEM((length, PAIR), F32)] * 3,
                pltpu.VMEM((length, 3 * PAIR), BF16),
                pltpu.VMEM((length, width), F32),
            ],
        ),
        out_shape=[
            jax.ShapeDtypeStruct((pairs * 3 * PAIR, width), BF16),
            jax.ShapeDtypeStruct(mine.shape, F32),
            jax.ShapeDtypeStruct(mine.shape, BF16),
            jax.ShapeDtypeStruct(norm.shape, F32),
        ],
        cost_estimate=pl.CostEstimate(
            flops=pairs * 40 * area * HEAD + 6 * length * width * width,
            bytes_accessed=8 * length * width,
            transcendentals=pairs * area,
        ),
        name="attend_back",
    )(core, place, to, qkv, grad, sums, stats, normed, mine, other, norm, w_qkv, w_qkv, w_qkv)


def merge_kernel(keep_ref, other_ref, norm_ref, out_ref):
    half = keep_ref.shape[1]
    block = norm_ref.shape[1] // keep_ref.shape[0]
    norms = norm_ref[...].astype(BF16)
    for at in range(keep_ref.shape[0]):
        out_ref[at, :half] = (keep_ref[at] + other_ref[at].astype(F32)).astype(BF16)
        out_ref[at, half:] = jnp.zeros_like(out_ref[at, half:])
        out_ref[at, half:, :block] = norms[:, at * block : (at + 1) * block]


def merge(keep, other, norm):
    blocks, half, width = keep.shape
    return pl.pallas_call(
        merge_kernel,
        grid=(1,),
        in_specs=[fixed2(keep.shape), fixed2(keep.shape), fixed2(norm.shape)],
        out_specs=fixed2((blocks, half + norm.shape[0], width)),
        out_shape=jax.ShapeDtypeStruct((blocks, half + norm.shape[0], width), BF16),
        cost_estimate=pl.CostEstimate(
            flops=blocks * half * width, bytes_accessed=8 * blocks * half * width, transcendentals=0
        ),
        name="merge",
    )(keep, other, norm)


@functools.lru_cache
def strips(width, plane):
    near, owned = plane // 2, 3 * width // plane // STRIP
    side, pair = width // 2 // STRIP, PAIR // STRIP
    slots = []
    for core in range(2):
        slot, count = {}, [0, 0]
        for col in range(2 * near * owned):
            if col % (2 * side) // side == core:
                away = (col // owned % 2) ^ core
                slot[col] = (away, count[away])
                count[away] += 1
        assert count == [near * owned // 2] * 2
        slots.append(slot)
    stay = near * owned // 2
    to, found = [], []
    for core in range(2):
        order = [
            kind * 2 * side + core * side + p * pair + strip
            for p in range(side // pair)
            for kind in range(3)
            for strip in range(pair)
        ]
        to.append([slots[core][col][0] * stay + slots[core][col][1] for col in order])
        row = []
        for chip in range(near):
            for strip in range(owned):
                col = (2 * chip + core) * owned + strip
                row.append(slots[core][col][1] if col in slots[core] else stay + slots[1 - core][col][1])
        found.append(row)
    return to, found


def tiles_kernel(near, owned, chip_ref, found_ref, keep_ref, given_ref, *outs):
    stay = keep_ref.shape[0] // STRIP
    for k in range(near):
        for strip in range(owned):
            at = found_ref[(chip_ref[0] ^ k) * owned + strip]
            here = pl.multiple_of(jnp.minimum(at, stay - 1) * STRIP, STRIP)
            there = pl.multiple_of(jnp.maximum(at - stay, 0) * STRIP, STRIP)
            outs[k][strip * STRIP : (strip + 1) * STRIP, :] = jnp.where(
                at < stay, keep_ref[pl.ds(here, STRIP), :], given_ref[pl.ds(there, STRIP), :]
            )


def qkv_tiles(chip, found, grad, given, near):
    size, width = given.shape
    owned = 2 * size // near // STRIP
    shape = (owned * STRIP, width)
    return pl.pallas_call(
        functools.partial(tiles_kernel, near, owned),
        grid_spec=pltpu.PrefetchScalarGridSpec(
            num_scalar_prefetch=2,
            grid=(1,),
            in_specs=[fixed2(given.shape), fixed2(given.shape)],
            out_specs=[fixed2(shape)] * near,
        ),
        out_shape=[jax.ShapeDtypeStruct(shape, BF16)] * near,
        cost_estimate=pl.CostEstimate(flops=size * width, bytes_accessed=size * width, transcendentals=0),
        name="qkv_tiles",
    )(chip, found, grad, given)


def gelu_pair(u):
    c = 0.7978845608028654
    square = u * u
    t = jnp.tanh(c * u * (1.0 + 0.044715 * square))
    half = 0.5 * (1.0 + t)
    slope = half + 0.5 * c * u * (1.0 - t * t) * (1.0 + 3.0 * 0.044715 * square)
    return u * half, slope


def norm_back(values, gain_vec, grad):
    average = jnp.mean(values, axis=-1, keepdims=True)
    centred = values - average
    spread = jnp.mean(centred * centred, axis=-1, keepdims=True)
    scale = lax.rsqrt(spread + norm_eps)
    unit = centred * scale
    scaled = grad * gain_vec
    back = scale * (
        scaled
        - jnp.mean(scaled, axis=-1, keepdims=True)
        - unit * jnp.mean(scaled * unit, axis=-1, keepdims=True)
    )
    return back, jnp.sum(grad * unit, axis=0, keepdims=True), jnp.sum(grad, axis=0, keepdims=True)


def ff_kernel(seqs, plane, *refs):
    me_ref, x_ref, att_ref, cot_ref, w_out_ref, gain_ref, shift_ref, *refs = refs
    ups, downs, refs = refs[:2], refs[2:4], refs[4:]
    out_ref, res_ref, *refs = refs
    ga_ref, norm_ref, gu_send, gu_keep, gd_send, gd_keep, gp_send, gp_keep, *refs = refs
    att_sc, residual_sc, normed_sc, normed_t, turned_sc, acc_out, acc_grad = refs
    step = pl.program_id(0)
    tokens, width = x_ref.shape
    rows = tokens // seqs
    block = width // plane
    near = plane // 2

    def turn(values):
        turned = values.T
        for j in range(plane):
            t = me_ref[0] ^ j
            slot = (1 - (t & 1)) * near + (t >> 1)
            at = pl.multiple_of(slot * block, block)
            turned_sc[pl.ds(at, block), :] = turned[j * block : (j + 1) * block]

    @pl.when(step == 0)
    def _():
        for seq in range(seqs):
            for core in range(2):
                cols = slice(core * width // 2, (core + 1) * width // 2)
                att_sc[seq * rows : (seq + 1) * rows, cols] = att_ref[seq * 2 + core]
        residual = x_ref[...].astype(F32) + jnp.dot(att_sc[...], w_out_ref[...], preferred_element_type=F32)
        residual_sc[...] = residual
        normed = norm_rows(residual, gain_ref[...], shift_ref[...]).astype(BF16)
        normed_sc[...] = normed
        normed_t[...] = normed.T
        turn(cot_ref[...])
        acc_out[...] = jnp.zeros_like(acc_out)
        acc_grad[...] = jnp.zeros_like(acc_grad)

    up = jnp.concatenate([r[...] for r in ups], axis=1)
    down = jnp.concatenate([r[...] for r in downs], axis=0)
    pre = jnp.dot(normed_sc[...], up, preferred_element_type=F32)
    active, slope = gelu_pair(pre)
    active = active.astype(BF16)
    grad_pre = (dot(cot_ref[...], down, (1, 1)) * slope).astype(BF16)
    acc_out[...] += jnp.dot(active, down, preferred_element_type=F32)
    acc_grad[...] += dot(grad_pre, up, (1, 1))
    grad_up = jnp.dot(normed_t[...], grad_pre, preferred_element_type=F32).astype(BF16)
    grad_down = jnp.dot(turned_sc[...], active, preferred_element_type=F32).astype(BF16)
    part = ups[0].shape[1]
    for half in range(2):
        spot = ((me_ref[0] >> 1) ^ half) & 1
        cols = slice(half * part, (half + 1) * part)
        for slot in range(near):
            gd_send[slot, 0, spot, 0] = grad_down[slot * block : (slot + 1) * block, cols]
            gd_keep[slot, 0, spot, 0] = grad_down[(near + slot) * block : (near + slot + 1) * block, cols]

        @pl.when(step < near // 2)
        def _():
            gu_send[half] = grad_up[:, cols]

        @pl.when(step >= near // 2)
        def _():
            gu_keep[half] = grad_up[:, cols]

    @pl.when(step == near - 1)
    def _():
        residual = residual_sc[...]
        out_ref[...] = (residual + acc_out[...]).astype(BF16)
        back, gain_grad, shift_grad = norm_back(residual, gain_ref[...], acc_grad[...])
        norm_ref[...] = jnp.zeros_like(norm_ref)
        norm_ref[2:3, :] = gain_grad
        norm_ref[3:4, :] = shift_grad
        grad_res = cot_ref[...].astype(F32) + back
        res_ref[...] = grad_res
        grad_z = grad_res.astype(BF16)
        grad_att = dot(grad_z, w_out_ref[...], (1, 1)).astype(BF16)
        for seq in range(seqs):
            for core in range(2):
                cols = slice(core * width // 2, (core + 1) * width // 2)
                ga_ref[seq * 2 + core] = grad_att[seq * rows : (seq + 1) * rows, cols]
        turn(grad_z)
        grad_proj = jnp.dot(turned_sc[...], att_sc[...], preferred_element_type=F32).astype(BF16)
        for slot in range(near):
            gp_send[slot] = grad_proj[slot * block : (slot + 1) * block]
            gp_keep[slot] = grad_proj[(near + slot) * block : (near + slot + 1) * block]


def feed_forward(me, x, attended, cotangent, w_out, gain, shift, w_up, w_down, plane):
    seqs, rows, width = x.shape
    hidden = w_up.shape[1]
    tokens, near, part, block = seqs * rows, plane // 2, hidden // plane, width // plane

    def at(i, me, half=0):
        return me[0] ^ (4 * (i % (near // 2)) + 2 * half + jnp.where(i < near // 2, 1, 0))

    def fixed(shape):
        return pl.BlockSpec(shape, lambda i, me, n=len(shape): (0,) * n)

    joined = attended.shape
    outs = [
        ((tokens, width), BF16, fixed((tokens, width))),
        ((tokens, width), F32, fixed((tokens, width))),
        (joined, BF16, fixed(joined)),
        ((8, width), F32, fixed((8, width))),
        ((near, width, part), BF16, pl.BlockSpec((2, width, part), lambda i, me: (jnp.minimum(i, near // 2 - 1), 0, 0))),
        ((near, width, part), BF16, pl.BlockSpec((2, width, part), lambda i, me: (jnp.maximum(i - near // 2, 0), 0, 0))),
        *[
            (
                (near, plane // 4, 2, 2, block, part),
                BF16,
                pl.BlockSpec(
                    (near, 1, 2, 1, block, part), lambda i, me: (0, at(i, me) >> 2, 0, at(i, me) & 1, 0, 0)
                ),
            )
        ]
        * 2,
        *[((near, block, width), BF16, fixed((near, block, width)))] * 2,
    ]
    return pl.pallas_call(
        functools.partial(ff_kernel, seqs, plane),
        grid_spec=pltpu.PrefetchScalarGridSpec(
            num_scalar_prefetch=1,
            grid=(near,),
            in_specs=[fixed((tokens, width))]
            + [fixed(joined), fixed((tokens, width)), fixed((width, width)), fixed((width,)), fixed((width,))]
            + [
                pl.BlockSpec((width, part), lambda i, me: (0, at(i, me))),
                pl.BlockSpec((width, part), lambda i, me: (0, at(i, me, 1))),
                pl.BlockSpec((part, width), lambda i, me: (at(i, me), 0)),
                pl.BlockSpec((part, width), lambda i, me: (at(i, me, 1), 0)),
            ],
            out_specs=[o[2] for o in outs],
            scratch_shapes=[
                pltpu.VMEM((tokens, width), BF16),
                pltpu.VMEM((tokens, width), F32),
                pltpu.VMEM((tokens, width), BF16),
                pltpu.VMEM((width, tokens), BF16),
                pltpu.VMEM((width, tokens), BF16),
                pltpu.VMEM((tokens, width), F32),
                pltpu.VMEM((tokens, width), F32),
            ],
        ),
        out_shape=[jax.ShapeDtypeStruct(o[0], o[1]) for o in outs],
        cost_estimate=pl.CostEstimate(
            flops=12 * tokens * width * hidden + 6 * tokens * width * width,
            bytes_accessed=8 * width * hidden,
            transcendentals=tokens * hidden,
        ),
        name="feed_forward",
    )(
        me,
        x.reshape(tokens, width),
        attended,
        cotangent.reshape(tokens, width),
        w_out,
        gain,
        shift,
        w_up,
        w_up,
        w_down,
        w_down,
    )


def first_norm_kernel(seqs, x_ref, gain_ref, grad_ref, res_ref, out_ref, norm_ref):
    half = x_ref.shape[0] // seqs // 2
    for piece in range(2 * seqs):
        at = slice(piece * half, (piece + 1) * half)
        values = x_ref[at].astype(F32)
        centred = values - jnp.mean(values, axis=-1, keepdims=True)
        scale = lax.rsqrt(jnp.mean(centred * centred, axis=-1, keepdims=True) + norm_eps)
        unit = centred * scale
        scaled = grad_ref[piece, :half].astype(F32) * gain_ref[...]
        back = scale * (
            scaled
            - jnp.mean(scaled, axis=-1, keepdims=True)
            - unit * jnp.mean(scaled * unit, axis=-1, keepdims=True)
        )
        out_ref[at] = (res_ref[at] + back).astype(BF16)
    norms = grad_ref[0, half:, :PAIR].astype(F32)
    for piece in range(1, 2 * seqs):
        norms = norms + grad_ref[piece, half:, :PAIR].astype(F32)
    norm_ref[...] = norms


def first_norm_back(x, gain, grad, grad_res):
    seqs, rows, width = x.shape
    tokens = seqs * rows
    return pl.pallas_call(
        functools.partial(first_norm_kernel, seqs),
        grid=(1,),
        in_specs=[fixed2((tokens, width)), fixed2((width,)), fixed2(grad.shape), fixed2((tokens, width))],
        out_specs=[fixed2((tokens, width)), fixed2((8, PAIR))],
        out_shape=[jax.ShapeDtypeStruct((tokens, width), BF16), jax.ShapeDtypeStruct((8, PAIR), F32)],
        cost_estimate=pl.CostEstimate(flops=20 * tokens * width, bytes_accessed=12 * tokens * width, transcendentals=0),
        name="first_norm_back",
    )(x.reshape(tokens, width), gain, grad, grad_res)


def exchange(blocks):
    return lax.all_to_all(blocks, ("pb", "ka"), 0, 0, tiled=True)


def swap(values, axes, size, bit):
    return lax.ppermute(values, axes, [(i, i ^ bit) for i in range(size)])


def add_pair_kernel(near, batch, *refs):
    _, up_a, up_b, down_a, down_b, proj_a, proj_b, *outs = refs
    outs, down_outs = outs[:near], outs[near:]
    step = pl.program_id(0)
    part = outs[0].shape[1]

    def both(a, b):
        return a + b

    @pl.when(step < batch)
    def _():
        for k in range(near):
            outs[k][...] = both(up_a[k], up_b[k])

    for far in range(batch):

        @pl.when(step == far)
        def _():
            for k in range(near):
                total = both(down_a[k], down_b[k])
                slab = total.shape[0] * total.shape[1]
                target, at = down_outs[far in (1, 2)], (far > 1) * near * slab + k * slab
                target[at : at + slab] = total.reshape(slab, part)

    @pl.when(step == batch)
    def _():
        for k in range(near):
            total = both(proj_a[k], proj_b[k])
            outs[k][...] = jnp.concatenate([total[:, :part], total[:, part:]], axis=0)


def add_pair(mine, up, down, proj, batch):
    near, width, part = up[0].shape
    plane, block = down[0].shape[1:3]
    tall, few = width // batch, plane // batch
    up_spec = pl.BlockSpec((near, tall, part), lambda i, m: (0, jnp.minimum(i, batch - 1), 0))
    down_spec = pl.BlockSpec(
        (near, few, block, part), lambda i, m: (0, m[0] ^ jnp.minimum(i, batch - 1), 0, 0)
    )
    proj_spec = pl.BlockSpec((near, block, width), lambda i, m: (0, 0, 0))
    last = lambda i, m: (i, 0)
    down_shape = (2 * near * few * block, part)
    return pl.pallas_call(
        functools.partial(add_pair_kernel, near, batch),
        grid_spec=pltpu.PrefetchScalarGridSpec(
            num_scalar_prefetch=1,
            grid=(batch + 1,),
            in_specs=[up_spec] * 2 + [down_spec] * 2 + [proj_spec] * 2,
            out_specs=[pl.BlockSpec((tall, part), last)] * near
            + [pl.BlockSpec(down_shape, lambda i, m: (0, 0))] * 2,
        ),
        out_shape=[jax.ShapeDtypeStruct((width + tall, part), BF16)] * near
        + [jax.ShapeDtypeStruct(down_shape, BF16)] * 2,
        cost_estimate=pl.CostEstimate(
            flops=near * 9 * tall * part, bytes_accessed=6 * near * 9 * tall * part, transcendentals=0
        ),
        name="add_pair",
    )(mine, *up, *down, *proj)


def add_all(parts):
    total = parts[0].astype(F32)
    for p in parts[1:]:
        total = total + p.astype(F32)
    return total


def over_batch(stacked):
    return lax.psum_scatter(stacked, "batch", scatter_dimension=0, tiled=True)[0].astype(F32)


def over_plane(tiles, plane):
    return [tiles[0]] + [swap(tiles[k], ("pb", "ka"), plane, 2 * k) for k in range(1, len(tiles))]


def pack_kernel(batch, mine_ref, *refs):
    early_ref, late_ref, *outs, side_sc = refs
    width, slab = side_sc.shape[0], outs[0].shape[0] // 2
    block = (early_ref.shape[0] - width) // 2
    proj = jnp.concatenate([early_ref[width : width + block], early_ref[width + block :]], axis=1)
    side_sc[...] = jnp.concatenate([late_ref[...], proj], axis=0).T
    for far in range(batch):
        at = pl.multiple_of((mine_ref[0] ^ far) * slab, slab)
        outs[far][:slab] = early_ref[pl.ds(at, slab), :]
        outs[far][slab:] = side_sc[pl.ds(at, slab), :]


def pack(mine, early, late, batch):
    width, part = late.shape[1], early.shape[1]
    shape = (2 * width // batch, part)
    return pl.pallas_call(
        functools.partial(pack_kernel, batch),
        grid_spec=pltpu.PrefetchScalarGridSpec(
            num_scalar_prefetch=1,
            grid=(1,),
            in_specs=[fixed2(early.shape), fixed2(late.shape)],
            out_specs=[fixed2(shape)] * batch,
            scratch_shapes=[pltpu.VMEM((width, part), BF16)],
        ),
        out_shape=[jax.ShapeDtypeStruct(shape, BF16)] * batch,
        cost_estimate=pl.CostEstimate(flops=8 * width * part, bytes_accessed=20 * width * part, transcendentals=0),
        name="pack",
    )(mine, early, late)


def finish_kernel(*refs):
    parts, (up_ref, qkv_ref, proj_ref) = refs[:-3], refs[-3:]
    slab, owned = qkv_ref.shape
    total = add_all([r[...] for r in parts])
    up_ref[...] = total[:slab]
    qkv_ref[...] = total[slab:, :owned]
    proj_ref[...] = total[slab:, owned:]


def finish_down_kernel(*refs):
    parts, down_ref = refs[:-1], refs[-1]
    total = add_all([r[...] for r in parts])
    block, part = down_ref.shape[0], total.shape[1]
    for at in range(total.shape[0] // block):
        down_ref[:, at * part : (at + 1) * part] = total[at * block : (at + 1) * block]


def finish(kernel, parts, shapes):
    rows, part = parts[0].shape
    return pl.pallas_call(
        kernel,
        grid=(1,),
        in_specs=[fixed2(a.shape) for a in parts],
        out_specs=[fixed2(s) for s in shapes],
        out_shape=[jax.ShapeDtypeStruct(s, F32) for s in shapes],
        cost_estimate=pl.CostEstimate(flops=8 * rows * part, bytes_accessed=16 * rows * part, transcendentals=0),
        name="finish",
    )(*parts)


def shards(
    inputs,
    block_place,
    ln1_gain,
    ln1_shift,
    w_qkv,
    w_out,
    ln2_gain,
    ln2_shift,
    w_up,
    w_down,
    cotangent,
):
    seqs, rows, width = inputs.shape
    hidden = w_up.shape[1]
    plane = lax.axis_size("pb") * lax.axis_size("ka")
    planes = ("pb", "ka")
    batch = lax.axis_size("batch")
    near = plane // 2
    few = batch == 4
    me = lax.axis_index(planes)
    scalar = lambda value: value.astype(jnp.int32).reshape(1)
    core, chip = scalar(me & 1), scalar(me >> 1)
    part, block, slab = hidden // plane, width // plane, width // batch
    place = lax.dynamic_index_in_dim(block_place, me >> 1, 0, False)
    to, found = [jnp.where(core == 0, *(jnp.array(t, jnp.int32) for t in both)) for both in strips(width, plane)]

    mine = exchange(inputs.reshape(plane, seqs * rows // plane, width))
    other = swap(mine, planes, plane, 1)
    attended, normed1, packed, sums, stats = attend(core, place, mine, other, ln1_gain, ln1_shift, w_qkv)
    outputs, grad_res, grad_att, norm2, *grads = feed_forward(
        scalar(me), inputs, exchange(attended), cotangent, w_out, ln2_gain, ln2_shift, w_up, w_down, plane
    )
    grad_att = exchange(grad_att)
    grads[2:4] = [g.reshape(near, plane, block, part) for g in grads[2:4]]
    up, down, proj = [(grads[2 * i + 1], swap(grads[2 * i], planes, plane, 1)) for i in range(3)]
    if few:
        sums_up = add_pair(scalar(lax.axis_index("batch")), up, down, proj, batch)
        grad_att, sums_up = lax.optimization_barrier((grad_att, sums_up))
        tiles, down = sums_up[:near], sums_up[near:]
    else:
        tiles = [
            jnp.concatenate(
                [add_all([t[k] for t in up])]
                + [add_all([t[k] for t in down]).reshape(width, part)]
                + [add_all([t[k] for t in proj]).reshape(block, 2, part).transpose(1, 0, 2).reshape(2 * block, part)]
            ).astype(BF16)
            for k in range(near)
        ]
    early = add_all(over_plane(tiles, plane)).astype(BF16)
    if few:
        down = add_all([down[0], swap(down[1], "batch", batch, 1)]).astype(BF16)

    grad_qkv, keep, send, norm = attend_back(
        core, place, to, packed, grad_att, sums, stats, normed1, mine, other, norm2, w_qkv
    )
    given = swap(grad_qkv[grad_qkv.shape[0] // 2 :], planes, plane, 1)
    if few:
        given, early, down = lax.optimization_barrier((given, early, down))
        down = jnp.split(down, 2)
        down[1] = swap(down[1], "batch", batch, 3)
    late = qkv_tiles(chip, found, grad_qkv, given, near)
    keep, late = lax.optimization_barrier((keep, late))
    returned = exchange(merge(keep, swap(send, planes, plane, 1), norm))
    late = add_all(over_plane(late, plane)).astype(BF16)
    owned = 3 * width // plane
    if few:
        along = scalar(lax.axis_index("batch"))
        sums = pack(along, early, late, batch)
        sums = [sums[0]] + [swap(sums[bit], "batch", batch, bit) for bit in range(1, batch)]
        returned, down = lax.optimization_barrier((returned, add_all(down).astype(BF16)))
        down = over_plane(jnp.split(down, near), plane)
    grad_inputs, norms = first_norm_back(inputs, ln1_gain, returned, grad_res)
    if few:
        for bit in (1, 2):
            norms = norms + swap(norms, "batch", batch, bit)
        grad_up, grad_qkv, grad_proj = finish(finish_kernel, sums, [(slab, part), (slab, owned), (slab, block)])
        (grad_down,) = finish(finish_down_kernel, down, [(block, hidden // batch)])
        grad_down = grad_down.T
    else:
        tile, cut = early, batch // plane
        down_tile = tile[width : 2 * width].reshape(plane, block, cut, part // cut).transpose(0, 2, 1, 3)
        grad_down = over_batch(down_tile.reshape(batch, block, part // cut)).T
        proj_tile = tile[-2 * block :].reshape(2, block, part).transpose(1, 0, 2).reshape(block, batch, slab)
        grad_proj = over_batch(proj_tile.transpose(1, 0, 2)).T
        grad_up = over_batch(tile[:width].reshape(batch, slab, part))
        grad_qkv = over_batch(late.reshape(owned, batch, slab).transpose(1, 0, 2)).T
        norms = lax.psum(norms, "batch")
    return (
        outputs.reshape(inputs.shape),
        grad_inputs.reshape(inputs.shape),
        grad_qkv,
        grad_proj,
        grad_up,
        grad_down,
        norms[:4, :block],
    )


def solution(mesh):
    placed = (
        P("batch", ("pb", "ka"), None),
        P("batch", None),
        P(),
        P(),
        P(),
        P(),
        P(),
        P(),
        P(),
        P(),
        P("batch", ("pb", "ka"), None),
    )
    return jax.shard_map(
        shards,
        mesh=mesh,
        in_specs=placed,
        out_specs=(
            P("batch", ("pb", "ka"), None),
            P("batch", ("pb", "ka"), None),
            P("batch", ("pb", "ka")),
            P("batch", ("pb", "ka")),
            P("batch", ("pb", "ka")),
            P("batch", ("pb", "ka")),
            P(None, ("pb", "ka")),
        ),
        check_vma=False,
    )
```

```python
import functools

import jax
import jax.numpy as jnp
from jax import lax
from jax.experimental import pallas as pl
from jax.experimental.pallas import tpu as pltpu
from jax.sharding import PartitionSpec as P

HEADS = 12
HEAD = 64
PAIR = 2 * HEAD
QTILE = 128
STRIP = 32
SCALE = HEAD ** (-0.5)
HUGE = 3e38
HIDDEN = -1e30

norm_eps = 1e-05
BF16 = jnp.bfloat16
F32 = jnp.float32


def norm_rows(values, gain_vec, shift_vec):
    average = jnp.mean(values, axis=-1, keepdims=True)
    centred = values - average
    spread = jnp.mean(centred * centred, axis=-1, keepdims=True)
    return centred * lax.rsqrt(spread + norm_eps) * gain_vec + shift_vec


def gelu_tanh(values):
    return jax.nn.gelu(values, approximate=True)


def dot(a, b, contract):
    return lax.dot_general(a, b, ((contract[:1], contract[1:]), ((), ())), preferred_element_type=F32)


def head_lanes(values, head):
    lane = lax.broadcasted_iota(jnp.int32, values.shape, 1)
    mine = lane < HEAD if head == 0 else lane >= HEAD
    return jnp.where(mine, values, jnp.zeros_like(values))


def hide_later(magnitude):
    keys = magnitude.shape[0]
    key = lax.broadcasted_iota(jnp.int32, (QTILE, QTILE), 0)
    query = lax.broadcasted_iota(jnp.int32, (QTILE, QTILE), 1)
    last = jnp.where(key <= query, magnitude[keys - QTILE :], HIDDEN)
    return last if keys == QTILE else jnp.concatenate([magnitude[: keys - QTILE], last], axis=0)


def sign_of(scores):
    return jnp.clip(scores * HUGE, -1.0, 1.0)


def attend_kernel(
    core_ref, place_ref, mine_ref, other_ref, gain_ref, shift_ref, wq_ref, wk_ref, wv_ref,
    out_ref, normed_ref, qkv_ref, sums_ref, stats_ref, o_sc,
):
    blocks, half = mine_ref.shape[0], mine_ref.shape[1]
    rows = 2 * half
    total_rows = normed_ref.shape[0]

    @pl.when(pl.program_id(0) == 0)
    def _():
        @pl.loop(0, blocks)
        def _(block):
            for ref, part in ((mine_ref, core_ref[0]), (other_ref, 1 - core_ref[0])):
                at = pl.multiple_of(place_ref[block] * rows + part * half, half)
                normed = norm_rows(ref[block].astype(F32), gain_ref[...], shift_ref[...])
                normed_ref[pl.ds(at, half), :] = normed.astype(BF16)

    weights = jnp.concatenate([wq_ref[...], wk_ref[...], wv_ref[...]], axis=1)
    qkv_ref[0] = jnp.dot(normed_ref[...], weights, preferred_element_type=F32).astype(BF16)
    v_t = qkv_ref[0, :, 2 * PAIR :].T
    for tile in range(total_rows // QTILE):
        span = slice(tile * QTILE, (tile + 1) * QTILE)
        keys = (tile + 1) * QTILE
        queries = qkv_ref[0, span, :PAIR] * SCALE
        for head in range(2):
            scores = dot(qkv_ref[0, :keys, PAIR : 2 * PAIR], head_lanes(queries, head).astype(BF16), (1, 1))
            magnitude = hide_later(jnp.abs(scores))
            peak = jnp.max(magnitude, axis=0, keepdims=True)
            exponents = jnp.exp(magnitude - peak)
            total = jnp.sum(exponents, axis=0, keepdims=True)
            weights = (exponents * sign_of(scores)).astype(BF16)
            summed = dot(v_t[head * HEAD : (head + 1) * HEAD, :keys], weights, (1, 0))
            sums_ref[0, head * HEAD : (head + 1) * HEAD, span] = summed / total
            stats_ref[0, head : head + 1, span] = peak + jnp.log(total)
        o_sc[span, :] = sums_ref[0, :, span].T
    for block in range(blocks):
        at = pl.multiple_of(place_ref[block] * rows, rows)
        out_ref[block] = o_sc[pl.ds(at, rows), :].astype(BF16)


def columns_of(width, size, kind, pairs):
    return pl.BlockSpec(
        (width, size), lambda i, core, place: (0, kind * (width // size) + core[0] * pairs + jnp.minimum(i, pairs - 1))
    )


def fixed2(shape):
    return pl.BlockSpec(shape, lambda i, *scalars, n=len(shape): (0,) * n)


def attend(core, place, mine, other, gain, shift, w_qkv):
    blocks, half, width = mine.shape
    length, pairs = 2 * half * blocks, width // PAIR // 2
    area = length * length
    return pl.pallas_call(
        attend_kernel,
        grid_spec=pltpu.PrefetchScalarGridSpec(
            num_scalar_prefetch=2,
            grid=(pairs,),
            in_specs=[fixed2(mine.shape), fixed2(mine.shape), fixed2((width,)), fixed2((width,))]
            + [columns_of(width, PAIR, kind, pairs) for kind in range(3)],
            out_specs=[
                pl.BlockSpec((blocks, 2 * half, PAIR), lambda i, c, p: (0, 0, i)),
                fixed2((length, width)),
                pl.BlockSpec((1, length, 3 * PAIR), lambda i, c, p: (i, 0, 0)),
                pl.BlockSpec((1, PAIR, length), lambda i, c, p: (i, 0, 0)),
                pl.BlockSpec((1, 8, length), lambda i, c, p: (i, 0, 0)),
            ],
            scratch_shapes=[pltpu.VMEM((length, PAIR), F32)],
        ),
        out_shape=[
            jax.ShapeDtypeStruct((blocks, 2 * half, pairs * PAIR), BF16),
            jax.ShapeDtypeStruct((length, width), BF16),
            jax.ShapeDtypeStruct((pairs, length, 3 * PAIR), BF16),
            jax.ShapeDtypeStruct((pairs, PAIR, length), F32),
            jax.ShapeDtypeStruct((pairs, 8, length), F32),
        ],
        cost_estimate=pl.CostEstimate(
            flops=pairs * 16 * area * HEAD + 3 * length * width * width,
            bytes_accessed=8 * length * width,
            transcendentals=pairs * area,
        ),
        name="attend",
    )(core, place, mine, other, gain, shift, w_qkv, w_qkv, w_qkv)


def attend_back_kernel(
    core_ref, place_ref, to_ref, qkv_ref, g_ref, sums_ref, stats_ref, normed_ref, mine_ref, other_ref, norm_ref,
    wq_ref, wk_ref, wv_ref, gq_ref, keep_ref, send_ref, norms_ref, g_sc, dq_sc, dk_sc, dv_sc, packed_sc, back_sc,
):
    blocks, rows = g_ref.shape[0], g_ref.shape[1]
    for block in range(blocks):
        at = pl.multiple_of(place_ref[block] * rows, rows)
        g_sc[pl.ds(at, rows), :] = g_ref[block]
    total_rows = g_sc.shape[0]
    k_t = qkv_ref[0, :, PAIR : 2 * PAIR].T
    g_t = g_sc[...].astype(F32).T
    products = g_t * sums_ref[0]
    deltas = [
        jnp.sum(products[head * HEAD : (head + 1) * HEAD], axis=0, keepdims=True) for head in range(2)
    ]
    dk_sc[...] = jnp.zeros_like(dk_sc)
    dv_sc[...] = jnp.zeros_like(dv_sc)
    for tile in range(total_rows // QTILE):
        span = slice(tile * QTILE, (tile + 1) * QTILE)
        keys = (tile + 1) * QTILE
        queries = qkv_ref[0, span, :PAIR] * SCALE
        parts = []
        for head in range(2):
            q_head = head_lanes(queries, head).astype(BF16)
            g_head = head_lanes(g_sc[span, :], head)
            scores = dot(qkv_ref[0, :keys, PAIR : 2 * PAIR], q_head, (1, 1))
            magnitude = hide_later(jnp.abs(scores))
            sign = sign_of(scores)
            signed = jnp.exp(magnitude - stats_ref[0, head : head + 1, span]) * sign
            grad_weights = dot(qkv_ref[0, :keys, 2 * PAIR :], g_head, (1, 1))
            grad_scores = (signed * (sign * grad_weights - deltas[head][:, span])).astype(BF16)
            dv_sc[:keys, :] += dot(signed.astype(BF16), g_head, (1, 0))
            dk_sc[:keys, :] += dot(grad_scores, q_head, (1, 0))
            parts.append(dot(k_t[head * HEAD : (head + 1) * HEAD, :keys], grad_scores, (1, 0)))
        dq_sc[span, :] = jnp.concatenate(parts, axis=0).T * SCALE
    for kind, ref in enumerate((dq_sc, dk_sc, dv_sc)):
        grad = ref[...].astype(BF16)
        packed_sc[:, kind * PAIR : (kind + 1) * PAIR] = grad
        turned = jnp.dot(grad.T, normed_ref[...], preferred_element_type=F32).astype(BF16)
        for strip in range(PAIR // STRIP):
            at = to_ref[(pl.program_id(0) * 3 + kind) * (PAIR // STRIP) + strip]
            at = pl.multiple_of(at * STRIP, STRIP)
            gq_ref[pl.ds(at, STRIP), :] = turned[strip * STRIP : (strip + 1) * STRIP]

    step, half = pl.program_id(0), mine_ref.shape[1]
    weights = jnp.concatenate([wq_ref[...], wk_ref[...], wv_ref[...]], axis=1)
    back = dot(packed_sc[...], weights, (1, 1))

    @pl.when(step == 0)
    def _():
        back_sc[...] = back

    @pl.when(step > 0)
    def _():
        back_sc[...] += back

    @pl.when(step == pl.num_programs(0) - 1)
    def _():
        norms_ref[...] = norm_ref[...]

        @pl.loop(0, blocks)
        def _(block):
            for ref, out_ref, part in ((mine_ref, keep_ref, core_ref[0]), (other_ref, send_ref, 1 - core_ref[0])):
                at = pl.multiple_of(place_ref[block] * rows + part * half, half)
                grad = back_sc[pl.ds(at, half), :]
                out_ref[block] = grad.astype(out_ref.dtype)
                x = ref[block].astype(F32)
                centred = x - jnp.mean(x, axis=-1, keepdims=True)
                unit = centred * lax.rsqrt(jnp.mean(centred * centred, axis=-1, keepdims=True) + norm_eps)
                norms_ref[0:1, :] += jnp.sum(grad * unit, axis=0, keepdims=True)
                norms_ref[1:2, :] += jnp.sum(grad, axis=0, keepdims=True)


def attend_back(core, place, to, qkv, grad, sums, stats, normed, mine, other, norm, w_qkv):
    pairs, length, _ = qkv.shape
    blocks, rows, _ = grad.shape
    width = normed.shape[1]
    area = length * length
    one = lambda i, c, p, t: (i, 0, 0)

    def columns(kind):
        size = width // PAIR
        return pl.BlockSpec((width, PAIR), lambda i, core, p, t: (0, kind * size + core[0] * pairs + i))

    return pl.pallas_call(
        attend_back_kernel,
        grid_spec=pltpu.PrefetchScalarGridSpec(
            num_scalar_prefetch=3,
            grid=(pairs,),
            in_specs=[
                pl.BlockSpec((1, length, 3 * PAIR), one),
                pl.BlockSpec((blocks, rows, PAIR), lambda i, c, p, t: (0, 0, i)),
                pl.BlockSpec((1, PAIR, length), one),
                pl.BlockSpec((1, 8, length), one),
                fixed2(normed.shape),
                fixed2(mine.shape),
                fixed2(mine.shape),
                fixed2(norm.shape),
                *(columns(kind) for kind in range(3)),
            ],
            out_specs=[
                fixed2((pairs * 3 * PAIR, width)),
                fixed2(mine.shape),
                fixed2(mine.shape),
                fixed2(norm.shape),
            ],
            scratch_shapes=[
                pltpu.VMEM((length, PAIR), BF16),
                *[pltpu.VMEM((length, PAIR), F32)] * 3,
                pltpu.VMEM((length, 3 * PAIR), BF16),
                pltpu.VMEM((length, width), F32),
            ],
        ),
        out_shape=[
            jax.ShapeDtypeStruct((pairs * 3 * PAIR, width), BF16),
            jax.ShapeDtypeStruct(mine.shape, F32),
            jax.ShapeDtypeStruct(mine.shape, BF16),
            jax.ShapeDtypeStruct(norm.shape, F32),
        ],
        cost_estimate=pl.CostEstimate(
            flops=pairs * 40 * area * HEAD + 6 * length * width * width,
            bytes_accessed=8 * length * width,
            transcendentals=pairs * area,
        ),
        name="attend_back",
    )(core, place, to, qkv, grad, sums, stats, normed, mine, other, norm, w_qkv, w_qkv, w_qkv)


def merge_kernel(keep_ref, other_ref, norm_ref, out_ref):
    half = keep_ref.shape[1]
    block = norm_ref.shape[1] // keep_ref.shape[0]
    norms = norm_ref[...].astype(BF16)
    for at in range(keep_ref.shape[0]):
        out_ref[at, :half] = (keep_ref[at] + other_ref[at].astype(F32)).astype(BF16)
        out_ref[at, half:] = jnp.zeros_like(out_ref[at, half:])
        out_ref[at, half:, :block] = norms[:, at * block : (at + 1) * block]


def merge(keep, other, norm):
    blocks, half, width = keep.shape
    return pl.pallas_call(
        merge_kernel,
        grid=(1,),
        in_specs=[fixed2(keep.shape), fixed2(keep.shape), fixed2(norm.shape)],
        out_specs=fixed2((blocks, half + norm.shape[0], width)),
        out_shape=jax.ShapeDtypeStruct((blocks, half + norm.shape[0], width), BF16),
        cost_estimate=pl.CostEstimate(
            flops=blocks * half * width, bytes_accessed=8 * blocks * half * width, transcendentals=0
        ),
        name="merge",
    )(keep, other, norm)


@functools.lru_cache
def strips(width, plane):
    near, owned = plane // 2, 3 * width // plane // STRIP
    side, pair = width // 2 // STRIP, PAIR // STRIP
    slots = []
    for core in range(2):
        slot, count = {}, [0, 0]
        for col in range(2 * near * owned):
            if col % (2 * side) // side == core:
                away = (col // owned % 2) ^ core
                slot[col] = (away, count[away])
                count[away] += 1
        assert count == [near * owned // 2] * 2
        slots.append(slot)
    stay = near * owned // 2
    to, found = [], []
    for core in range(2):
        order = [
            kind * 2 * side + core * side + p * pair + strip
            for p in range(side // pair)
            for kind in range(3)
            for strip in range(pair)
        ]
        to.append([slots[core][col][0] * stay + slots[core][col][1] for col in order])
        row = []
        for chip in range(near):
            for strip in range(owned):
                col = (2 * chip + core) * owned + strip
                row.append(slots[core][col][1] if col in slots[core] else stay + slots[1 - core][col][1])
        found.append(row)
    return to, found


def tiles_kernel(near, owned, chip_ref, found_ref, keep_ref, given_ref, *outs):
    stay = keep_ref.shape[0] // STRIP
    for k in range(near):
        for strip in range(owned):
            at = found_ref[(chip_ref[0] ^ k) * owned + strip]
            here = pl.multiple_of(jnp.minimum(at, stay - 1) * STRIP, STRIP)
            there = pl.multiple_of(jnp.maximum(at - stay, 0) * STRIP, STRIP)
            outs[k][strip * STRIP : (strip + 1) * STRIP, :] = jnp.where(
                at < stay, keep_ref[pl.ds(here, STRIP), :], given_ref[pl.ds(there, STRIP), :]
            )


def qkv_tiles(chip, found, grad, given, near):
    size, width = given.shape
    owned = 2 * size // near // STRIP
    shape = (owned * STRIP, width)
    return pl.pallas_call(
        functools.partial(tiles_kernel, near, owned),
        grid_spec=pltpu.PrefetchScalarGridSpec(
            num_scalar_prefetch=2,
            grid=(1,),
            in_specs=[fixed2(given.shape), fixed2(given.shape)],
            out_specs=[fixed2(shape)] * near,
        ),
        out_shape=[jax.ShapeDtypeStruct(shape, BF16)] * near,
        cost_estimate=pl.CostEstimate(flops=size * width, bytes_accessed=size * width, transcendentals=0),
        name="qkv_tiles",
    )(chip, found, grad, given)


def gelu_pair(u):
    c = 0.7978845608028654
    square = u * u
    t = jnp.tanh(c * u * (1.0 + 0.044715 * square))
    half = 0.5 * (1.0 + t)
    slope = half + 0.5 * c * u * (1.0 - t * t) * (1.0 + 3.0 * 0.044715 * square)
    return u * half, slope


def norm_back(values, gain_vec, grad):
    average = jnp.mean(values, axis=-1, keepdims=True)
    centred = values - average
    spread = jnp.mean(centred * centred, axis=-1, keepdims=True)
    scale = lax.rsqrt(spread + norm_eps)
    unit = centred * scale
    scaled = grad * gain_vec
    back = scale * (
        scaled
        - jnp.mean(scaled, axis=-1, keepdims=True)
        - unit * jnp.mean(scaled * unit, axis=-1, keepdims=True)
    )
    return back, jnp.sum(grad * unit, axis=0, keepdims=True), jnp.sum(grad, axis=0, keepdims=True)


def ff_kernel(seqs, plane, *refs):
    me_ref, x_ref, att_ref, cot_ref, w_out_ref, gain_ref, shift_ref, *refs = refs
    ups, downs, refs = refs[:2], refs[2:4], refs[4:]
    out_ref, res_ref, *refs = refs
    ga_ref, norm_ref, gu_send, gu_keep, gd_send, gd_keep, gp_send, gp_keep, *refs = refs
    att_sc, residual_sc, normed_sc, normed_t, turned_sc, acc_out, acc_grad = refs
    step = pl.program_id(0)
    tokens, width = x_ref.shape
    rows = tokens // seqs
    block = width // plane
    near = plane // 2

    def turn(values):
        turned = values.T
        for j in range(plane):
            t = me_ref[0] ^ j
            slot = (1 - (t & 1)) * near + (t >> 1)
            at = pl.multiple_of(slot * block, block)
            turned_sc[pl.ds(at, block), :] = turned[j * block : (j + 1) * block]

    @pl.when(step == 0)
    def _():
        for seq in range(seqs):
            for core in range(2):
                cols = slice(core * width // 2, (core + 1) * width // 2)
                att_sc[seq * rows : (seq + 1) * rows, cols] = att_ref[seq * 2 + core]
        residual = x_ref[...].astype(F32) + jnp.dot(att_sc[...], w_out_ref[...], preferred_element_type=F32)
        residual_sc[...] = residual
        normed = norm_rows(residual, gain_ref[...], shift_ref[...]).astype(BF16)
        normed_sc[...] = normed
        normed_t[...] = normed.T
        turn(cot_ref[...])
        acc_out[...] = jnp.zeros_like(acc_out)
        acc_grad[...] = jnp.zeros_like(acc_grad)

    up = jnp.concatenate([r[...] for r in ups], axis=1)
    down = jnp.concatenate([r[...] for r in downs], axis=0)
    pre = jnp.dot(normed_sc[...], up, preferred_element_type=F32)
    active, slope = gelu_pair(pre)
    active = active.astype(BF16)
    grad_pre = (dot(cot_ref[...], down, (1, 1)) * slope).astype(BF16)
    acc_out[...] += jnp.dot(active, down, preferred_element_type=F32)
    acc_grad[...] += dot(grad_pre, up, (1, 1))
    grad_up = jnp.dot(normed_t[...], grad_pre, preferred_element_type=F32).astype(BF16)
    grad_down = jnp.dot(turned_sc[...], active, preferred_element_type=F32).astype(BF16)
    part = ups[0].shape[1]
    for half in range(2):
        spot = ((me_ref[0] >> 1) ^ half) & 1
        cols = slice(half * part, (half + 1) * part)
        for slot in range(near):
            gd_send[slot, 0, spot, 0] = grad_down[slot * block : (slot + 1) * block, cols]
            gd_keep[slot, 0, spot, 0] = grad_down[(near + slot) * block : (near + slot + 1) * block, cols]

        @pl.when(step < near // 2)
        def _():
            gu_send[half] = grad_up[:, cols]

        @pl.when(step >= near // 2)
        def _():
            gu_keep[half] = grad_up[:, cols]

    @pl.when(step == near - 1)
    def _():
        residual = residual_sc[...]
        out_ref[...] = (residual + acc_out[...]).astype(BF16)
        back, gain_grad, shift_grad = norm_back(residual, gain_ref[...], acc_grad[...])
        norm_ref[...] = jnp.zeros_like(norm_ref)
        norm_ref[2:3, :] = gain_grad
        norm_ref[3:4, :] = shift_grad
        grad_res = cot_ref[...].astype(F32) + back
        res_ref[...] = grad_res
        grad_z = grad_res.astype(BF16)
        grad_att = dot(grad_z, w_out_ref[...], (1, 1)).astype(BF16)
        for seq in range(seqs):
            for core in range(2):
                cols = slice(core * width // 2, (core + 1) * width // 2)
                ga_ref[seq * 2 + core] = grad_att[seq * rows : (seq + 1) * rows, cols]
        turn(grad_z)
        grad_proj = jnp.dot(turned_sc[...], att_sc[...], preferred_element_type=F32).astype(BF16)
        for slot in range(near):
            gp_send[slot] = grad_proj[slot * block : (slot + 1) * block]
            gp_keep[slot] = grad_proj[(near + slot) * block : (near + slot + 1) * block]


def feed_forward(me, x, attended, cotangent, w_out, gain, shift, w_up, w_down, plane):
    seqs, rows, width = x.shape
    hidden = w_up.shape[1]
    tokens, near, part, block = seqs * rows, plane // 2, hidden // plane, width // plane

    def at(i, me, half=0):
        return me[0] ^ (4 * (i % (near // 2)) + 2 * half + jnp.where(i < near // 2, 1, 0))

    def fixed(shape):
        return pl.BlockSpec(shape, lambda i, me, n=len(shape): (0,) * n)

    joined = attended.shape
    outs = [
        ((tokens, width), BF16, fixed((tokens, width))),
        ((tokens, width), F32, fixed((tokens, width))),
        (joined, BF16, fixed(joined)),
        ((8, width), F32, fixed((8, width))),
        ((near, width, part), BF16, pl.BlockSpec((2, width, part), lambda i, me: (jnp.minimum(i, near // 2 - 1), 0, 0))),
        ((near, width, part), BF16, pl.BlockSpec((2, width, part), lambda i, me: (jnp.maximum(i - near // 2, 0), 0, 0))),
        *[
            (
                (near, plane // 4, 2, 2, block, part),
                BF16,
                pl.BlockSpec(
                    (near, 1, 2, 1, block, part), lambda i, me: (0, at(i, me) >> 2, 0, at(i, me) & 1, 0, 0)
                ),
            )
        ]
        * 2,
        *[((near, block, width), BF16, fixed((near, block, width)))] * 2,
    ]
    return pl.pallas_call(
        functools.partial(ff_kernel, seqs, plane),
        grid_spec=pltpu.PrefetchScalarGridSpec(
            num_scalar_prefetch=1,
            grid=(near,),
            in_specs=[fixed((tokens, width))]
            + [fixed(joined), fixed((tokens, width)), fixed((width, width)), fixed((width,)), fixed((width,))]
            + [
                pl.BlockSpec((width, part), lambda i, me: (0, at(i, me))),
                pl.BlockSpec((width, part), lambda i, me: (0, at(i, me, 1))),
                pl.BlockSpec((part, width), lambda i, me: (at(i, me), 0)),
                pl.BlockSpec((part, width), lambda i, me: (at(i, me, 1), 0)),
            ],
            out_specs=[o[2] for o in outs],
            scratch_shapes=[
                pltpu.VMEM((tokens, width), BF16),
                pltpu.VMEM((tokens, width), F32),
                pltpu.VMEM((tokens, width), BF16),
                pltpu.VMEM((width, tokens), BF16),
                pltpu.VMEM((width, tokens), BF16),
                pltpu.VMEM((tokens, width), F32),
                pltpu.VMEM((tokens, width), F32),
            ],
        ),
        out_shape=[jax.ShapeDtypeStruct(o[0], o[1]) for o in outs],
        cost_estimate=pl.CostEstimate(
            flops=12 * tokens * width * hidden + 6 * tokens * width * width,
            bytes_accessed=8 * width * hidden,
            transcendentals=tokens * hidden,
        ),
        name="feed_forward",
    )(
        me,
        x.reshape(tokens, width),
        attended,
        cotangent.reshape(tokens, width),
        w_out,
        gain,
        shift,
        w_up,
        w_up,
        w_down,
        w_down,
    )


def first_norm_kernel(seqs, x_ref, gain_ref, grad_ref, res_ref, out_ref, norm_ref):
    half = x_ref.shape[0] // seqs // 2
    for piece in range(2 * seqs):
        at = slice(piece * half, (piece + 1) * half)
        values = x_ref[at].astype(F32)
        centred = values - jnp.mean(values, axis=-1, keepdims=True)
        scale = lax.rsqrt(jnp.mean(centred * centred, axis=-1, keepdims=True) + norm_eps)
        unit = centred * scale
        scaled = grad_ref[piece, :half].astype(F32) * gain_ref[...]
        back = scale * (
            scaled
            - jnp.mean(scaled, axis=-1, keepdims=True)
            - unit * jnp.mean(scaled * unit, axis=-1, keepdims=True)
        )
        out_ref[at] = (res_ref[at] + back).astype(BF16)
    norms = grad_ref[0, half:, :PAIR].astype(F32)
    for piece in range(1, 2 * seqs):
        norms = norms + grad_ref[piece, half:, :PAIR].astype(F32)
    norm_ref[...] = norms


def first_norm_back(x, gain, grad, grad_res):
    seqs, rows, width = x.shape
    tokens = seqs * rows
    return pl.pallas_call(
        functools.partial(first_norm_kernel, seqs),
        grid=(1,),
        in_specs=[fixed2((tokens, width)), fixed2((width,)), fixed2(grad.shape), fixed2((tokens, width))],
        out_specs=[fixed2((tokens, width)), fixed2((8, PAIR))],
        out_shape=[jax.ShapeDtypeStruct((tokens, width), BF16), jax.ShapeDtypeStruct((8, PAIR), F32)],
        cost_estimate=pl.CostEstimate(flops=20 * tokens * width, bytes_accessed=12 * tokens * width, transcendentals=0),
        name="first_norm_back",
    )(x.reshape(tokens, width), gain, grad, grad_res)


def exchange(blocks):
    return lax.all_to_all(blocks, ("pb", "ka"), 0, 0, tiled=True)


def swap(values, axes, size, bit):
    return lax.ppermute(values, axes, [(i, i ^ bit) for i in range(size)])


def add_pair_kernel(near, batch, *refs):
    _, up_a, up_b, down_a, down_b, proj_a, proj_b, *outs = refs
    outs, down_outs = outs[:near], outs[near:]
    step = pl.program_id(0)
    part = outs[0].shape[1]

    def both(a, b):
        return a + b

    @pl.when(step < batch)
    def _():
        for k in range(near):
            outs[k][...] = both(up_a[k], up_b[k])

    for far in range(batch):

        @pl.when(step == far)
        def _():
            for k in range(near):
                total = both(down_a[k], down_b[k])
                slab = total.shape[0] * total.shape[1]
                target, at = down_outs[far in (1, 2)], (far > 1) * near * slab + k * slab
                target[at : at + slab] = total.reshape(slab, part)

    @pl.when(step == batch)
    def _():
        for k in range(near):
            total = both(proj_a[k], proj_b[k])
            outs[k][...] = jnp.concatenate([total[:, :part], total[:, part:]], axis=0)


def add_pair(mine, up, down, proj, batch):
    near, width, part = up[0].shape
    plane, block = down[0].shape[1:3]
    tall, few = width // batch, plane // batch
    up_spec = pl.BlockSpec((near, tall, part), lambda i, m: (0, jnp.minimum(i, batch - 1), 0))
    down_spec = pl.BlockSpec(
        (near, few, block, part), lambda i, m: (0, m[0] ^ jnp.minimum(i, batch - 1), 0, 0)
    )
    proj_spec = pl.BlockSpec((near, block, width), lambda i, m: (0, 0, 0))
    last = lambda i, m: (i, 0)
    down_shape = (2 * near * few * block, part)
    return pl.pallas_call(
        functools.partial(add_pair_kernel, near, batch),
        grid_spec=pltpu.PrefetchScalarGridSpec(
            num_scalar_prefetch=1,
            grid=(batch + 1,),
            in_specs=[up_spec] * 2 + [down_spec] * 2 + [proj_spec] * 2,
            out_specs=[pl.BlockSpec((tall, part), last)] * near
            + [pl.BlockSpec(down_shape, lambda i, m: (0, 0))] * 2,
        ),
        out_shape=[jax.ShapeDtypeStruct((width + tall, part), BF16)] * near
        + [jax.ShapeDtypeStruct(down_shape, BF16)] * 2,
        cost_estimate=pl.CostEstimate(
            flops=near * 9 * tall * part, bytes_accessed=6 * near * 9 * tall * part, transcendentals=0
        ),
        name="add_pair",
    )(mine, *up, *down, *proj)


def add_all(parts):
    total = parts[0].astype(F32)
    for p in parts[1:]:
        total = total + p.astype(F32)
    return total


def over_batch(stacked):
    return lax.psum_scatter(stacked, "batch", scatter_dimension=0, tiled=True)[0].astype(F32)


def over_plane(tiles, plane):
    return [tiles[0]] + [swap(tiles[k], ("pb", "ka"), plane, 2 * k) for k in range(1, len(tiles))]


def pack_kernel(batch, mine_ref, *refs):
    early_ref, late_ref, *outs, side_sc = refs
    width, slab = side_sc.shape[0], outs[0].shape[0] // 2
    block = (early_ref.shape[0] - width) // 2
    proj = jnp.concatenate([early_ref[width : width + block], early_ref[width + block :]], axis=1)
    side_sc[...] = jnp.concatenate([late_ref[...], proj], axis=0).T
    for far in range(batch):
        at = pl.multiple_of((mine_ref[0] ^ far) * slab, slab)
        outs[far][:slab] = early_ref[pl.ds(at, slab), :]
        outs[far][slab:] = side_sc[pl.ds(at, slab), :]


def pack(mine, early, late, batch):
    width, part = late.shape[1], early.shape[1]
    shape = (2 * width // batch, part)
    return pl.pallas_call(
        functools.partial(pack_kernel, batch),
        grid_spec=pltpu.PrefetchScalarGridSpec(
            num_scalar_prefetch=1,
            grid=(1,),
            in_specs=[fixed2(early.shape), fixed2(late.shape)],
            out_specs=[fixed2(shape)] * batch,
            scratch_shapes=[pltpu.VMEM((width, part), BF16)],
        ),
        out_shape=[jax.ShapeDtypeStruct(shape, BF16)] * batch,
        cost_estimate=pl.CostEstimate(flops=8 * width * part, bytes_accessed=20 * width * part, transcendentals=0),
        name="pack",
    )(mine, early, late)


def finish_kernel(*refs):
    parts, (up_ref, qkv_ref, proj_ref) = refs[:-3], refs[-3:]
    slab, owned = qkv_ref.shape
    total = add_all([r[...] for r in parts])
    up_ref[...] = total[:slab]
    qkv_ref[...] = total[slab:, :owned]
    proj_ref[...] = total[slab:, owned:]


def finish_down_kernel(*refs):
    parts, down_ref = refs[:-1], refs[-1]
    total = add_all([r[...] for r in parts])
    block, part = down_ref.shape[0], total.shape[1]
    for at in range(total.shape[0] // block):
        down_ref[:, at * part : (at + 1) * part] = total[at * block : (at + 1) * block]


def finish(kernel, parts, shapes):
    rows, part = parts[0].shape
    return pl.pallas_call(
        kernel,
        grid=(1,),
        in_specs=[fixed2(a.shape) for a in parts],
        out_specs=[fixed2(s) for s in shapes],
        out_shape=[jax.ShapeDtypeStruct(s, F32) for s in shapes],
        cost_estimate=pl.CostEstimate(flops=8 * rows * part, bytes_accessed=16 * rows * part, transcendentals=0),
        name="finish",
    )(*parts)


def shards(
    inputs,
    block_place,
    ln1_gain,
    ln1_shift,
    w_qkv,
    w_out,
    ln2_gain,
    ln2_shift,
    w_up,
    w_down,
    cotangent,
):
    seqs, rows, width = inputs.shape
    hidden = w_up.shape[1]
    plane = lax.axis_size("pb") * lax.axis_size("ka")
    planes = ("pb", "ka")
    batch = lax.axis_size("batch")
    near = plane // 2
    few = batch == 4
    me = lax.axis_index(planes)
    scalar = lambda value: value.astype(jnp.int32).reshape(1)
    core, chip = scalar(me & 1), scalar(me >> 1)
    part, block, slab = hidden // plane, width // plane, width // batch
    place = lax.dynamic_index_in_dim(block_place, me >> 1, 0, False)
    to, found = [jnp.where(core == 0, *(jnp.array(t, jnp.int32) for t in both)) for both in strips(width, plane)]

    mine = exchange(inputs.reshape(plane, seqs * rows // plane, width))
    other = swap(mine, planes, plane, 1)
    attended, normed1, packed, sums, stats = attend(core, place, mine, other, ln1_gain, ln1_shift, w_qkv)
    outputs, grad_res, grad_att, norm2, *grads = feed_forward(
        scalar(me), inputs, exchange(attended), cotangent, w_out, ln2_gain, ln2_shift, w_up, w_down, plane
    )
    grad_att = exchange(grad_att)
    grads[2:4] = [g.reshape(near, plane, block, part) for g in grads[2:4]]
    up, down, proj = [(grads[2 * i + 1], swap(grads[2 * i], planes, plane, 1)) for i in range(3)]
    if few:
        sums_up = add_pair(scalar(lax.axis_index("batch")), up, down, proj, batch)
        grad_att, sums_up = lax.optimization_barrier((grad_att, sums_up))
        tiles, down = sums_up[:near], sums_up[near:]
    else:
        tiles = [
            jnp.concatenate(
                [add_all([t[k] for t in up])]
                + [add_all([t[k] for t in down]).reshape(width, part)]
                + [add_all([t[k] for t in proj]).reshape(block, 2, part).transpose(1, 0, 2).reshape(2 * block, part)]
            ).astype(BF16)
            for k in range(near)
        ]
    early = add_all(over_plane(tiles, plane)).astype(BF16)
    if few:
        down = add_all([down[0], swap(down[1], "batch", batch, 1)]).astype(BF16)

    grad_qkv, keep, send, norm = attend_back(
        core, place, to, packed, grad_att, sums, stats, normed1, mine, other, norm2, w_qkv
    )
    given = swap(grad_qkv[grad_qkv.shape[0] // 2 :], planes, plane, 1)
    if few:
        given, early, down = lax.optimization_barrier((given, early, down))
        down = jnp.split(down, 2)
        down[1] = swap(down[1], "batch", batch, 3)
    late = qkv_tiles(chip, found, grad_qkv, given, near)
    keep, late = lax.optimization_barrier((keep, late))
    returned = exchange(merge(keep, swap(send, planes, plane, 1), norm))
    late = add_all(over_plane(late, plane)).astype(BF16)
    owned = 3 * width // plane
    if few:
        along = scalar(lax.axis_index("batch"))
        sums = pack(along, early, late, batch)
        sums = [sums[0]] + [swap(sums[bit], "batch", batch, bit) for bit in range(1, batch)]
        returned, down = lax.optimization_barrier((returned, add_all(down).astype(BF16)))
        down = over_plane(jnp.split(down, near), plane)
    grad_inputs, norms = first_norm_back(inputs, ln1_gain, returned, grad_res)
    if few:
        for bit in (1, 2):
            norms = norms + swap(norms, "batch", batch, bit)
        grad_up, grad_qkv, grad_proj = finish(finish_kernel, sums, [(slab, part), (slab, owned), (slab, block)])
        (grad_down,) = finish(finish_down_kernel, down, [(block, hidden // batch)])
        grad_down = grad_down.T
    else:
        tile, cut = early, batch // plane
        down_tile = tile[width : 2 * width].reshape(plane, block, cut, part // cut).transpose(0, 2, 1, 3)
        grad_down = over_batch(down_tile.reshape(batch, block, part // cut)).T
        proj_tile = tile[-2 * block :].reshape(2, block, part).transpose(1, 0, 2).reshape(block, batch, slab)
        grad_proj = over_batch(proj_tile.transpose(1, 0, 2)).T
        grad_up = over_batch(tile[:width].reshape(batch, slab, part))
        grad_qkv = over_batch(late.reshape(owned, batch, slab).transpose(1, 0, 2)).T
        norms = lax.psum(norms, "batch")
    return (
        outputs.reshape(inputs.shape),
        grad_inputs.reshape(inputs.shape),
        grad_qkv,
        grad_proj,
        grad_up,
        grad_down,
        norms[:4, :block],
    )


def solution(mesh):
    placed = (
        P("batch", ("pb", "ka"), None),
        P("batch", None),
        P(),
        P(),
        P(),
        P(),
        P(),
        P(),
        P(),
        P(),
        P("batch", ("pb", "ka"), None),
    )
    return jax.shard_map(
        shards,
        mesh=mesh,
        in_specs=placed,
        out_specs=(
            P("batch", ("pb", "ka"), None),
            P("batch", ("pb", "ka"), None),
            P("batch", ("pb", "ka")),
            P("batch", ("pb", "ka")),
            P("batch", ("pb", "ka")),
            P("batch", ("pb", "ka")),
            P(None, ("pb", "ka")),
        ),
        check_vma=False,
    )
```
